256 devices in a mesh: group: 4 (over x), member: 64 (over z, y, core).
Axes of the slice: x: 4, y: 4, z: 8, core: 2. Of those that a mesh axis runs over, the one named last changes fastest.
Arguments:
- a_band: bfloat16 [49152, 3, 64, 64], P(('group', 'member')), as said below
- p_tent: bfloat16 [49152, 6, 64], P(('group', 'member')), may hold values from -0.8984375 to 0.8984375
- new_owner: int32 [49152], P(('group', 'member')), may hold values from 0 to 63, as said below
Outputs:
- p_smooth: bfloat16 [49152, 3, 6, 64], P(('group', 'member'))
- coarse: float32 [49152, 252], P(('group', 'member'))
The draws below stay inside these ranges and needn't reach their ends.
Inputs may be any that keep to these rules, and one draw needn't show every extreme that they name: `new_owner`: within each group, every device sends between 1 and 6 of its block rows to every member of its group, exactly 6 to at least one member, and every member receives exactly 192 block rows. a_band[n, 1, i, i] lies between 2 and 6.
All inputs are finite; a program needn't handle non-finite values.
Results may differ from the reference program's by a relative error of at most 0.0027.
The reference program's roundings to bfloat16 on the way (of `ap`) count: a program that leaves them out, or rounds other values in their place, can miss the bound.
Values may be sent and summed in bfloat16 or wider, within the bound.
No kernel may reach another device: no remote copies, remote signals or barrier semaphores. Data moves between devices by JAX's collectives and lax.ppermute only.
A program may use at most 128 MiB of HBM per device.

```python
import jax
import jax.numpy as jnp

TILE = 64
MODES = 6
BR_DEV = 192
CAP = 6
BLOCKS = 49152
N_MEMBER = 64


def draw_a_band(key, part):
    key_one, key_two = jax.random.split(key)
    values = jax.random.normal(key_one, (BLOCKS, 3, TILE, TILE), jnp.float32) * (3 * TILE) ** (-0.5)
    diag = jnp.exp(jax.random.uniform(key_two, (BLOCKS, 3, TILE, TILE), jnp.float32, jnp.log(2.0), jnp.log(6.0)))
    rows = jnp.arange(TILE)[:, None] == jnp.arange(TILE)[None, :]
    center = (jnp.arange(3) == 1)[:, None, None]
    mask = jnp.logical_and(rows[None, :, :], center)[None]
    return jnp.where(mask, diag, values).astype(jnp.bfloat16)


def draw_new_owner(key, part):
    groups = BLOCKS // (BR_DEV * N_MEMBER)
    units = (N_MEMBER - 1) * (CAP - 1)
    extra_total = BR_DEV - N_MEMBER - (CAP - 1)

    def one_group(group_key):
        key_max, key_units, key_src = jax.random.split(group_key, 3)
        heavy = jax.random.randint(key_max, (), 0, N_MEMBER)
        chosen = (jax.random.permutation(key_units, units) < extra_total).astype(jnp.int32)
        extra = chosen.reshape(N_MEMBER - 1, CAP - 1).sum(1)
        bucket = jnp.arange(N_MEMBER - 1, dtype=jnp.int32)
        target = bucket + (bucket >= heavy).astype(jnp.int32)
        counts = jnp.ones((N_MEMBER,), jnp.int32).at[target].add(extra).at[heavy].set(CAP)
        offsets = jnp.repeat(jnp.arange(N_MEMBER, dtype=jnp.int32), counts, total_repeat_length=BR_DEV)

        def one_source(src_key, source):
            order = jax.random.permutation(src_key, BR_DEV)
            return (source + offsets[order]) % N_MEMBER
        src_keys = jax.random.split(key_src, N_MEMBER)
        return jax.vmap(one_source)(src_keys, jnp.arange(N_MEMBER, dtype=jnp.int32)).reshape(-1)
    group_keys = jax.random.split(key, groups)
    return jax.vmap(one_group)(group_keys).reshape(-1).astype(jnp.int32)


def steps_of(stream_key, shape, shards, least, top_value):
    factor_of, own = 1.0, jax.random.fold_in(stream_key, 6)
    for dim, shards_of in shards:
        heights = jnp.exp(jax.random.uniform(jax.random.fold_in(own, dim), (shards_of,), jnp.float32, least / len(shards), top_value / len(shards)))
        factor_of = factor_of * jnp.repeat(heights, shape[dim] // shards_of).reshape([-1 if axis == dim else 1 for axis in range(len(shape))])
    return factor_of


def noise(stream_key, dims, spread, most, pieces=(), kind=jnp.bfloat16):
    array = spread * jax.random.normal(stream_key, dims, jnp.float32)
    if pieces:
        array = array * steps_of(stream_key, dims, pieces, -0.22, 0.18)
    return jnp.clip(array, -most, most).astype(kind)


def setup_inputs(seed: int = 0) -> dict:
    splits = jax.random.split(jax.random.key(seed), 4)
    return {
        "a_band": draw_a_band(jax.random.fold_in(splits[3], 71), 0),
        "p_tent": noise(splits[1], (BLOCKS, MODES, TILE), 0.15, 0.8984375, ((0, 256),)),
        "new_owner": draw_new_owner(jax.random.fold_in(splits[3], 71), 0),
    }


def reference(a_band, p_tent, new_owner):
    nb = a_band.shape[0]
    old_dev = jnp.arange(nb, dtype=jnp.int32) // BR_DEV
    key = (old_dev // N_MEMBER) * N_MEMBER + new_owner.astype(jnp.int32)
    order = jnp.argsort(key, stable=True)
    a_new = a_band[order]
    p_new = p_tent[order]
    dinv = 1.0 / jnp.diagonal(a_new[:, 1], axis1=1, axis2=2).astype(jnp.float32)
    p_rim = jnp.pad(p_new, ((1, 1), (0, 0), (0, 0))).astype(jnp.float32)
    p_self = p_new.astype(jnp.float32)
    tiles = []
    for k in range(3):
        prod = jnp.einsum("nij,ncj->nci", a_new[:, k].astype(jnp.float32), p_rim[k:k + nb])
        base = p_self if k == 1 else jnp.zeros_like(p_self)
        tiles.append(base - 0.6 * dinv[:, None, :] * prod)
    p_smooth = jnp.stack(tiles, 1).astype(jnp.bfloat16)
    s_rim = jnp.pad(p_smooth, ((1, 1), (0, 0), (0, 0), (0, 0))).astype(jnp.float32)
    ap = jnp.zeros((nb, 5, MODES, TILE), jnp.float32)
    for k in range(3):
        prod = jnp.einsum("nij,ntcj->ntci", a_new[:, k].astype(jnp.float32), s_rim[k:k + nb])
        ap = ap + jnp.pad(prod, ((0, 0), (k, 2 - k), (0, 0), (0, 0)))
    ap = ap.astype(jnp.bfloat16)
    both = jnp.concatenate([p_smooth, ap], 1)
    b_rim = jnp.pad(both, ((1, 1), (0, 0), (0, 0), (0, 0))).astype(jnp.float32)
    coarse = jnp.zeros((nb, 7, MODES, MODES), jnp.float32)
    for dn in (-1, 0, 1):
        near = b_rim[1 + dn:1 + dn + nb]
        term = jnp.einsum("nci,nedi->necd", near[:, 1 - dn], near[:, 3:8])
        coarse = coarse + jnp.pad(term, ((0, 0), (1 + dn, 1 - dn), (0, 0), (0, 0)))
    return p_smooth, coarse.reshape(nb, 7 * MODES * MODES)
```

```python
import functools

import jax
import jax.numpy as jnp
from jax import lax
from jax.experimental import pallas as pl
from jax.experimental.pallas import tpu as pltpu
from jax.sharding import PartitionSpec as P

ROWS = 192
WIDE = 256
TILE = 64
MODES = 6
MEMBERS = 64
SLOTS = 8
COLS = 3 * MODES * TILE
F32 = jnp.float32
BF16 = jnp.bfloat16
NT = (((1,), (1,)), ((), ()))
TN = (((0,), (0,)), ((), ()))
VMEM_BYTES = 56 * 1024 * 1024


def iota(shape, axis):
    return lax.broadcasted_iota(jnp.int32, shape, axis)


def ones_where(mask):
    return jnp.where(mask, 1.0, 0.0).astype(BF16)


def dot(a, b):
    return jnp.dot(a, b, preferred_element_type=F32)


def parts_of(x):
    high = x.astype(BF16)
    rest = x - high.astype(F32)
    mid = rest.astype(BF16)
    low = (rest - mid.astype(F32)).astype(BF16)
    return high, mid, low


def exact_dot(pick, x, dims, pick_first):
    total = None
    for part in parts_of(x):
        ab = (pick, part) if pick_first else (part, pick)
        prod = lax.dot_general(*ab, dims, preferred_element_type=F32)
        total = prod if total is None else total + prod
    return total


def ranks(owner_row):
    wide = jnp.broadcast_to(owner_row.astype(F32), (WIDE, WIDE))
    tall = wide.T[:ROWS]
    wide = wide[:ROWS]
    lane = iota((ROWS, WIDE), 1)
    row_l = jnp.where(lane < ROWS, lane, lane - TILE)
    row_s = iota((ROWS, WIDE), 0)
    same = wide == tall
    one = jnp.where(same, 1.0, 0.0)
    less, more = row_s < row_l, row_s > row_l
    rank_l = jnp.sum(jnp.where(less, one, 0.0), 0, keepdims=True)
    after_l = jnp.sum(jnp.where(more, one, 0.0), 0, keepdims=True)
    once = jnp.where(lane < ROWS, one, 0.0)
    rank_s = jnp.sum(jnp.where(more, once, 0.0), 1, keepdims=True)
    after_s = jnp.sum(jnp.where(less, once, 0.0), 1, keepdims=True)
    return dict(
        wide=wide[:1], tall=tall[:, :128], same=same, row_l=row_l, row_s=row_s,
        rank_l=rank_l, after_l=after_l, rank_s=rank_s, after_s=after_s,
    )


def rim_picks(r, me):
    lane = iota((ROWS, 128), 1)
    first, last = r["rank_s"] == 0.0, r["after_s"] == 0.0
    picks = []
    for half in (0, 1):
        slot = lane - TILE * half
        inside = (slot >= 0) & (slot < TILE)
        to_left = jnp.where(inside, slot + jnp.where(me == 0, 1, 0), -1).astype(F32)
        to_right = jnp.where(inside, slot - jnp.where(me == MEMBERS - 1, 1, 0), -1).astype(F32)
        left = ones_where((r["tall"] == to_left) & first)
        right = ones_where((r["tall"] == to_right) & last)
        far_first = (slot == TILE - 1) & (me == 0) & (r["tall"] == 0.0) & first
        far_last = (slot == 0) & (me == MEMBERS - 1) & (r["tall"] == MEMBERS - 1.0) & last
        far = ones_where(far_first | far_last)
        picks.append((left, right, far))
    return picks


def rims_of(rows, r, me):
    half = rows.shape[0] // 2
    top, bottom = rim_picks(r, me)
    return [
        (dot(rows[:half], a) + dot(rows[half:], b)).astype(BF16) for a, b in zip(top, bottom)
    ]


def neighbours(rows, from_left, from_right, far, r, me):
    half = rows.shape[0] // 2
    zero = jnp.zeros_like(far)
    from_left = from_left + jnp.where(me == MEMBERS - 1, zero, far)
    from_right = from_right + jnp.where(me == 0, zero, far)
    before = ones_where(r["same"] & (r["rank_s"] + 1.0 == r["rank_l"]))
    after = ones_where(r["same"] & (r["rank_s"] == r["rank_l"] + 1.0))
    here = ones_where(r["row_s"] == r["row_l"])
    bucket = iota((128, WIDE), 0)
    result = []
    for local, rim, edge in ((before, from_left, "rank_l"), (here, None, None), (after, from_right, "after_l")):
        own = dot(rows, local)
        if rim is not None:
            ends = []
            for side in (0, 1):
                want = bucket - TILE * side
                want = jnp.where((want >= 0) & (want < TILE), want, -1).astype(F32)
                ends.append(dot(rim, ones_where((want == r["wide"]) & (r[edge] == 0.0))))
            own = own + jnp.concatenate(ends, 0)
        result.append(own)
    return result


def set_wide(ref, k, value):
    for tile in (0, 1):
        part = value[:, 128 * tile : 128 * (tile + 1)]
        ref[tile, k] = part.reshape(-1, TILE, 128)


def set_groups(a_ref, group_ref):
    for k in range(3):
        for i in range(8):
            low, high = a_ref[k, i].astype(F32), a_ref[k, i + 8].astype(F32)
            group_ref[0, k, i] = low[:, :128]
            group_ref[1, k, i] = high[:, :128]
            group_ref[2, k, i] = jnp.concatenate([low[:, 128:], high[:, 128:]], 1)


def folded(terms):
    sub = iota((8, 128), 0)
    for shift in (1, 2, 4):
        keep = (sub & shift) == 0
        terms = [
            jnp.where(keep, x, y) + pltpu.roll(jnp.where(keep, y, x), shift, 0)
            for x, y in zip(terms[::2], terms[1::2])
        ]
    return terms[0]


def contracted(group_ref, wide_ref, g, tile, pairs, columns):
    totals = [[None] * 8 for _ in columns]
    for jb in range(TILE // 8):
        j = pl.ds(8 * jb, 8)
        for k, base in pairs:
            a = [group_ref[g, k, i, j, :] for i in range(8)]
            for n, column in enumerate(columns):
                x = wide_ref[tile, k, base + column, j, :]
                for i in range(8):
                    term = a[i] * x
                    totals[n][i] = term if totals[n][i] is None else totals[n][i] + term
    return [folded(t) for t in totals]


def ungrouped(out_ref, index):
    low, high, both = out_ref[0, index], out_ref[1, index], out_ref[2, index]
    top = jnp.concatenate([low, both[:, :TILE]], 1)
    bottom = jnp.concatenate([high, both[:, TILE:]], 1)
    return jnp.concatenate([top, bottom], 0)


def first_kernel(me_ref, owner_ref, p_ref, left_ref, right_ref, far_ref):
    r = ranks(owner_ref[...])
    me = me_ref[0]
    for ref, rim in zip((left_ref, right_ref, far_ref), rims_of(p_ref[...], r, me)):
        ref[...] = rim


def smooth_kernel(
    me_ref, owner_ref, a_ref, p_ref, from_left_ref, from_right_ref, far_ref,
    s_ref, left_out, right_out, far_out, group_ref, wide_ref, out_ref,
):
    ib = pl.program_id(0)
    me = me_ref[0]

    @pl.when(ib == 0)
    def _():
        r = ranks(owner_ref[...])
        near = neighbours(p_ref[...], from_left_ref[...], from_right_ref[...], far_ref[...], r, me)
        for k, value in enumerate(near):
            set_wide(wide_ref, k, value)

    set_groups(a_ref, group_ref)
    sub, lane = iota((8, 128), 0), iota((8, 128), 1)

    def one_group(g, carry):
        tile = jnp.where(g == 2, 1, 0)
        second = (g == 1) | ((g == 2) & (lane >= TILE))
        lower, upper = pl.ds(pl.multiple_of(16 * ib, 8), 8), pl.ds(pl.multiple_of(16 * ib + 8, 8), 8)
        diag = jnp.zeros((8, 128), F32)
        for i in range(8):
            entry = jnp.where(second, group_ref[g, 1, i, upper, :], group_ref[g, 1, i, lower, :])
            diag = jnp.where(sub == i, entry, diag)
        scale = 0.6 * (1.0 / diag)
        for k in range(3):
            for half in (0, 1):
                columns = [3 * half + c for c in range(3)]
                sums = contracted(group_ref, wide_ref, g, tile, [(k, 0)], columns)
                for c, total in zip(columns, sums):
                    value = scale * total
                    if k == 1:
                        own = jnp.where(second, wide_ref[tile, 1, c, upper, :], wide_ref[tile, 1, c, lower, :])
                        value = own - value
                    else:
                        value = 0.0 - value
                    out_ref[g, 6 * k + c] = value
        return carry

    lax.fori_loop(0, 3, one_group, 0)
    rows = pl.ds(pl.multiple_of(16 * ib, 16), 16)
    for index in range(18):
        s_ref[index, rows, :] = ungrouped(out_ref, index).astype(BF16)

    @pl.when(ib == pl.num_programs(0) - 1)
    def _():
        r = ranks(owner_ref[...])
        flat = s_ref[...].reshape(COLS, ROWS)
        for ref, rim in zip((left_out, right_out, far_out), rims_of(flat, r, me)):
            ref[...] = rim


def slot_grid(width):
    spot = iota((MEMBERS * SLOTS, width), 0)
    return (spot // SLOTS).astype(F32), (spot % SLOTS).astype(F32)


def pack_kernel(owner_ref, s_ref, out_ref):
    r = ranks(owner_ref[...])
    member, slot = slot_grid(ROWS)
    owner, rank = r["wide"][:, :ROWS], r["rank_l"][:, :ROWS]
    mine = owner == member
    pick = ones_where(mine & (rank == slot))
    count = jnp.sum(jnp.where(mine, 1.0, 0.0), 1, keepdims=True)
    spot, lane = iota((MEMBERS * SLOTS, 128), 0) % SLOTS, iota((MEMBERS * SLOTS, 128), 1)
    for block in range(COLS // 128):
        value = lax.dot_general(
            pick, s_ref[128 * block : 128 * (block + 1), :], NT, preferred_element_type=F32
        )
        if block == 0:
            value = jnp.where((spot == 6) & (lane == 0), count, value)
        out_ref[:, 128 * block : 128 * (block + 1)] = value.astype(BF16)


OFFSETS = [[(k, 6 * (e - k)) for k in range(3) if 0 <= e - k <= 2] for e in range(5)]


def product_kernel(
    me_ref, owner_ref, a_ref, s_ref, from_left_ref, from_right_ref, far_ref,
    out_ref, far_out, group_ref, wide_ref, ap_ref, own_ref, term_ref,
):
    ib = pl.program_id(0)
    me = me_ref[0]

    @pl.when(ib == 0)
    def _():
        r = ranks(owner_ref[...])
        near = neighbours(s_ref[...], from_left_ref[...], from_right_ref[...], far_ref[...], r, me)
        for k, value in enumerate(near):
            set_wide(wide_ref, k, value)
        term_ref[...] = jnp.zeros_like(term_ref)

    set_groups(a_ref, group_ref)
    lane = iota((8, 128), 1)

    def one_group(step, carry):
        g, half = step // 2, step % 2
        tile = jnp.where(g == 2, 1, 0)
        for e in range(5):
            columns = [3 * half + c for c in range(3)]
            sums = contracted(group_ref, wide_ref, g, tile, OFFSETS[e], columns)
            for c, total in zip(columns, sums):
                ap_ref[g, ib, 6 * e + c] = total.astype(BF16).astype(F32)
        second = (g == 1) | ((g == 2) & (lane >= TILE))
        lower, upper = pl.ds(pl.multiple_of(16 * ib, 8), 8), pl.ds(pl.multiple_of(16 * ib + 8, 8), 8)
        for c in range(9):
            column = 9 * half + c
            own_ref[g, ib, column] = jnp.where(
                second, wide_ref[tile, 1, column, upper, :], wide_ref[tile, 1, column, lower, :]
            )
        return carry

    lax.fori_loop(0, 6, one_group, 0)

    @pl.when(ib == pl.num_programs(0) - 1)
    def _():
        def one_pair(step, carry):
            k, e = step // 5, step % 5
            for c in range(6):
                near, far = [None] * 6, [None] * 6
                for block in range(TILE // 16):
                    for g in range(3):
                        x = own_ref[g, block, 6 * k + c]
                        for d in range(6):
                            term = x * ap_ref[g, block, 6 * e + d]
                            sums = far if g == 2 else near
                            sums[d] = term if sums[d] is None else sums[d] + term
                for d in range(6):
                    row = slice(6 * c + d, 6 * c + d + 1)
                    tail = jnp.sum(far[d], 0, keepdims=True)
                    term_ref[step, row, 0:128] = jnp.sum(near[d], 0, keepdims=True)
                    term_ref[step, row, 128:ROWS] = tail[:, :TILE] + tail[:, TILE:]
            return carry

        lax.fori_loop(0, 15, one_pair, 0)
        r = ranks(owner_ref[...])
        owner, rank, after = (r[n][:, :ROWS] for n in ("wide", "rank_l", "after_l"))
        member, slot = slot_grid(ROWS)
        mine, row_slot = owner == member, slot < 6.0
        here = ones_where(mine & (rank == slot))
        back_to = member + jnp.where(me == 0, 1.0, 0.0)
        on_to = member - jnp.where(me == MEMBERS - 1, 1.0, 0.0)
        back = (mine & row_slot & (rank == slot + 1.0)) | ((slot == 6.0) & (owner == back_to) & (rank == 0.0))
        on = (mine & row_slot & (rank == slot - 1.0) & (after > 0.0)) | (
            (slot == 7.0) & (owner == on_to) & (after == 0.0)
        )
        picks = [ones_where(back), here, ones_where(on)]
        terms = []
        for k in range(3):
            pieces = [term_ref[5 * k + e][:36, :ROWS] for e in range(5)]
            pieces.append(jnp.zeros((4 + 36 * k, ROWS), F32))
            if k < 2:
                pieces.insert(0, jnp.zeros((72 - 36 * k, ROWS), F32))
            terms.append(jnp.concatenate(pieces, 0))
        total = None
        for k in range(3):
            prod = exact_dot(picks[k], terms[k], NT, True)
            total = prod if total is None else total + prod
        out_ref[...] = total
        top = iota((8, ROWS), 0) == 0
        far_back = ones_where(top & (me == 0) & (owner == 0.0) & (rank == 0.0))
        far_on = ones_where(top & (me == MEMBERS - 1) & (owner == MEMBERS - 1.0) & (after == 0.0))
        far_out[...] = exact_dot(far_back, terms[0], NT, True) + exact_dot(
            far_on, terms[2], NT, True
        )


def arrivals(counts):
    size = MEMBERS * SLOTS
    spot, lane = iota((size, 128), 0) % SLOTS, iota((size, 128), 1)
    marked = jnp.where((spot == 6) & (lane == 0), counts.astype(F32), 0.0).astype(BF16)
    source, other = iota((size, size), 0) // SLOTS, iota((size, size), 1) // SLOTS
    start = dot(ones_where(other < source), marked)[:, :1]
    count = dot(ones_where(other == source), marked)[:, :1]
    slot = (iota((size, 1), 0) % SLOTS).astype(F32)
    return slot, start, count


def unpack_smooth_kernel(recv_ref, out_ref):
    slot, start, count = arrivals(recv_ref[:, :128])
    place = jnp.where(slot < count, start + slot, -1.0)
    pick = ones_where(place == iota((MEMBERS * SLOTS, ROWS), 1).astype(F32))
    for block in range(COLS // 128):
        at = slice(128 * block, 128 * (block + 1))
        value = lax.dot_general(recv_ref[:, at], pick, TN, preferred_element_type=F32)
        out_ref[at, :] = value.astype(BF16)


def unpack_coarse_kernel(me_ref, recv_ref, sums_ref, far_ref, out_ref):
    me = me_ref[0]
    slot, start, count = arrivals(recv_ref[...])
    place = jnp.where(slot < count, start + slot, -1.0)
    place = jnp.where(slot == 6.0, jnp.where(start == 0.0, ROWS - 1.0, start - 1.0), place)
    stop = start + count
    place = jnp.where(slot == 7.0, jnp.where(stop == float(ROWS), 0.0, stop), place)
    pick = ones_where(place == iota((MEMBERS * SLOTS, ROWS), 1).astype(F32))
    total = exact_dot(pick, sums_ref[...], TN, True)
    row = iota((ROWS, WIDE), 0)
    edge = jnp.where(me == 0, 0, ROWS - 1)
    far = jnp.broadcast_to(far_ref[0:1, :], (ROWS, WIDE))
    total = total + jnp.where(row == edge, far, 0.0)
    out_ref[...] = total[:, :252]


def call(kernel, outs, args, grid=None, in_specs=None, scratch=(), flops=0, name=None):
    whole = lambda shape: pl.BlockSpec(shape, lambda *_: (0,) * len(shape))
    specs = []
    for n, arg in enumerate(args):
        spec = None if in_specs is None else in_specs.get(n)
        if spec is None:
            spec = pl.BlockSpec(memory_space=pltpu.SMEM) if arg.shape == (1,) else whole(arg.shape)
        specs.append(spec)
    moved = sum(a.size * a.dtype.itemsize for a in args) + sum(o.size * o.dtype.itemsize for o in outs)
    return pl.pallas_call(
        kernel,
        grid=(1,) if grid is None else grid,
        in_specs=specs,
        out_specs=[whole(o.shape) for o in outs],
        out_shape=outs,
        scratch_shapes=list(scratch),
        compiler_params=pltpu.CompilerParams(vmem_limit_bytes=VMEM_BYTES),
        cost_estimate=pl.CostEstimate(flops=flops, bytes_accessed=moved, transcendentals=0),
        name=name,
    )(*args)


def shaped(shape, dtype=BF16):
    return jax.ShapeDtypeStruct(shape, dtype)


def exchanged(left, right, far, groups):
    ring = MEMBERS
    axes = ("group", "member")
    to_left = [(g * ring + i, g * ring + (i - 1) % ring) for g in range(groups) for i in range(ring)]
    to_right = [(b, a) for a, b in to_left]
    across = []
    for g in range(groups - 1):
        across += [(g * ring + ring - 1, (g + 1) * ring), ((g + 1) * ring, g * ring + ring - 1)]
    from_right = lax.ppermute(left, axes, to_left)
    from_left = lax.ppermute(right, axes, to_right)
    return from_left, from_right, lax.ppermute(far, axes, across), across


def per_device(a_band, p_tent, new_owner):
    groups = lax.axis_size("group")
    me = lax.axis_index("member").astype(jnp.int32).reshape(1)
    owner = jnp.concatenate([new_owner, new_owner[128:]]).reshape(1, WIDE)
    a = a_band.transpose(1, 2, 3, 0)
    p = p_tent.transpose(1, 2, 0).reshape(MODES * TILE, ROWS)
    a_spec = pl.BlockSpec((3, 16, TILE, ROWS), lambda i: (0, i, 0, 0))
    grid = (TILE // 16,)
    group_scratch = pltpu.VMEM((3, 3, 8, TILE, 128), F32)

    rim = shaped((MODES * TILE // 2, 128))
    left, right, far = call(first_kernel, [rim] * 3, (me, owner, p), name="rims")
    from_left, from_right, from_far, across = exchanged(left, right, far, groups)

    rim = shaped((COLS // 2, 128))
    s, left, right, far = call(
        smooth_kernel,
        [shaped((18, TILE, ROWS)), rim, rim, rim],
        (me, owner, a, p, from_left, from_right, from_far),
        grid=grid,
        in_specs={2: a_spec},
        scratch=[
            group_scratch,
            pltpu.VMEM((2, 3, MODES, TILE, 128), F32),
            pltpu.VMEM((3, 18, 8, 128), F32),
        ],
        flops=10**9,
        name="smooth",
    )
    from_left, from_right, from_far, _ = exchanged(left, right, far, groups)
    s = s.reshape(COLS, ROWS)
    (packed,) = call(pack_kernel, [shaped((MEMBERS * SLOTS, COLS))], (owner, s), name="pack")
    packed, from_left, from_right, from_far = lax.optimization_barrier(
        (packed, from_left, from_right, from_far)
    )
    recv = lax.all_to_all(
        packed.reshape(MEMBERS, SLOTS, COLS), "member", split_axis=0, concat_axis=0, tiled=True
    ).reshape(MEMBERS * SLOTS, COLS)

    sums, far = call(
        product_kernel,
        [shaped((MEMBERS * SLOTS, WIDE), F32), shaped((8, WIDE), F32)],
        (me, owner, a, s, from_left, from_right, from_far),
        grid=grid,
        in_specs={2: a_spec},
        scratch=[
            group_scratch,
            pltpu.VMEM((2, 3, 18, TILE, 128), F32),
            pltpu.VMEM((3, TILE // 16, 30, 8, 128), F32),
            pltpu.VMEM((3, TILE // 16, 18, 8, 128), F32),
            pltpu.VMEM((15, 40, WIDE), F32),
        ],
        flops=10**10,
        name="product",
    )
    far = lax.ppermute(far, ("group", "member"), across)
    sums = lax.all_to_all(
        sums.reshape(MEMBERS, SLOTS, WIDE), "member", split_axis=0, concat_axis=0, tiled=True
    ).reshape(MEMBERS * SLOTS, WIDE)
    (smooth,) = call(unpack_smooth_kernel, [shaped((COLS, ROWS))], (recv,), name="unpack_smooth")
    (coarse,) = call(
        unpack_coarse_kernel,
        [shaped((ROWS, 252), F32)],
        (me, recv, sums, far),
        in_specs={1: pl.BlockSpec((MEMBERS * SLOTS, 128), lambda i: (0, 0))},
        name="unpack_coarse",
    )
    return smooth.reshape(3, MODES, TILE, ROWS).transpose(3, 0, 1, 2), coarse


def solution(mesh):
    in_specs = (
        P(("group", "member"), None, None, None),
        P(("group", "member"), None, None),
        P(("group", "member")),
    )
    out_specs = (P(("group", "member"), None, None, None), P(("group", "member"), None))
    return jax.shard_map(
        per_device, mesh=mesh, in_specs=in_specs, out_specs=out_specs, check_vma=False
    )
```

```python
import jax
import jax.numpy as jnp
from jax import lax
from jax.experimental import pallas as pl
from jax.experimental.pallas import tpu as pltpu
from jax.sharding import PartitionSpec as P

ROWS = 192
WIDE = 256
TILE = 64
MODES = 6
MEMBERS = 64
SLOTS = 8
COLS = 3 * MODES * TILE
F32 = jnp.float32
BF16 = jnp.bfloat16
NT = (((1,), (1,)), ((), ()))
TN = (((0,), (0,)), ((), ()))
MIB = 1024 * 1024
PACKED = 56


def iota(shape, axis):
    return lax.broadcasted_iota(jnp.int32, shape, axis)


def ones_where(mask):
    return jnp.where(mask, 1.0, 0.0).astype(BF16)


def dot(a, b):
    return jnp.dot(a, b, preferred_element_type=F32)


def parts_of(x):
    high = x.astype(BF16)
    rest = x - high.astype(F32)
    mid = rest.astype(BF16)
    low = (rest - mid.astype(F32)).astype(BF16)
    return high, mid, low


def exact_dot(pick, x, dims, pick_first):
    total = None
    for part in parts_of(x):
        ab = (pick, part) if pick_first else (part, pick)
        prod = lax.dot_general(*ab, dims, preferred_element_type=F32)
        total = prod if total is None else total + prod
    return total


def rank_arrays(owner_row):
    owner_row = owner_row.astype(F32)
    owner_row = jnp.concatenate([owner_row, owner_row[:, 128:]], 1)
    wide = jnp.broadcast_to(owner_row, (WIDE, WIDE))
    tall = wide.T[:ROWS]
    wide = wide[:ROWS]
    lane = iota((ROWS, WIDE), 1)
    row_l = jnp.where(lane < ROWS, lane, lane - TILE)
    row_s = iota((ROWS, WIDE), 0)
    one = jnp.where(wide == tall, 1.0, 0.0)
    less, more = row_s < row_l, row_s > row_l
    rank_l = jnp.sum(jnp.where(less, one, 0.0), 0, keepdims=True)
    after_l = jnp.sum(jnp.where(more, one, 0.0), 0, keepdims=True)
    once = jnp.where(lane < ROWS, one, 0.0)
    rank_s = jnp.sum(jnp.where(more, once, 0.0), 1, keepdims=True)
    after_s = jnp.sum(jnp.where(less, once, 0.0), 1, keepdims=True)
    return (wide[:1], rank_l, after_l), (tall[:, :1], rank_s, after_s)


class Order:
    def __init__(self, wide_ref, tall_ref):
        self.owner_l, self.rank_l, self.after_l = (wide_ref[n : n + 1, :] for n in range(3))
        self.owner_s, self.rank_s, self.after_s = (tall_ref[:, n : n + 1] for n in range(3))


def rim_picks(r, me):
    lane = iota((ROWS, 128), 1)
    first, last = r.rank_s == 0.0, r.after_s == 0.0
    even = me % 2 == 0
    picks = []
    for half in (0, 1):
        slot = lane - TILE * half
        inside = (slot >= 0) & (slot < TILE)
        to_left = jnp.where(inside, slot + jnp.where(me == 0, 1, 0), -1).astype(F32)
        to_right = jnp.where(inside, slot - jnp.where(me == MEMBERS - 1, 1, 0), -1).astype(F32)
        left = jnp.where((r.owner_s == to_left) & first, 1.0, 0.0)
        right = jnp.where((r.owner_s == to_right) & last, 1.0, 0.0)
        near = jnp.where(even, right, left).astype(BF16)
        far = jnp.where(even, left, right).astype(BF16)
        picks.append((near, far))
    return picks


def far_pick(r, me, width):
    top = iota((8, width), 0) == 0
    owner, rank, after = r.owner_l[:, :width], r.rank_l[:, :width], r.after_l[:, :width]
    head = top & (me == 0) & (owner == 0.0) & (rank == 0.0)
    tail = top & (me == MEMBERS - 1) & (owner == MEMBERS - 1.0) & (after == 0.0)
    return ones_where(head), ones_where(tail)


def rims_of(rows, r, me):
    half = rows.shape[0] // 2
    top, bottom = rim_picks(r, me)
    rims = [(dot(rows[:half], a) + dot(rows[half:], b)).astype(BF16) for a, b in zip(top, bottom)]
    head, tail = far_pick(r, me, ROWS)
    far = lax.dot_general(head + tail, rows, NT, preferred_element_type=F32).astype(BF16)
    return [far] + rims[::-1]


def neighbours(rows, near, away, far, r, me):
    lane = iota((ROWS, WIDE), 1)
    row_l = jnp.where(lane < ROWS, lane, lane - TILE)
    same = r.owner_l == r.owner_s
    before = ones_where(same & (r.rank_s + 1.0 == r.rank_l))
    after = ones_where(same & (r.rank_s == r.rank_l + 1.0))
    here = ones_where(iota((ROWS, WIDE), 0) == row_l)
    bucket = iota((128, WIDE), 0)
    even = me % 2 == 0
    from_left = jnp.where(even, away, near)
    from_right = jnp.where(even, near, away)
    head, tail = far_pick(r, me, WIDE)
    result = []
    for local, rim, edge, end in (
        (before, from_left, r.rank_l, head), (here, None, None, None), (after, from_right, r.after_l, tail)
    ):
        own = dot(rows, local)
        if rim is not None:
            ends = []
            for side in (0, 1):
                want = bucket - TILE * side
                want = jnp.where((want >= 0) & (want < TILE), want, -1).astype(F32)
                ends.append(dot(rim, ones_where((want == r.owner_l) & (edge == 0.0))))
            own = own + jnp.concatenate(ends, 0)
            own = own + lax.dot_general(far, end, TN, preferred_element_type=F32)
        result.append(own)
    return result


def set_wide(ref, k, value):
    for tile in (0, 1):
        part = value[:, 128 * tile : 128 * (tile + 1)]
        ref[tile, k] = part.reshape(-1, TILE, 128)


def chunk_copy(a_hbm, a_ref, sems, n):
    return pltpu.make_async_copy(a_hbm.at[:, pl.ds(16 * n, 16)], a_ref.at[:, pl.ds(16 * n, 16)], sems.at[n])


def start_copies(a_hbm, a_ref, sems):
    for n in range(TILE // 16):
        chunk_copy(a_hbm, a_ref, sems, n).start()


def set_groups(a_ref, ib, group_ref):
    for k in range(3):
        for i in range(8):
            low, high = (a_ref[k, 16 * ib + i + n].astype(F32) for n in (0, 8))
            group_ref[0, k, i] = low[:, :128]
            group_ref[1, k, i] = high[:, :128]
            group_ref[2, k, i] = jnp.concatenate([low[:, 128:], high[:, 128:]], 1)


def folded(terms):
    sub = iota((8, 128), 0)
    for shift in (1, 2, 4):
        keep = (sub & shift) == 0
        terms = [
            jnp.where(keep, x, y) + pltpu.roll(jnp.where(keep, y, x), shift, 0)
            for x, y in zip(terms[::2], terms[1::2])
        ]
    return terms[0]


def contracted(group_ref, wide_ref, g, tile, pairs, columns):
    totals = [[None] * 8 for _ in columns]
    for jb in range(TILE // 8):
        j = pl.ds(8 * jb, 8)
        for k, base in pairs:
            a = [group_ref[g, k, i, j, :] for i in range(8)]
            for n, column in enumerate(columns):
                x = wide_ref[tile, k, base + column, j, :]
                for i in range(8):
                    term = a[i] * x
                    totals[n][i] = term if totals[n][i] is None else totals[n][i] + term
    return [folded(t) for t in totals]


def ungrouped(out_ref, index):
    low, high, both = out_ref[0, index], out_ref[1, index], out_ref[2, index]
    top = jnp.concatenate([low, both[:, :TILE]], 1)
    bottom = jnp.concatenate([high, both[:, TILE:]], 1)
    return jnp.concatenate([top, bottom], 0)


def first_kernel(me_ref, owner_ref, p_ref, wide_ref, tall_ref, far_out, away_out, near_out):
    rows, columns = rank_arrays(owner_ref[...])
    wide_ref[...] = jnp.zeros_like(wide_ref)
    for n in range(3):
        wide_ref[n : n + 1, :] = rows[n]
    lane = iota((ROWS, 128), 1)
    tall_ref[...] = jnp.where(lane == 0, columns[0], jnp.where(lane == 1, columns[1], columns[2]))
    r = Order(wide_ref, tall_ref)
    for ref, rim in zip((far_out, away_out, near_out), rims_of(p_ref[...], r, me_ref[0])):
        ref[...] = rim


def smooth_kernel(
    me_ref, order_l_ref, order_s_ref, a_hbm, p_ref, far_ref, away_ref, near_ref,
    s_ref, far_out, away_out, near_out, a_ref, sems, group_ref, wide_ref, out_ref,
):
    ib = pl.program_id(0)
    me = me_ref[0]

    @pl.when(ib == 0)
    def _():
        start_copies(a_hbm, a_ref, sems)
        r = Order(order_l_ref, order_s_ref)
        near = neighbours(p_ref[...], near_ref[...], away_ref[...], far_ref[...], r, me)
        for k, value in enumerate(near):
            set_wide(wide_ref, k, value)

    chunk_copy(a_hbm, a_ref, sems, ib).wait()
    set_groups(a_ref, ib, group_ref)
    sub, lane = iota((8, 128), 0), iota((8, 128), 1)

    def one_group(g, carry):
        tile = jnp.where(g == 2, 1, 0)
        second = (g == 1) | ((g == 2) & (lane >= TILE))
        lower, upper = pl.ds(pl.multiple_of(16 * ib, 8), 8), pl.ds(pl.multiple_of(16 * ib + 8, 8), 8)
        diag = jnp.zeros((8, 128), F32)
        for i in range(8):
            entry = jnp.where(second, group_ref[g, 1, i, upper, :], group_ref[g, 1, i, lower, :])
            diag = jnp.where(sub == i, entry, diag)
        scale = 0.6 * (1.0 / diag)
        for k in range(3):
            for half in (0, 1):
                columns = [3 * half + c for c in range(3)]
                sums = contracted(group_ref, wide_ref, g, tile, [(k, 0)], columns)
                for c, total in zip(columns, sums):
                    value = scale * total
                    if k == 1:
                        own = jnp.where(second, wide_ref[tile, 1, c, upper, :], wide_ref[tile, 1, c, lower, :])
                        value = own - value
                    else:
                        value = 0.0 - value
                    out_ref[g, 6 * k + c] = value
        return carry

    lax.fori_loop(0, 3, one_group, 0)
    rows = pl.ds(pl.multiple_of(16 * ib, 16), 16)
    for index in range(18):
        s_ref[index, rows, :] = ungrouped(out_ref, index).astype(BF16)

    @pl.when(ib == pl.num_programs(0) - 1)
    def _():
        r = Order(order_l_ref, order_s_ref)
        flat = s_ref[...].reshape(COLS, ROWS)
        for ref, rim in zip((far_out, away_out, near_out), rims_of(flat, r, me)):
            ref[...] = rim


def slot_grid(width):
    spot = iota((MEMBERS * SLOTS, width), 0)
    return (spot // SLOTS).astype(F32), (spot % SLOTS).astype(F32)


def pack_kernel(order_l_ref, s_ref, out_ref):
    member, slot = slot_grid(ROWS)
    owner, rank = order_l_ref[0:1, :ROWS], order_l_ref[1:2, :ROWS]
    mine = owner == member
    pick = ones_where(mine & (rank == slot))
    count = jnp.sum(jnp.where(mine, 1.0, 0.0), 1, keepdims=True)
    for block in range(COLS // 128):
        value = lax.dot_general(
            pick, s_ref[128 * block : 128 * (block + 1), :], NT, preferred_element_type=F32
        ).reshape(MEMBERS, SLOTS, 128)
        out_ref[:, 6 * block : 6 * block + 6, :] = value[:, :6, :].astype(BF16)
    counts = jnp.broadcast_to(count, (MEMBERS * SLOTS, 128)).reshape(MEMBERS, SLOTS, 128)
    out_ref[:, 54:56, :] = counts[:, :2, :].astype(BF16)


OFFSETS = [[(k, 6 * (e - k)) for k in range(3) if 0 <= e - k <= 2] for e in range(5)]


def product_kernel(
    me_ref, order_l_ref, order_s_ref, a_hbm, s_ref, far_ref, away_ref, near_ref,
    out_ref, far_out, a_ref, sems, group_ref, wide_ref, ap_ref, own_ref, term_ref,
):
    ib = pl.program_id(0)
    me = me_ref[0]

    @pl.when(ib == 0)
    def _():
        start_copies(a_hbm, a_ref, sems)
        r = Order(order_l_ref, order_s_ref)
        near = neighbours(s_ref[...], near_ref[...], away_ref[...], far_ref[...], r, me)
        for k, value in enumerate(near):
            set_wide(wide_ref, k, value)
        term_ref[...] = jnp.zeros_like(term_ref)

    chunk_copy(a_hbm, a_ref, sems, ib).wait()
    set_groups(a_ref, ib, group_ref)
    lane = iota((8, 128), 1)

    def one_group(step, carry):
        g, half = step // 2, step % 2
        tile = jnp.where(g == 2, 1, 0)
        for e in range(5):
            columns = [3 * half + c for c in range(3)]
            sums = contracted(group_ref, wide_ref, g, tile, OFFSETS[e], columns)
            for c, total in zip(columns, sums):
                ap_ref[g, ib, 6 * e + c] = total.astype(BF16).astype(F32)
        second = (g == 1) | ((g == 2) & (lane >= TILE))
        lower, upper = pl.ds(pl.multiple_of(16 * ib, 8), 8), pl.ds(pl.multiple_of(16 * ib + 8, 8), 8)
        for c in range(9):
            column = 9 * half + c
            own_ref[g, ib, column] = jnp.where(
                second, wide_ref[tile, 1, column, upper, :], wide_ref[tile, 1, column, lower, :]
            )
        return carry

    lax.fori_loop(0, 6, one_group, 0)

    @pl.when(ib == pl.num_programs(0) - 1)
    def _():
        def one_pair(step, carry):
            k, e = step // 5, step % 5
            for c in range(6):
                near, far = [None] * 6, [None] * 6
                for block in range(TILE // 16):
                    for g in range(3):
                        x = own_ref[g, block, 6 * k + c]
                        for d in range(6):
                            term = x * ap_ref[g, block, 6 * e + d]
                            sums = far if g == 2 else near
                            sums[d] = term if sums[d] is None else sums[d] + term
                for d in range(6):
                    row = slice(6 * c + d, 6 * c + d + 1)
                    tail = jnp.sum(far[d], 0, keepdims=True)
                    term_ref[step, row, 0:128] = jnp.sum(near[d], 0, keepdims=True)
                    term_ref[step, row, 128:ROWS] = tail[:, :TILE] + tail[:, TILE:]
            return carry

        lax.fori_loop(0, 15, one_pair, 0)
        r = Order(order_l_ref, order_s_ref)
        owner, rank, after = (x[:, :ROWS] for x in (r.owner_l, r.rank_l, r.after_l))
        member, slot = slot_grid(ROWS)
        mine, row_slot = owner == member, slot < 6.0
        here = ones_where(mine & (rank == slot))
        back_to = member + jnp.where(me == 0, 1.0, 0.0)
        on_to = member - jnp.where(me == MEMBERS - 1, 1.0, 0.0)
        back = (mine & row_slot & (rank == slot + 1.0)) | ((slot == 6.0) & (owner == back_to) & (rank == 0.0))
        on = (mine & row_slot & (rank == slot - 1.0) & (after > 0.0)) | (
            (slot == 7.0) & (owner == on_to) & (after == 0.0)
        )
        picks = [ones_where(back), here, ones_where(on)]
        terms = []
        for k in range(3):
            pieces = [term_ref[5 * k + e][:36, :ROWS] for e in range(5)]
            pieces.append(jnp.zeros((4 + 36 * k, ROWS), F32))
            if k < 2:
                pieces.insert(0, jnp.zeros((72 - 36 * k, ROWS), F32))
            terms.append(jnp.concatenate(pieces, 0))
        total = None
        for k in range(3):
            prod = exact_dot(picks[k], terms[k], NT, True)
            total = prod if total is None else total + prod
        out_ref[...] = total
        head, tail = far_pick(r, me, ROWS)
        far_out[...] = exact_dot(head, terms[0], NT, True) + exact_dot(tail, terms[2], NT, True)


def unpack_smooth_kernel(recv_ref, out_ref, pick_out):
    size = MEMBERS * SLOTS
    count = jnp.broadcast_to(recv_ref[:, 54:55, :].astype(F32), (MEMBERS, SLOTS, 128)).reshape(size, 128)
    source, other = iota((size, size), 0) // SLOTS, iota((size, size), 1) // SLOTS
    first_slot = iota((size, size), 1) % SLOTS == 0
    earlier = ones_where((other < source) & first_slot)
    start = dot(earlier, count.astype(BF16))[:, :1]
    count = count[:, :1]
    slot = (iota((size, 1), 0) % SLOTS).astype(F32)
    place = jnp.where(slot < count, start + slot, -1.0)
    column = iota((size, ROWS), 1).astype(F32)
    pick = ones_where(place == column)
    for block in range(COLS // 128):
        rows = recv_ref[:, 6 * block : 6 * block + 6, :].astype(F32)
        rows = jnp.concatenate([rows, jnp.zeros((MEMBERS, 2, 128), F32)], 1).reshape(size, 128)
        value = lax.dot_general(rows.astype(BF16), pick, TN, preferred_element_type=F32)
        out_ref[128 * block : 128 * (block + 1), :] = value.astype(BF16)
    place = jnp.where(slot == 6.0, jnp.where(start == 0.0, ROWS - 1.0, start - 1.0), place)
    stop = start + count
    place = jnp.where(slot == 7.0, jnp.where(stop == float(ROWS), 0.0, stop), place)
    column = iota((size, WIDE), 1).astype(F32)
    pick_out[...] = jnp.where(place == column, 1.0, 0.0).T[:ROWS].astype(BF16)


def unpack_coarse_kernel(me_ref, pick_ref, sums_ref, far_ref, out_ref):
    me = me_ref[0]
    total = exact_dot(pick_ref[...], sums_ref[...], (((1,), (0,)), ((), ())), True)
    row = iota((ROWS, WIDE), 0)
    edge = jnp.where(me == 0, 0, ROWS - 1)
    far = jnp.broadcast_to(far_ref[0:1, :], (ROWS, WIDE))
    total = total + jnp.where(row == edge, far, 0.0)
    out_ref[...] = total[:, :252]


def call(kernel, outs, args, grid=None, in_specs=None, scratch=(), flops=0, mib=16, name=None):
    whole = lambda shape: pl.BlockSpec(shape, lambda *_: (0,) * len(shape))
    specs = []
    for n, arg in enumerate(args):
        spec = None if in_specs is None else in_specs.get(n)
        if spec is None:
            spec = pl.BlockSpec(memory_space=pltpu.SMEM) if arg.shape == (1,) else whole(arg.shape)
        specs.append(spec)
    moved = sum(a.size * a.dtype.itemsize for a in args) + sum(o.size * o.dtype.itemsize for o in outs)
    return pl.pallas_call(
        kernel,
        grid=(1,) if grid is None else grid,
        in_specs=specs,
        out_specs=[whole(o.shape) for o in outs],
        out_shape=outs,
        scratch_shapes=list(scratch),
        compiler_params=pltpu.CompilerParams(vmem_limit_bytes=mib * MIB),
        cost_estimate=pl.CostEstimate(flops=flops, bytes_accessed=moved, transcendentals=0),
        name=name,
    )(*args)


def shaped(shape, dtype=BF16):
    return jax.ShapeDtypeStruct(shape, dtype)


def swaps(groups):
    ring, axes = MEMBERS, range(groups)
    both = lambda pairs: [q for a, b in pairs for q in ((a, b), (b, a))]
    across = both([(g * ring - 1, g * ring) for g in range(1, groups)])
    away = both([(g * ring + i, g * ring + (i + 1) % ring) for g in axes for i in range(1, ring, 2)])
    near = both([(g * ring + i, g * ring + i + 1) for g in axes for i in range(0, ring, 2)])
    return across, away, near


def per_device(a_band, p_tent, new_owner):
    axes = ("group", "member")
    across, away_pairs, near_pairs = swaps(lax.axis_size("group"))
    me = lax.axis_index("member").astype(jnp.int32).reshape(1)
    a = a_band.transpose(1, 2, 3, 0)
    p = p_tent.transpose(1, 2, 0).reshape(MODES * TILE, ROWS)
    a_spec = pl.BlockSpec(memory_space=pltpu.HBM)
    grid = (TILE // 16,)
    a_scratch = [
        pltpu.VMEM((3, TILE, TILE, ROWS), BF16),
        pltpu.SemaphoreType.DMA((TILE // 16,)),
        pltpu.VMEM((3, 3, 8, TILE, 128), F32),
    ]

    def exchanged(far, away, near):
        far = lax.ppermute(far, axes, across)
        away = lax.ppermute(away, axes, away_pairs)
        return far, away, lax.ppermute(near, axes, near_pairs)

    def rims(length):
        return [shaped((8, length)), shaped((length // 2, 128)), shaped((length // 2, 128))]

    order_l, order_s, *sent = call(
        first_kernel,
        [shaped((8, WIDE), F32), shaped((ROWS, 128), F32)] + rims(MODES * TILE),
        (me, new_owner.reshape(1, ROWS), p),
        name="rims",
    )
    got = exchanged(*sent)

    s, *sent = call(
        smooth_kernel,
        [shaped((18, TILE, ROWS))] + rims(COLS),
        (me, order_l, order_s, a, p, *got),
        grid=grid,
        in_specs={3: a_spec},
        scratch=[
            *a_scratch,
            pltpu.VMEM((2, 3, MODES, TILE, 128), F32),
            pltpu.VMEM((3, 18, 8, 128), F32),
        ],
        flops=10**9,
        mib=50,
        name="smooth",
    )
    got = exchanged(*sent)
    s = s.reshape(COLS, ROWS)
    (packed,) = call(pack_kernel, [shaped((MEMBERS, PACKED, 128))], (order_l, s), name="pack")
    packed, *got = lax.optimization_barrier((packed, *got))
    recv = lax.all_to_all(packed, "member", split_axis=0, concat_axis=0, tiled=True)

    sums, far = call(
        product_kernel,
        [shaped((MEMBERS * SLOTS, WIDE), F32), shaped((8, WIDE), F32)],
        (me, order_l, order_s, a, s, *got),
        grid=grid,
        in_specs={3: a_spec},
        scratch=[
            *a_scratch,
            pltpu.VMEM((2, 3, 18, TILE, 128), F32),
            pltpu.VMEM((3, TILE // 16, 30, 8, 128), F32),
            pltpu.VMEM((3, TILE // 16, 18, 8, 128), F32),
            pltpu.VMEM((15, 40, WIDE), F32),
        ],
        flops=10**10,
        mib=50,
        name="product",
    )
    far = lax.ppermute(far, axes, across)
    sums = lax.all_to_all(
        sums.reshape(MEMBERS, SLOTS, WIDE), "member", split_axis=0, concat_axis=0, tiled=True
    ).reshape(MEMBERS * SLOTS, WIDE)
    smooth, pick = call(
        unpack_smooth_kernel,
        [shaped((COLS, ROWS)), shaped((ROWS, MEMBERS * SLOTS))],
        (recv,),
        flops=10**9,
        name="unpack_smooth",
    )
    (coarse,) = call(
        unpack_coarse_kernel, [shaped((ROWS, 252), F32)], (me, pick, sums, far), name="unpack_coarse"
    )
    return smooth.reshape(3, MODES, TILE, ROWS).transpose(3, 0, 1, 2), coarse


def solution(mesh):
    in_specs = (
        P(("group", "member"), None, None, None),
        P(("group", "member"), None, None),
        P(("group", "member")),
    )
    out_specs = (P(("group", "member"), None, None, None), P(("group", "member"), None))
    return jax.shard_map(
        per_device, mesh=mesh, in_specs=in_specs, out_specs=out_specs, check_vma=False
    )
```

```python
import jax
import jax.numpy as jnp
from jax import lax
from jax.experimental import pallas as pl
from jax.experimental.pallas import tpu as pltpu
from jax.sharding import PartitionSpec as P

ROWS = 192
WIDE = 256
TILE = 64
MODES = 6
MEMBERS = 64
SLOTS = 8
COLS = 3 * MODES * TILE
F32 = jnp.float32
BF16 = jnp.bfloat16
NT = (((1,), (1,)), ((), ()))
TN = (((0,), (0,)), ((), ()))
MIB = 1024 * 1024
PACKED = 56


def iota(shape, axis):
    return lax.broadcasted_iota(jnp.int32, shape, axis)


def ones_where(mask):
    return jnp.where(mask, 1.0, 0.0).astype(BF16)


def dot(a, b):
    return jnp.dot(a, b, preferred_element_type=F32)


def parts_of(x):
    high = x.astype(BF16)
    rest = x - high.astype(F32)
    mid = rest.astype(BF16)
    low = (rest - mid.astype(F32)).astype(BF16)
    return high, mid, low


def exact_dot(pick, x, dims, pick_first):
    total = None
    for part in parts_of(x):
        ab = (pick, part) if pick_first else (part, pick)
        prod = lax.dot_general(*ab, dims, preferred_element_type=F32)
        total = prod if total is None else total + prod
    return total


def rank_arrays(owner_row):
    owner_row = owner_row.astype(F32)
    owner_row = jnp.concatenate([owner_row, owner_row[:, 128:]], 1)
    wide = jnp.broadcast_to(owner_row, (WIDE, WIDE))
    tall = wide.T[:ROWS]
    wide = wide[:ROWS]
    lane = iota((ROWS, WIDE), 1)
    row_l = jnp.where(lane < ROWS, lane, lane - TILE)
    row_s = iota((ROWS, WIDE), 0)
    one = jnp.where(wide == tall, 1.0, 0.0)
    less, more = row_s < row_l, row_s > row_l
    rank_l = jnp.sum(jnp.where(less, one, 0.0), 0, keepdims=True)
    after_l = jnp.sum(jnp.where(more, one, 0.0), 0, keepdims=True)
    once = jnp.where(lane < ROWS, one, 0.0)
    rank_s = jnp.sum(jnp.where(more, once, 0.0), 1, keepdims=True)
    after_s = jnp.sum(jnp.where(less, once, 0.0), 1, keepdims=True)
    return (wide[:1], rank_l, after_l), (tall[:, :1], rank_s, after_s)


class Order:
    def __init__(self, wide_ref, tall_ref):
        self.owner_l, self.rank_l, self.after_l = (wide_ref[n : n + 1, :] for n in range(3))
        self.owner_s, self.rank_s, self.after_s = (tall_ref[:, n : n + 1] for n in range(3))


def rim_picks(r, me):
    lane = iota((ROWS, 128), 1)
    first, last = r.rank_s == 0.0, r.after_s == 0.0
    even = me % 2 == 0
    picks = []
    for half in (0, 1):
        slot = lane - TILE * half
        inside = (slot >= 0) & (slot < TILE)
        to_left = jnp.where(inside, slot + jnp.where(me == 0, 1, 0), -1).astype(F32)
        to_right = jnp.where(inside, slot - jnp.where(me == MEMBERS - 1, 1, 0), -1).astype(F32)
        left = jnp.where((r.owner_s == to_left) & first, 1.0, 0.0)
        right = jnp.where((r.owner_s == to_right) & last, 1.0, 0.0)
        near = jnp.where(even, right, left).astype(BF16)
        far = jnp.where(even, left, right).astype(BF16)
        picks.append((near, far))
    return picks


def far_pick(r, me, width):
    top = iota((8, width), 0) == 0
    owner, rank, after = r.owner_l[:, :width], r.rank_l[:, :width], r.after_l[:, :width]
    head = top & (me == 0) & (owner == 0.0) & (rank == 0.0)
    tail = top & (me == MEMBERS - 1) & (owner == MEMBERS - 1.0) & (after == 0.0)
    return ones_where(head), ones_where(tail)


def rims_of(rows, r, me):
    half = rows.shape[0] // 2
    top, bottom = rim_picks(r, me)
    rims = [(dot(rows[:half], a) + dot(rows[half:], b)).astype(BF16) for a, b in zip(top, bottom)]
    head, tail = far_pick(r, me, ROWS)
    far = lax.dot_general(head + tail, rows, NT, preferred_element_type=F32).astype(BF16)
    return [far] + rims[::-1]


def local_rows(rows, r):
    lane = iota((ROWS, WIDE), 1)
    row_l = jnp.where(lane < ROWS, lane, lane - TILE)
    same = r.owner_l == r.owner_s
    before = ones_where(same & (r.rank_s + 1.0 == r.rank_l))
    after = ones_where(same & (r.rank_s == r.rank_l + 1.0))
    here = ones_where(iota((ROWS, WIDE), 0) == row_l)
    return [dot(rows, pick) for pick in (before, here, after)]


def rim_rows(near, away, far, r, me):
    bucket = iota((128, WIDE), 0)
    even = me % 2 == 0
    result = []
    for rim, edge, end in zip(
        (jnp.where(even, away, near), jnp.where(even, near, away)), (r.rank_l, r.after_l), far_pick(r, me, WIDE)
    ):
        ends = []
        for side in (0, 1):
            want = bucket - TILE * side
            want = jnp.where((want >= 0) & (want < TILE), want, -1).astype(F32)
            ends.append(dot(rim, ones_where((want == r.owner_l) & (edge == 0.0))))
        result.append(jnp.concatenate(ends, 0) + lax.dot_general(far, end, TN, preferred_element_type=F32))
    return result


def set_wide(ref, k, value):
    for tile in (0, 1):
        part = value[:, 128 * tile : 128 * (tile + 1)]
        ref[tile, k] = part.reshape(-1, TILE, 128)


def chunk_copies(a_hbm, a_ref, sems, planes, n):
    rows = pl.ds(16 * n, 16)
    return [
        pltpu.make_async_copy(a_hbm.at[k, rows], a_ref.at[at, rows], sems.at[at, n])
        for at, k in enumerate(planes)
    ]


def start_copies(a_hbm, a_ref, sems, planes):
    for n in range(TILE // 16):
        for copy in chunk_copies(a_hbm, a_ref, sems, planes, n):
            copy.start()


def next_groups(a_hbm, a_ref, sems, planes, ib, group_ref):
    for copy in chunk_copies(a_hbm, a_ref, sems, planes, ib):
        copy.wait()
    for k in range(len(planes)):
        for i in range(8):
            low, high = (a_ref[k, 16 * ib + i + n].astype(F32) for n in (0, 8))
            group_ref[0, k, i] = low[:, :128]
            group_ref[1, k, i] = high[:, :128]
            group_ref[2, k, i] = jnp.concatenate([low[:, 128:], high[:, 128:]], 1)


def folded(terms):
    sub = iota((8, 128), 0)
    for shift in (1, 2, 4):
        keep = (sub & shift) == 0
        terms = [
            jnp.where(keep, x, y) + pltpu.roll(jnp.where(keep, y, x), shift, 0)
            for x, y in zip(terms[::2], terms[1::2])
        ]
    return terms[0]


def contracted(group_ref, wide_ref, g, tile, pairs, columns):
    totals = [[None] * 8 for _ in columns]
    for jb in range(TILE // 8):
        j = pl.ds(8 * jb, 8)
        for k, base in pairs:
            a = [group_ref[g, k, i, j, :] for i in range(8)]
            for n, column in enumerate(columns):
                x = wide_ref[tile, k, base + column, j, :]
                for i in range(8):
                    term = a[i] * x
                    totals[n][i] = term if totals[n][i] is None else totals[n][i] + term
    return [folded(t) for t in totals]


def ungrouped(out_ref, index):
    low, high, both = out_ref[0, index], out_ref[1, index], out_ref[2, index]
    top = jnp.concatenate([low, both[:, :TILE]], 1)
    bottom = jnp.concatenate([high, both[:, TILE:]], 1)
    return jnp.concatenate([top, bottom], 0)


def first_kernel(me_ref, owner_ref, p_ref, wide_ref, tall_ref, p_out, far_out, away_out, near_out):
    rows, columns = rank_arrays(owner_ref[...])
    p_out[...] = p_ref[...]
    wide_ref[...] = jnp.zeros_like(wide_ref)
    for n in range(3):
        wide_ref[n : n + 1, :] = rows[n]
    lane = iota((ROWS, 128), 1)
    tall_ref[...] = jnp.where(lane == 0, columns[0], jnp.where(lane == 1, columns[1], columns[2]))
    r = Order(wide_ref, tall_ref)
    for ref, rim in zip((far_out, away_out, near_out), rims_of(p_ref[...], r, me_ref[0])):
        ref[...] = rim


def halves(ib):
    return pl.ds(pl.multiple_of(16 * ib, 8), 8), pl.ds(pl.multiple_of(16 * ib + 8, 8), 8)


def middle_kernel(
    order_l_ref, order_s_ref, a_hbm, p_ref, mid_ref, scale_ref, local_ref,
    a_ref, sems, group_ref, wide_ref, out_ref,
):
    ib = pl.program_id(0)

    @pl.when(ib == 0)
    def _():
        start_copies(a_hbm, a_ref, sems, (1,))
        before, here, after = local_rows(p_ref[...], Order(order_l_ref, order_s_ref))
        set_wide(wide_ref, 0, here)
        set_wide(local_ref, 0, before)
        set_wide(local_ref, 1, after)

    next_groups(a_hbm, a_ref, sems, (1,), ib, group_ref)
    sub, lane = iota((8, 128), 0), iota((8, 128), 1)
    lower, upper = halves(ib)

    def one_group(g, carry):
        tile = jnp.where(g == 2, 1, 0)
        second = (g == 1) | ((g == 2) & (lane >= TILE))
        diag = jnp.zeros((8, 128), F32)
        for i in range(8):
            entry = jnp.where(second, group_ref[g, 0, i, upper, :], group_ref[g, 0, i, lower, :])
            diag = jnp.where(sub == i, entry, diag)
        scale = 0.6 * (1.0 / diag)
        scale_ref[ib, g] = scale
        for half in (0, 1):
            columns = [3 * half + c for c in range(3)]
            sums = contracted(group_ref, wide_ref, g, tile, [(0, 0)], columns)
            for c, total in zip(columns, sums):
                own = jnp.where(second, wide_ref[tile, 0, c, upper, :], wide_ref[tile, 0, c, lower, :])
                out_ref[g, c] = own - scale * total
        return carry

    lax.fori_loop(0, 3, one_group, 0)
    rows = pl.ds(pl.multiple_of(16 * ib, 16), 16)
    for index in range(6):
        mid_ref[index, rows, :] = ungrouped(out_ref, index).astype(BF16)


def smooth_kernel(
    me_ref, order_l_ref, order_s_ref, a_hbm, mid_ref, scale_ref, local_ref, far_ref, away_ref, near_ref,
    s_ref, far_out, away_out, near_out, a_ref, sems, group_ref, wide_ref, out_ref,
):
    ib = pl.program_id(0)
    me = me_ref[0]

    @pl.when(ib == 0)
    def _():
        start_copies(a_hbm, a_ref, sems, (0, 2))
        r = Order(order_l_ref, order_s_ref)
        for k, value in enumerate(rim_rows(near_ref[...], away_ref[...], far_ref[...], r, me)):
            set_wide(wide_ref, k, value)
        wide_ref[...] += local_ref[...]
        s_ref[6:12] = mid_ref[...]

    next_groups(a_hbm, a_ref, sems, (0, 2), ib, group_ref)

    def one_group(g, carry):
        tile = jnp.where(g == 2, 1, 0)
        scale = 0.0 - scale_ref[ib, g]
        for k in range(2):
            for half in (0, 1):
                columns = [3 * half + c for c in range(3)]
                sums = contracted(group_ref, wide_ref, g, tile, [(k, 0)], columns)
                for c, total in zip(columns, sums):
                    out_ref[g, 6 * k + c] = scale * total
        return carry

    lax.fori_loop(0, 3, one_group, 0)
    rows = pl.ds(pl.multiple_of(16 * ib, 16), 16)
    for index in range(12):
        s_ref[index if index < 6 else index + 6, rows, :] = ungrouped(out_ref, index).astype(BF16)

    @pl.when(ib == pl.num_programs(0) - 1)
    def _():
        r = Order(order_l_ref, order_s_ref)
        flat = s_ref[...].reshape(COLS, ROWS)
        for ref, rim in zip((far_out, away_out, near_out), rims_of(flat, r, me)):
            ref[...] = rim


def slot_grid(width):
    spot = iota((MEMBERS * SLOTS, width), 0)
    return (spot // SLOTS).astype(F32), (spot % SLOTS).astype(F32)


def pack_kernel(order_l_ref, s_ref, out_ref):
    member, slot = slot_grid(ROWS)
    owner, rank = order_l_ref[0:1, :ROWS], order_l_ref[1:2, :ROWS]
    mine = owner == member
    pick = ones_where(mine & (rank == slot))
    count = jnp.sum(jnp.where(mine, 1.0, 0.0), 1, keepdims=True)
    for block in range(COLS // 128):
        value = lax.dot_general(
            pick, s_ref[128 * block : 128 * (block + 1), :], NT, preferred_element_type=F32
        ).reshape(MEMBERS, SLOTS, 128)
        out_ref[:, 6 * block : 6 * block + 6, :] = value[:, :6, :].astype(BF16)
    counts = jnp.broadcast_to(count, (MEMBERS * SLOTS, 128)).reshape(MEMBERS, SLOTS, 128)
    out_ref[:, 54:56, :] = counts[:, :2, :].astype(BF16)


OFFSETS = [[(k, 6 * (e - k)) for k in range(3) if 0 <= e - k <= 2] for e in range(5)]


def product_kernel(
    me_ref, order_l_ref, order_s_ref, a_hbm, s_ref, far_ref, away_ref, near_ref,
    out_ref, far_out, a_ref, sems, group_ref, wide_ref, ap_ref, own_ref, term_ref,
):
    ib = pl.program_id(0)
    me = me_ref[0]

    @pl.when(ib == 0)
    def _():
        start_copies(a_hbm, a_ref, sems, (0, 1, 2))
        r = Order(order_l_ref, order_s_ref)
        before, here, after = local_rows(s_ref[...], r)
        left, right = rim_rows(near_ref[...], away_ref[...], far_ref[...], r, me)
        for k, value in enumerate((before + left, here, after + right)):
            set_wide(wide_ref, k, value)
        term_ref[...] = jnp.zeros_like(term_ref)

    next_groups(a_hbm, a_ref, sems, (0, 1, 2), ib, group_ref)
    lane = iota((8, 128), 1)

    def one_group(step, carry):
        g, half = step // 2, step % 2
        tile = jnp.where(g == 2, 1, 0)
        for e in range(5):
            columns = [3 * half + c for c in range(3)]
            sums = contracted(group_ref, wide_ref, g, tile, OFFSETS[e], columns)
            for c, total in zip(columns, sums):
                ap_ref[g, ib, 6 * e + c] = total.astype(BF16).astype(F32)
        second = (g == 1) | ((g == 2) & (lane >= TILE))
        lower, upper = pl.ds(pl.multiple_of(16 * ib, 8), 8), pl.ds(pl.multiple_of(16 * ib + 8, 8), 8)
        for c in range(9):
            column = 9 * half + c
            own_ref[g, ib, column] = jnp.where(
                second, wide_ref[tile, 1, column, upper, :], wide_ref[tile, 1, column, lower, :]
            )
        return carry

    lax.fori_loop(0, 6, one_group, 0)

    @pl.when(ib == pl.num_programs(0) - 1)
    def _():
        def one_pair(step, carry):
            k, e = step // 5, step % 5
            for c in range(6):
                near, far = [None] * 6, [None] * 6
                for block in range(TILE // 16):
                    for g in range(3):
                        x = own_ref[g, block, 6 * k + c]
                        for d in range(6):
                            term = x * ap_ref[g, block, 6 * e + d]
                            sums = far if g == 2 else near
                            sums[d] = term if sums[d] is None else sums[d] + term
                for d in range(6):
                    row = slice(6 * c + d, 6 * c + d + 1)
                    tail = jnp.sum(far[d], 0, keepdims=True)
                    term_ref[step, row, 0:128] = jnp.sum(near[d], 0, keepdims=True)
                    term_ref[step, row, 128:ROWS] = tail[:, :TILE] + tail[:, TILE:]
            return carry

        lax.fori_loop(0, 15, one_pair, 0)
        r = Order(order_l_ref, order_s_ref)
        owner, rank, after = (x[:, :ROWS] for x in (r.owner_l, r.rank_l, r.after_l))
        member, slot = slot_grid(ROWS)
        mine, row_slot = owner == member, slot < 6.0
        here = ones_where(mine & (rank == slot))
        back_to = member + jnp.where(me == 0, 1.0, 0.0)
        on_to = member - jnp.where(me == MEMBERS - 1, 1.0, 0.0)
        back = (mine & row_slot & (rank == slot + 1.0)) | ((slot == 6.0) & (owner == back_to) & (rank == 0.0))
        on = (mine & row_slot & (rank == slot - 1.0) & (after > 0.0)) | (
            (slot == 7.0) & (owner == on_to) & (after == 0.0)
        )
        picks = [ones_where(back), here, ones_where(on)]
        terms = []
        for k in range(3):
            pieces = [term_ref[5 * k + e][:36, :ROWS] for e in range(5)]
            pieces.append(jnp.zeros((4 + 36 * k, ROWS), F32))
            if k < 2:
                pieces.insert(0, jnp.zeros((72 - 36 * k, ROWS), F32))
            terms.append(jnp.concatenate(pieces, 0))
        total = None
        for k in range(3):
            prod = exact_dot(picks[k], terms[k], NT, True)
            total = prod if total is None else total + prod
        out_ref[...] = total
        head, tail = far_pick(r, me, ROWS)
        far_out[...] = exact_dot(head, terms[0], NT, True) + exact_dot(tail, terms[2], NT, True)


def unpack_smooth_kernel(recv_ref, out_ref, pick_out):
    size = MEMBERS * SLOTS
    count = jnp.broadcast_to(recv_ref[:, 54:55, :].astype(F32), (MEMBERS, SLOTS, 128)).reshape(size, 128)
    source, other = iota((size, size), 0) // SLOTS, iota((size, size), 1) // SLOTS
    first_slot = iota((size, size), 1) % SLOTS == 0
    earlier = ones_where((other < source) & first_slot)
    start = dot(earlier, count.astype(BF16))[:, :1]
    count = count[:, :1]
    slot = (iota((size, 1), 0) % SLOTS).astype(F32)
    place = jnp.where(slot < count, start + slot, -1.0)
    column = iota((size, ROWS), 1).astype(F32)
    pick = ones_where(place == column)
    for block in range(COLS // 128):
        rows = recv_ref[:, 6 * block : 6 * block + 6, :].astype(F32)
        rows = jnp.concatenate([rows, jnp.zeros((MEMBERS, 2, 128), F32)], 1).reshape(size, 128)
        value = lax.dot_general(rows.astype(BF16), pick, TN, preferred_element_type=F32)
        out_ref[128 * block : 128 * (block + 1), :] = value.astype(BF16)
    place = jnp.where(slot == 6.0, jnp.where(start == 0.0, ROWS - 1.0, start - 1.0), place)
    stop = start + count
    place = jnp.where(slot == 7.0, jnp.where(stop == float(ROWS), 0.0, stop), place)
    column = iota((size, WIDE), 1).astype(F32)
    pick_out[...] = jnp.where(place == column, 1.0, 0.0).T[:ROWS].astype(BF16)


def unpack_coarse_kernel(me_ref, pick_ref, sums_ref, far_ref, out_ref):
    me = me_ref[0]
    total = exact_dot(pick_ref[...], sums_ref[...], (((1,), (0,)), ((), ())), True)
    row = iota((ROWS, WIDE), 0)
    edge = jnp.where(me == 0, 0, ROWS - 1)
    far = jnp.broadcast_to(far_ref[0:1, :], (ROWS, WIDE))
    total = total + jnp.where(row == edge, far, 0.0)
    out_ref[...] = total[:, :252]


def call(kernel, outs, args, grid=None, in_specs=None, scratch=(), flops=0, mib=16, name=None):
    whole = lambda shape: pl.BlockSpec(shape, lambda *_: (0,) * len(shape))
    specs = []
    for n, arg in enumerate(args):
        spec = None if in_specs is None else in_specs.get(n)
        if spec is None:
            spec = pl.BlockSpec(memory_space=pltpu.SMEM) if arg.shape == (1,) else whole(arg.shape)
        specs.append(spec)
    moved = sum(a.size * a.dtype.itemsize for a in args) + sum(o.size * o.dtype.itemsize for o in outs)
    return pl.pallas_call(
        kernel,
        grid=(1,) if grid is None else grid,
        in_specs=specs,
        out_specs=[whole(o.shape) for o in outs],
        out_shape=outs,
        scratch_shapes=list(scratch),
        compiler_params=pltpu.CompilerParams(vmem_limit_bytes=mib * MIB),
        cost_estimate=pl.CostEstimate(flops=flops, bytes_accessed=moved, transcendentals=0),
        name=name,
    )(*args)


def shaped(shape, dtype=BF16):
    return jax.ShapeDtypeStruct(shape, dtype)


def swaps(groups):
    ring, axes = MEMBERS, range(groups)
    both = lambda pairs: [q for a, b in pairs for q in ((a, b), (b, a))]
    across = both([(g * ring - 1, g * ring) for g in range(1, groups)])
    away = both([(g * ring + i, g * ring + (i + 1) % ring) for g in axes for i in range(1, ring, 2)])
    near = both([(g * ring + i, g * ring + i + 1) for g in axes for i in range(0, ring, 2)])
    return across, away, near


def per_device(a_band, p_tent, new_owner):
    axes = ("group", "member")
    across, away_pairs, near_pairs = swaps(lax.axis_size("group"))
    me = lax.axis_index("member").astype(jnp.int32).reshape(1)
    a = a_band.transpose(1, 2, 3, 0)
    p = p_tent.transpose(1, 2, 0).reshape(MODES * TILE, ROWS)
    a_spec = pl.BlockSpec(memory_space=pltpu.HBM)
    grid = (TILE // 16,)

    def a_scratch(planes):
        return [
            pltpu.VMEM((planes, TILE, TILE, ROWS), BF16),
            pltpu.SemaphoreType.DMA((planes, TILE // 16)),
            pltpu.VMEM((3, planes, 8, TILE, 128), F32),
        ]

    def exchanged(far, away, near):
        far = lax.ppermute(far, axes, across)
        away = lax.ppermute(away, axes, away_pairs)
        return far, away, lax.ppermute(near, axes, near_pairs)

    def rims(length):
        return [shaped((8, length)), shaped((length // 2, 128)), shaped((length // 2, 128))]

    order_l, order_s, p, *sent = call(
        first_kernel,
        [shaped((8, WIDE), F32), shaped((ROWS, 128), F32), shaped(p.shape)] + rims(MODES * TILE),
        (me, new_owner.reshape(1, ROWS), p),
        name="rims",
    )
    got = exchanged(*sent)
    local = shaped((2, 2, MODES, TILE, 128), F32)
    parts = call(
        middle_kernel,
        [shaped((MODES, TILE, ROWS)), shaped((TILE // 16, 3, 8, 128), F32), local],
        (order_l, order_s, a, p),
        grid=grid,
        in_specs={2: a_spec},
        scratch=[
            *a_scratch(1),
            pltpu.VMEM((2, 1, MODES, TILE, 128), F32),
            pltpu.VMEM((3, MODES, 8, 128), F32),
        ],
        flops=10**9,
        mib=50,
        name="middle",
    )
    s, *sent = call(
        smooth_kernel,
        [shaped((18, TILE, ROWS))] + rims(COLS),
        (me, order_l, order_s, a, *parts, *got),
        grid=grid,
        in_specs={3: a_spec},
        scratch=[*a_scratch(2), pltpu.VMEM(local.shape, F32), pltpu.VMEM((3, 12, 8, 128), F32)],
        flops=10**9,
        mib=50,
        name="smooth",
    )
    got = exchanged(*sent)
    s = s.reshape(COLS, ROWS)
    (packed,) = call(pack_kernel, [shaped((MEMBERS, PACKED, 128))], (order_l, s), name="pack")
    packed, *got = lax.optimization_barrier((packed, *got))
    recv = lax.all_to_all(packed, "member", split_axis=0, concat_axis=0, tiled=True)

    sums, far = call(
        product_kernel,
        [shaped((MEMBERS * SLOTS, WIDE), F32), shaped((8, WIDE), F32)],
        (me, order_l, order_s, a, s, *got),
        grid=grid,
        in_specs={3: a_spec},
        scratch=[
            *a_scratch(3),
            pltpu.VMEM((2, 3, 18, TILE, 128), F32),
            pltpu.VMEM((3, TILE // 16, 30, 8, 128), F32),
            pltpu.VMEM((3, TILE // 16, 18, 8, 128), F32),
            pltpu.VMEM((15, 40, WIDE), F32),
        ],
        flops=10**10,
        mib=50,
        name="product",
    )
    far = lax.ppermute(far, axes, across)
    sums = lax.all_to_all(
        sums.reshape(MEMBERS, SLOTS, WIDE), "member", split_axis=0, concat_axis=0, tiled=True
    ).reshape(MEMBERS * SLOTS, WIDE)
    smooth, pick = call(
        unpack_smooth_kernel,
        [shaped((COLS, ROWS)), shaped((ROWS, MEMBERS * SLOTS))],
        (recv,),
        flops=10**9,
        name="unpack_smooth",
    )
    (coarse,) = call(
        unpack_coarse_kernel, [shaped((ROWS, 252), F32)], (me, pick, sums, far), name="unpack_coarse"
    )
    return smooth.reshape(3, MODES, TILE, ROWS).transpose(3, 0, 1, 2), coarse


def solution(mesh):
    in_specs = (
        P(("group", "member"), None, None, None),
        P(("group", "member"), None, None),
        P(("group", "member")),
    )
    out_specs = (P(("group", "member"), None, None, None), P(("group", "member"), None))
    return jax.shard_map(
        per_device, mesh=mesh, in_specs=in_specs, out_specs=out_specs, check_vma=False
    )
```

```python
import jax
import jax.numpy as jnp
from jax import lax
from jax.experimental import pallas as pl
from jax.experimental.pallas import tpu as pltpu
from jax.sharding import PartitionSpec as P

ROWS = 192
WIDE = 256
TILE = 64
MODES = 6
MEMBERS = 64
SLOTS = 8
COLS = 3 * MODES * TILE
F32 = jnp.float32
BF16 = jnp.bfloat16
NT = (((1,), (1,)), ((), ()))
TN = (((0,), (0,)), ((), ()))
MIB = 1024 * 1024
PACKED = 56


def iota(shape, axis):
    return lax.broadcasted_iota(jnp.int32, shape, axis)


def ones_where(mask):
    return jnp.where(mask, 1.0, 0.0).astype(BF16)


def dot(a, b):
    return jnp.dot(a, b, preferred_element_type=F32)


def parts_of(x):
    high = x.astype(BF16)
    rest = x - high.astype(F32)
    mid = rest.astype(BF16)
    low = (rest - mid.astype(F32)).astype(BF16)
    return high, mid, low


def exact_dot(pick, x, dims, pick_first):
    total = None
    for part in parts_of(x):
        ab = (pick, part) if pick_first else (part, pick)
        prod = lax.dot_general(*ab, dims, preferred_element_type=F32)
        total = prod if total is None else total + prod
    return total


def rank_arrays(owner_row):
    owner_row = owner_row.astype(F32)
    owner_row = jnp.concatenate([owner_row, owner_row[:, 128:]], 1)
    wide = jnp.broadcast_to(owner_row, (WIDE, WIDE))
    tall = wide.T[:ROWS]
    wide = wide[:ROWS]
    lane = iota((ROWS, WIDE), 1)
    row_l = jnp.where(lane < ROWS, lane, lane - TILE)
    row_s = iota((ROWS, WIDE), 0)
    one = jnp.where(wide == tall, 1.0, 0.0)
    less, more = row_s < row_l, row_s > row_l
    rank_l = jnp.sum(jnp.where(less, one, 0.0), 0, keepdims=True)
    after_l = jnp.sum(jnp.where(more, one, 0.0), 0, keepdims=True)
    once = jnp.where(lane < ROWS, one, 0.0)
    rank_s = jnp.sum(jnp.where(more, once, 0.0), 1, keepdims=True)
    after_s = jnp.sum(jnp.where(less, once, 0.0), 1, keepdims=True)
    return (wide[:1], rank_l, after_l), (tall[:, :1], rank_s, after_s)


class Order:
    def __init__(self, wide_ref, tall_ref):
        self.owner_l, self.rank_l, self.after_l = (wide_ref[n : n + 1, :] for n in range(3))
        self.owner_s, self.rank_s, self.after_s = (tall_ref[:, n : n + 1] for n in range(3))


def rim_picks(r, me):
    lane = iota((ROWS, 128), 1)
    first, last = r.rank_s == 0.0, r.after_s == 0.0
    even = me % 2 == 0
    picks = []
    for half in (0, 1):
        slot = lane - TILE * half
        inside = (slot >= 0) & (slot < TILE)
        to_left = jnp.where(inside, slot + jnp.where(me == 0, 1, 0), -1).astype(F32)
        to_right = jnp.where(inside, slot - jnp.where(me == MEMBERS - 1, 1, 0), -1).astype(F32)
        left = jnp.where((r.owner_s == to_left) & first, 1.0, 0.0)
        right = jnp.where((r.owner_s == to_right) & last, 1.0, 0.0)
        near = jnp.where(even, right, left).astype(BF16)
        far = jnp.where(even, left, right).astype(BF16)
        picks.append((near, far))
    return picks


def far_pick(r, me, width):
    top = iota((8, width), 0) == 0
    owner, rank, after = r.owner_l[:, :width], r.rank_l[:, :width], r.after_l[:, :width]
    head = top & (me == 0) & (owner == 0.0) & (rank == 0.0)
    tail = top & (me == MEMBERS - 1) & (owner == MEMBERS - 1.0) & (after == 0.0)
    return ones_where(head), ones_where(tail)


def rims_of(rows, r, me):
    half = rows.shape[0] // 2
    top, bottom = rim_picks(r, me)
    rims = [(dot(rows[:half], a) + dot(rows[half:], b)).astype(BF16) for a, b in zip(top, bottom)]
    head, tail = far_pick(r, me, ROWS)
    far = lax.dot_general(head + tail, rows, NT, preferred_element_type=F32).astype(BF16)
    return [far] + rims[::-1]


def local_rows(rows, r):
    lane = iota((ROWS, WIDE), 1)
    row_l = jnp.where(lane < ROWS, lane, lane - TILE)
    same = r.owner_l == r.owner_s
    before = ones_where(same & (r.rank_s + 1.0 == r.rank_l))
    after = ones_where(same & (r.rank_s == r.rank_l + 1.0))
    here = ones_where(iota((ROWS, WIDE), 0) == row_l)
    return [dot(rows, pick) for pick in (before, here, after)]


def rim_rows(near, away, far, r, me):
    bucket = iota((128, WIDE), 0)
    even = me % 2 == 0
    result = []
    for rim, edge, end in zip(
        (jnp.where(even, away, near), jnp.where(even, near, away)), (r.rank_l, r.after_l), far_pick(r, me, WIDE)
    ):
        ends = []
        for side in (0, 1):
            want = bucket - TILE * side
            want = jnp.where((want >= 0) & (want < TILE), want, -1).astype(F32)
            ends.append(dot(rim, ones_where((want == r.owner_l) & (edge == 0.0))))
        result.append(jnp.concatenate(ends, 0) + lax.dot_general(far, end, TN, preferred_element_type=F32))
    return result


def set_wide(ref, k, value):
    for tile in (0, 1):
        part = value[:, 128 * tile : 128 * (tile + 1)]
        ref[tile, k] = part.reshape(-1, TILE, 128)


def chunk_copies(a_hbm, a_ref, sems, planes, n):
    rows = pl.ds(16 * n, 16)
    return [
        pltpu.make_async_copy(a_hbm.at[k, rows], a_ref.at[at, rows], sems.at[at, n])
        for at, k in enumerate(planes)
    ]


def start_copies(a_hbm, a_ref, sems, planes):
    for n in range(TILE // 16):
        for copy in chunk_copies(a_hbm, a_ref, sems, planes, n):
            copy.start()


def next_groups(a_hbm, a_ref, sems, planes, ib, group_ref):
    for copy in chunk_copies(a_hbm, a_ref, sems, planes, ib):
        copy.wait()
    for k in range(len(planes)):
        for i in range(8):
            low, high = (a_ref[k, 16 * ib + i + n].astype(F32) for n in (0, 8))
            group_ref[0, k, i] = low[:, :128]
            group_ref[1, k, i] = high[:, :128]
            group_ref[2, k, i] = jnp.concatenate([low[:, 128:], high[:, 128:]], 1)


def folded(terms):
    sub = iota((8, 128), 0)
    for shift in (1, 2, 4):
        keep = (sub & shift) == 0
        terms = [
            jnp.where(keep, x, y) + pltpu.roll(jnp.where(keep, y, x), shift, 0)
            for x, y in zip(terms[::2], terms[1::2])
        ]
    return terms[0]


def contracted(group_ref, wide_ref, g, tile, pairs, columns):
    totals = [[None] * 8 for _ in columns]
    for jb in range(TILE // 8):
        j = pl.ds(8 * jb, 8)
        for k, base in pairs:
            a = [group_ref[g, k, i, j, :] for i in range(8)]
            for n, column in enumerate(columns):
                x = wide_ref[tile, k, base + column, j, :]
                for i in range(8):
                    term = a[i] * x
                    totals[n][i] = term if totals[n][i] is None else totals[n][i] + term
    return [folded(t) for t in totals]


def ungrouped(out_ref, index):
    low, high, both = out_ref[0, index], out_ref[1, index], out_ref[2, index]
    top = jnp.concatenate([low, both[:, :TILE]], 1)
    bottom = jnp.concatenate([high, both[:, TILE:]], 1)
    return jnp.concatenate([top, bottom], 0)


def first_kernel(me_ref, owner_ref, p_ref, wide_ref, tall_ref, p_out, far_out, away_out, near_out):
    rows, columns = rank_arrays(owner_ref[...])
    p_out[...] = p_ref[...]
    wide_ref[...] = jnp.zeros_like(wide_ref)
    for n in range(3):
        wide_ref[n : n + 1, :] = rows[n]
    lane = iota((ROWS, 128), 1)
    tall_ref[...] = jnp.where(lane == 0, columns[0], jnp.where(lane == 1, columns[1], columns[2]))
    r = Order(wide_ref, tall_ref)
    for ref, rim in zip((far_out, away_out, near_out), rims_of(p_ref[...], r, me_ref[0])):
        ref[...] = rim


def halves(ib):
    return pl.ds(pl.multiple_of(16 * ib, 8), 8), pl.ds(pl.multiple_of(16 * ib + 8, 8), 8)


def middle_kernel(
    order_l_ref, order_s_ref, a_hbm, p_ref, mid_ref, scale_ref, local_ref,
    a_ref, sems, group_ref, wide_ref, out_ref,
):
    ib = pl.program_id(0)

    @pl.when(ib == 0)
    def _():
        start_copies(a_hbm, a_ref, sems, (1,))
        before, here, after = local_rows(p_ref[...], Order(order_l_ref, order_s_ref))
        set_wide(wide_ref, 0, here)
        set_wide(local_ref, 0, before)
        set_wide(local_ref, 1, after)

    next_groups(a_hbm, a_ref, sems, (1,), ib, group_ref)
    sub, lane = iota((8, 128), 0), iota((8, 128), 1)
    lower, upper = halves(ib)

    def one_group(g, carry):
        tile = jnp.where(g == 2, 1, 0)
        second = (g == 1) | ((g == 2) & (lane >= TILE))
        diag = jnp.zeros((8, 128), F32)
        for i in range(8):
            entry = jnp.where(second, group_ref[g, 0, i, upper, :], group_ref[g, 0, i, lower, :])
            diag = jnp.where(sub == i, entry, diag)
        scale = 0.6 * (1.0 / diag)
        scale_ref[ib, g] = scale
        for half in (0, 1):
            columns = [3 * half + c for c in range(3)]
            sums = contracted(group_ref, wide_ref, g, tile, [(0, 0)], columns)
            for c, total in zip(columns, sums):
                own = jnp.where(second, wide_ref[tile, 0, c, upper, :], wide_ref[tile, 0, c, lower, :])
                out_ref[g, c] = own - scale * total
        return carry

    lax.fori_loop(0, 3, one_group, 0)
    rows = pl.ds(pl.multiple_of(16 * ib, 16), 16)
    for index in range(6):
        mid_ref[index, rows, :] = ungrouped(out_ref, index).astype(BF16)


def smooth_kernel(
    me_ref, order_l_ref, order_s_ref, a_hbm, mid_ref, scale_ref, local_ref, far_ref, away_ref, near_ref,
    s_ref, far_out, away_out, near_out, a_ref, sems, group_ref, wide_ref, out_ref,
):
    ib = pl.program_id(0)
    me = me_ref[0]

    @pl.when(ib == 0)
    def _():
        start_copies(a_hbm, a_ref, sems, (0, 2))
        r = Order(order_l_ref, order_s_ref)
        for k, value in enumerate(rim_rows(near_ref[...], away_ref[...], far_ref[...], r, me)):
            set_wide(wide_ref, k, value)
        wide_ref[...] += local_ref[...]
        s_ref[6:12] = mid_ref[...]

    next_groups(a_hbm, a_ref, sems, (0, 2), ib, group_ref)

    def one_group(g, carry):
        tile = jnp.where(g == 2, 1, 0)
        scale = 0.0 - scale_ref[ib, g]
        for k in range(2):
            for half in (0, 1):
                columns = [3 * half + c for c in range(3)]
                sums = contracted(group_ref, wide_ref, g, tile, [(k, 0)], columns)
                for c, total in zip(columns, sums):
                    out_ref[g, 6 * k + c] = scale * total
        return carry

    lax.fori_loop(0, 3, one_group, 0)
    rows = pl.ds(pl.multiple_of(16 * ib, 16), 16)
    for index in range(12):
        s_ref[index if index < 6 else index + 6, rows, :] = ungrouped(out_ref, index).astype(BF16)

    @pl.when(ib == pl.num_programs(0) - 1)
    def _():
        r = Order(order_l_ref, order_s_ref)
        flat = s_ref[...].reshape(COLS, ROWS)
        for ref, rim in zip((far_out, away_out, near_out), rims_of(flat, r, me)):
            ref[...] = rim


def slot_grid(width):
    spot = iota((MEMBERS * SLOTS, width), 0)
    return (spot // SLOTS).astype(F32), (spot % SLOTS).astype(F32)


def pack_kernel(order_l_ref, s_ref, out_ref):
    member, slot = slot_grid(ROWS)
    owner, rank = order_l_ref[0:1, :ROWS], order_l_ref[1:2, :ROWS]
    mine = owner == member
    pick = ones_where(mine & (rank == slot))
    count = jnp.sum(jnp.where(mine, 1.0, 0.0), 1, keepdims=True)
    for block in range(COLS // 128):
        value = lax.dot_general(
            pick, s_ref[128 * block : 128 * (block + 1), :], NT, preferred_element_type=F32
        ).reshape(MEMBERS, SLOTS, 128)
        out_ref[:, 6 * block : 6 * block + 6, :] = value[:, :6, :].astype(BF16)
    counts = jnp.broadcast_to(count, (MEMBERS * SLOTS, 128)).reshape(MEMBERS, SLOTS, 128)
    out_ref[:, 54:56, :] = counts[:, :2, :].astype(BF16)


OFFSETS = [[(k, 6 * (e - k)) for k in range(3) if 0 <= e - k <= 2] for e in range(5)]


def product_kernel(
    me_ref, order_l_ref, order_s_ref, a_hbm, s_ref, far_ref, away_ref, near_ref,
    out_ref, far_out, a_ref, sems, group_ref, wide_ref, ap_ref, own_ref, term_ref,
):
    ib = pl.program_id(0)
    me = me_ref[0]

    @pl.when(ib == 0)
    def _():
        start_copies(a_hbm, a_ref, sems, (0, 1, 2))
        r = Order(order_l_ref, order_s_ref)
        before, here, after = local_rows(s_ref[...], r)
        left, right = rim_rows(near_ref[...], away_ref[...], far_ref[...], r, me)
        for k, value in enumerate((before + left, here, after + right)):
            set_wide(wide_ref, k, value)
        term_ref[...] = jnp.zeros_like(term_ref)

    next_groups(a_hbm, a_ref, sems, (0, 1, 2), ib, group_ref)
    lane = iota((8, 128), 1)

    def one_group(step, carry):
        g, half = step // 2, step % 2
        tile = jnp.where(g == 2, 1, 0)
        for e in range(5):
            columns = [3 * half + c for c in range(3)]
            sums = contracted(group_ref, wide_ref, g, tile, OFFSETS[e], columns)
            for c, total in zip(columns, sums):
                ap_ref[g, ib, 6 * e + c] = total.astype(BF16).astype(F32)
        second = (g == 1) | ((g == 2) & (lane >= TILE))
        lower, upper = pl.ds(pl.multiple_of(16 * ib, 8), 8), pl.ds(pl.multiple_of(16 * ib + 8, 8), 8)
        for c in range(9):
            column = 9 * half + c
            own_ref[g, ib, column] = jnp.where(
                second, wide_ref[tile, 1, column, upper, :], wide_ref[tile, 1, column, lower, :]
            )
        return carry

    lax.fori_loop(0, 6, one_group, 0)

    @pl.when(ib == pl.num_programs(0) - 1)
    def _():
        def one_pair(step, carry):
            k, e = step // 5, step % 5
            for c in range(6):
                near, far = [None] * 6, [None] * 6
                for block in range(TILE // 16):
                    for g in range(3):
                        x = own_ref[g, block, 6 * k + c]
                        for d in range(6):
                            term = x * ap_ref[g, block, 6 * e + d]
                            sums = far if g == 2 else near
                            sums[d] = term if sums[d] is None else sums[d] + term
                for d in range(6):
                    row = slice(6 * c + d, 6 * c + d + 1)
                    tail = jnp.sum(far[d], 0, keepdims=True)
                    term_ref[step, row, 0:128] = jnp.sum(near[d], 0, keepdims=True)
                    term_ref[step, row, 128:ROWS] = tail[:, :TILE] + tail[:, TILE:]
            return carry

        lax.fori_loop(0, 15, one_pair, 0)
        r = Order(order_l_ref, order_s_ref)
        owner, rank, after = (x[:, :ROWS] for x in (r.owner_l, r.rank_l, r.after_l))
        member, slot = slot_grid(ROWS)
        mine, row_slot = owner == member, slot < 6.0
        here = ones_where(mine & (rank == slot))
        back_to = member + jnp.where(me == 0, 1.0, 0.0)
        on_to = member - jnp.where(me == MEMBERS - 1, 1.0, 0.0)
        back = (mine & row_slot & (rank == slot + 1.0)) | ((slot == 6.0) & (owner == back_to) & (rank == 0.0))
        on = (mine & row_slot & (rank == slot - 1.0) & (after > 0.0)) | (
            (slot == 7.0) & (owner == on_to) & (after == 0.0)
        )
        picks = [ones_where(back), here, ones_where(on)]
        terms = []
        for k in range(3):
            pieces = [term_ref[5 * k + e][:36, :ROWS] for e in range(5)]
            pieces.append(jnp.zeros((4 + 36 * k, ROWS), F32))
            if k < 2:
                pieces.insert(0, jnp.zeros((72 - 36 * k, ROWS), F32))
            terms.append(jnp.concatenate(pieces, 0))
        total = None
        for k in range(3):
            prod = exact_dot(picks[k], terms[k], NT, True)
            total = prod if total is None else total + prod
        out_ref[...] = total
        head, tail = far_pick(r, me, ROWS)
        far_out[...] = exact_dot(head, terms[0], NT, True) + exact_dot(tail, terms[2], NT, True)


def unpack_smooth_kernel(recv_ref, out_ref, pick_out):
    size = MEMBERS * SLOTS
    count = jnp.broadcast_to(recv_ref[:, 54:55, :].astype(F32), (MEMBERS, SLOTS, 128)).reshape(size, 128)
    source, other = iota((size, size), 0) // SLOTS, iota((size, size), 1) // SLOTS
    first_slot = iota((size, size), 1) % SLOTS == 0
    earlier = ones_where((other < source) & first_slot)
    start = dot(earlier, count.astype(BF16))[:, :1]
    count = count[:, :1]
    slot = (iota((size, 1), 0) % SLOTS).astype(F32)
    place = jnp.where(slot < count, start + slot, -1.0)
    column = iota((size, ROWS), 1).astype(F32)
    pick = ones_where(place == column)
    for block in range(COLS // 128):
        rows = recv_ref[:, 6 * block : 6 * block + 6, :].astype(F32)
        rows = jnp.concatenate([rows, jnp.zeros((MEMBERS, 2, 128), F32)], 1).reshape(size, 128)
        value = lax.dot_general(rows.astype(BF16), pick, TN, preferred_element_type=F32)
        out_ref[128 * block : 128 * (block + 1), :] = value.astype(BF16)
    place = jnp.where(slot == 6.0, jnp.where(start == 0.0, ROWS - 1.0, start - 1.0), place)
    stop = start + count
    place = jnp.where(slot == 7.0, jnp.where(stop == float(ROWS), 0.0, stop), place)
    column = iota((size, WIDE), 1).astype(F32)
    pick_out[...] = jnp.where(place == column, 1.0, 0.0).T[:ROWS].astype(BF16)


def unpack_coarse_kernel(me_ref, pick_ref, sums_ref, far_ref, out_ref):
    me = me_ref[0]
    total = exact_dot(pick_ref[...], sums_ref[...], (((1,), (0,)), ((), ())), True)
    row = iota((ROWS, WIDE), 0)
    edge = jnp.where(me == 0, 0, ROWS - 1)
    far = jnp.broadcast_to(far_ref[0:1, :], (ROWS, WIDE))
    total = total + jnp.where(row == edge, far, 0.0)
    out_ref[...] = total[:, :252]


def call(kernel, outs, args, grid=None, in_specs=None, scratch=(), flops=0, mib=16, name=None):
    whole = lambda shape: pl.BlockSpec(shape, lambda *_: (0,) * len(shape))
    specs = []
    for n, arg in enumerate(args):
        spec = None if in_specs is None else in_specs.get(n)
        if spec is None:
            spec = pl.BlockSpec(memory_space=pltpu.SMEM) if arg.shape == (1,) else whole(arg.shape)
        specs.append(spec)
    moved = sum(a.size * a.dtype.itemsize for a in args) + sum(o.size * o.dtype.itemsize for o in outs)
    return pl.pallas_call(
        kernel,
        grid=(1,) if grid is None else grid,
        in_specs=specs,
        out_specs=[whole(o.shape) for o in outs],
        out_shape=outs,
        scratch_shapes=list(scratch),
        compiler_params=pltpu.CompilerParams(vmem_limit_bytes=mib * MIB),
        cost_estimate=pl.CostEstimate(flops=flops, bytes_accessed=moved, transcendentals=0),
        name=name,
    )(*args)


def shaped(shape, dtype=BF16):
    return jax.ShapeDtypeStruct(shape, dtype)


def swaps(groups):
    ring, axes = MEMBERS, range(groups)
    both = lambda pairs: [q for a, b in pairs for q in ((a, b), (b, a))]
    across = both([(g * ring - 1, g * ring) for g in range(1, groups)])
    away = both([(g * ring + i, g * ring + (i + 1) % ring) for g in axes for i in range(1, ring, 2)])
    near = both([(g * ring + i, g * ring + i + 1) for g in axes for i in range(0, ring, 2)])
    return across, away, near


def per_device(a_band, p_tent, new_owner):
    axes = ("group", "member")
    across, away_pairs, near_pairs = swaps(lax.axis_size("group"))
    me = lax.axis_index("member").astype(jnp.int32).reshape(1)
    a = a_band.transpose(1, 2, 3, 0)
    p = p_tent.transpose(1, 2, 0).reshape(MODES * TILE, ROWS)
    a_spec = pl.BlockSpec(memory_space=pltpu.HBM)
    grid = (TILE // 16,)

    def a_scratch(planes):
        return [
            pltpu.VMEM((planes, TILE, TILE, ROWS), BF16),
            pltpu.SemaphoreType.DMA((planes, TILE // 16)),
            pltpu.VMEM((3, planes, 8, TILE, 128), F32),
        ]

    def exchanged(far, away, near):
        far = lax.ppermute(far, axes, across)
        away = lax.ppermute(away, axes, away_pairs)
        return far, away, lax.ppermute(near, axes, near_pairs)

    def rims(length):
        return [shaped((8, length)), shaped((length // 2, 128)), shaped((length // 2, 128))]

    order_l, order_s, p, *sent = call(
        first_kernel,
        [shaped((8, WIDE), F32), shaped((ROWS, 128), F32), shaped(p.shape)] + rims(MODES * TILE),
        (me, new_owner.reshape(1, ROWS), p),
        name="rims",
    )
    got = exchanged(*sent)
    local = shaped((2, 2, MODES, TILE, 128), F32)
    parts = call(
        middle_kernel,
        [shaped((MODES, TILE, ROWS)), shaped((TILE // 16, 3, 8, 128), F32), local],
        (order_l, order_s, a, p),
        grid=grid,
        in_specs={2: a_spec},
        scratch=[
            *a_scratch(1),
            pltpu.VMEM((2, 1, MODES, TILE, 128), F32),
            pltpu.VMEM((3, MODES, 8, 128), F32),
        ],
        flops=10**9,
        mib=50,
        name="middle",
    )
    s, *sent = call(
        smooth_kernel,
        [shaped((18, TILE, ROWS))] + rims(COLS),
        (me, order_l, order_s, a, *parts, *got),
        grid=grid,
        in_specs={3: a_spec},
        scratch=[*a_scratch(2), pltpu.VMEM(local.shape, F32), pltpu.VMEM((3, 12, 8, 128), F32)],
        flops=10**9,
        mib=50,
        name="smooth",
    )
    got = exchanged(*sent)
    s = s.reshape(COLS, ROWS)
    (packed,) = call(pack_kernel, [shaped((MEMBERS, PACKED, 128))], (order_l, s), name="pack")
    recv = lax.all_to_all(packed, "member", split_axis=0, concat_axis=0, tiled=True)

    sums, far = call(
        product_kernel,
        [shaped((MEMBERS * SLOTS, WIDE), F32), shaped((8, WIDE), F32)],
        (me, order_l, order_s, a, s, *got),
        grid=grid,
        in_specs={3: a_spec},
        scratch=[
            *a_scratch(3),
            pltpu.VMEM((2, 3, 18, TILE, 128), F32),
            pltpu.VMEM((3, TILE // 16, 30, 8, 128), F32),
            pltpu.VMEM((3, TILE // 16, 18, 8, 128), F32),
            pltpu.VMEM((15, 40, WIDE), F32),
        ],
        flops=10**10,
        mib=50,
        name="product",
    )
    far = lax.ppermute(far, axes, across)
    sums = lax.all_to_all(
        sums.reshape(MEMBERS, SLOTS, WIDE), "member", split_axis=0, concat_axis=0, tiled=True
    ).reshape(MEMBERS * SLOTS, WIDE)
    smooth, pick = call(
        unpack_smooth_kernel,
        [shaped((COLS, ROWS)), shaped((ROWS, MEMBERS * SLOTS))],
        (recv,),
        flops=10**9,
        name="unpack_smooth",
    )
    (coarse,) = call(
        unpack_coarse_kernel, [shaped((ROWS, 252), F32)], (me, pick, sums, far), name="unpack_coarse"
    )
    return smooth.reshape(3, MODES, TILE, ROWS).transpose(3, 0, 1, 2), coarse


def solution(mesh):
    in_specs = (
        P(("group", "member"), None, None, None),
        P(("group", "member"), None, None),
        P(("group", "member")),
    )
    out_specs = (P(("group", "member"), None, None, None), P(("group", "member"), None))
    return jax.shard_map(
        per_device, mesh=mesh, in_specs=in_specs, out_specs=out_specs, check_vma=False
    )
```

```python
import jax
import jax.numpy as jnp
from jax import lax
from jax.experimental import pallas as pl
from jax.experimental.pallas import tpu as pltpu
from jax.sharding import PartitionSpec as P

ROWS = 192
WIDE = 256
TILE = 64
MODES = 6
MEMBERS = 64
SLOTS = 8
COLS = 3 * MODES * TILE
F32 = jnp.float32
BF16 = jnp.bfloat16
NT = (((1,), (1,)), ((), ()))
TN = (((0,), (0,)), ((), ()))
MIB = 1024 * 1024
PACKED = 56


def iota(shape, axis):
    return lax.broadcasted_iota(jnp.int32, shape, axis)


def ones_where(mask):
    return jnp.where(mask, 1.0, 0.0).astype(BF16)


def dot(a, b):
    return jnp.dot(a, b, preferred_element_type=F32)


def parts_of(x):
    high = x.astype(BF16)
    rest = x - high.astype(F32)
    mid = rest.astype(BF16)
    low = (rest - mid.astype(F32)).astype(BF16)
    return high, mid, low


def exact_dot(pick, x, dims, pick_first):
    total = None
    for part in parts_of(x):
        ab = (pick, part) if pick_first else (part, pick)
        prod = lax.dot_general(*ab, dims, preferred_element_type=F32)
        total = prod if total is None else total + prod
    return total


def rank_arrays(owner_row):
    owner_row = owner_row.astype(F32)
    owner_row = jnp.concatenate([owner_row, owner_row[:, 128:]], 1)
    wide = jnp.broadcast_to(owner_row, (WIDE, WIDE))
    tall = wide.T[:ROWS]
    wide = wide[:ROWS]
    lane = iota((ROWS, WIDE), 1)
    row_l = jnp.where(lane < ROWS, lane, lane - TILE)
    row_s = iota((ROWS, WIDE), 0)
    one = jnp.where(wide == tall, 1.0, 0.0)
    less, more = row_s < row_l, row_s > row_l
    rank_l = jnp.sum(jnp.where(less, one, 0.0), 0, keepdims=True)
    after_l = jnp.sum(jnp.where(more, one, 0.0), 0, keepdims=True)
    once = jnp.where(lane < ROWS, one, 0.0)
    rank_s = jnp.sum(jnp.where(more, once, 0.0), 1, keepdims=True)
    after_s = jnp.sum(jnp.where(less, once, 0.0), 1, keepdims=True)
    return (wide[:1], rank_l, after_l), (tall[:, :1], rank_s, after_s)


class Order:
    def __init__(self, wide_ref, tall_ref):
        self.owner_l, self.rank_l, self.after_l = (wide_ref[n : n + 1, :] for n in range(3))
        self.owner_s, self.rank_s, self.after_s = (tall_ref[:, n : n + 1] for n in range(3))


def rim_picks(r, me):
    lane = iota((ROWS, 128), 1)
    first, last = r.rank_s == 0.0, r.after_s == 0.0
    even = me % 2 == 0
    picks = []
    for half in (0, 1):
        slot = lane - TILE * half
        inside = (slot >= 0) & (slot < TILE)
        to_left = jnp.where(inside, slot + jnp.where(me == 0, 1, 0), -1).astype(F32)
        to_right = jnp.where(inside, slot - jnp.where(me == MEMBERS - 1, 1, 0), -1).astype(F32)
        left = jnp.where((r.owner_s == to_left) & first, 1.0, 0.0)
        right = jnp.where((r.owner_s == to_right) & last, 1.0, 0.0)
        near = jnp.where(even, right, left).astype(BF16)
        far = jnp.where(even, left, right).astype(BF16)
        picks.append((near, far))
    return picks


def far_pick(r, me, width):
    top = iota((8, width), 0) == 0
    owner, rank, after = r.owner_l[:, :width], r.rank_l[:, :width], r.after_l[:, :width]
    head = top & (me == 0) & (owner == 0.0) & (rank == 0.0)
    tail = top & (me == MEMBERS - 1) & (owner == MEMBERS - 1.0) & (after == 0.0)
    return ones_where(head), ones_where(tail)


def rims_of(rows, r, me):
    half = rows.shape[0] // 2
    top, bottom = rim_picks(r, me)
    rims = [(dot(rows[:half], a) + dot(rows[half:], b)).astype(BF16) for a, b in zip(top, bottom)]
    head, tail = far_pick(r, me, ROWS)
    far = lax.dot_general(head + tail, rows, NT, preferred_element_type=F32).astype(BF16)
    return [far] + rims[::-1]


def local_rows(rows, r):
    lane = iota((ROWS, WIDE), 1)
    row_l = jnp.where(lane < ROWS, lane, lane - TILE)
    same = r.owner_l == r.owner_s
    before = ones_where(same & (r.rank_s + 1.0 == r.rank_l))
    after = ones_where(same & (r.rank_s == r.rank_l + 1.0))
    here = ones_where(iota((ROWS, WIDE), 0) == row_l)
    return [dot(rows, pick) for pick in (before, here, after)]


def rim_rows(near, away, far, r, me):
    bucket = iota((128, WIDE), 0)
    even = me % 2 == 0
    result = []
    for rim, edge, end in zip(
        (jnp.where(even, away, near), jnp.where(even, near, away)), (r.rank_l, r.after_l), far_pick(r, me, WIDE)
    ):
        ends = []
        for side in (0, 1):
            want = bucket - TILE * side
            want = jnp.where((want >= 0) & (want < TILE), want, -1).astype(F32)
            ends.append(dot(rim, ones_where((want == r.owner_l) & (edge == 0.0))))
        result.append(jnp.concatenate(ends, 0) + lax.dot_general(far, end, TN, preferred_element_type=F32))
    return result


def set_wide(ref, k, value):
    for tile in (0, 1):
        part = value[:, 128 * tile : 128 * (tile + 1)]
        ref[tile, k] = part.reshape(-1, TILE, 128)


def chunk_copies(a_hbm, a_ref, sems, planes, n):
    rows = pl.ds(16 * n, 16)
    return [
        pltpu.make_async_copy(a_hbm.at[k, rows], a_ref.at[at, rows], sems.at[at, n])
        for at, k in enumerate(planes)
    ]


def start_copies(a_hbm, a_ref, sems, planes):
    for n in range(TILE // 16):
        for copy in chunk_copies(a_hbm, a_ref, sems, planes, n):
            copy.start()


def next_groups(a_hbm, a_ref, sems, planes, ib, group_ref):
    for copy in chunk_copies(a_hbm, a_ref, sems, planes, ib):
        copy.wait()
    for k in range(len(planes)):
        for i in range(8):
            low, high = (a_ref[k, 16 * ib + i + n].astype(F32) for n in (0, 8))
            group_ref[0, k, i] = low[:, :128]
            group_ref[1, k, i] = high[:, :128]
            group_ref[2, k, i] = jnp.concatenate([low[:, 128:], high[:, 128:]], 1)


def folded(terms):
    sub = iota((8, 128), 0)
    for shift in (1, 2, 4):
        keep = (sub & shift) == 0
        terms = [
            jnp.where(keep, x, y) + pltpu.roll(jnp.where(keep, y, x), shift, 0)
            for x, y in zip(terms[::2], terms[1::2])
        ]
    return terms[0]


def contracted(group_ref, wide_ref, g, tile, pairs, columns):
    totals = [[None] * 8 for _ in columns]
    for jb in range(TILE // 8):
        j = pl.ds(8 * jb, 8)
        for k, base in pairs:
            a = [group_ref[g, k, i, j, :] for i in range(8)]
            for n, column in enumerate(columns):
                x = wide_ref[tile, k, base + column, j, :]
                for i in range(8):
                    term = a[i] * x
                    totals[n][i] = term if totals[n][i] is None else totals[n][i] + term
    return [folded(t) for t in totals]


def ungrouped(out_ref, index):
    low, high, both = out_ref[0, index], out_ref[1, index], out_ref[2, index]
    top = jnp.concatenate([low, both[:, :TILE]], 1)
    bottom = jnp.concatenate([high, both[:, TILE:]], 1)
    return jnp.concatenate([top, bottom], 0)


def first_kernel(me_ref, owner_ref, p_ref, wide_ref, tall_ref, p_out, far_out, away_out, near_out):
    rows, columns = rank_arrays(owner_ref[...])
    p_out[...] = p_ref[...]
    wide_ref[...] = jnp.zeros_like(wide_ref)
    for n in range(3):
        wide_ref[n : n + 1, :] = rows[n]
    lane = iota((ROWS, 128), 1)
    tall_ref[...] = jnp.where(lane == 0, columns[0], jnp.where(lane == 1, columns[1], columns[2]))
    r = Order(wide_ref, tall_ref)
    for ref, rim in zip((far_out, away_out, near_out), rims_of(p_ref[...], r, me_ref[0])):
        ref[...] = rim


def halves(ib):
    return pl.ds(pl.multiple_of(16 * ib, 8), 8), pl.ds(pl.multiple_of(16 * ib + 8, 8), 8)


def middle_kernel(
    order_l_ref, order_s_ref, a_hbm, p_ref, mid_ref, scale_ref, local_ref,
    a_ref, sems, group_ref, wide_ref, out_ref,
):
    ib = pl.program_id(0)

    @pl.when(ib == 0)
    def _():
        start_copies(a_hbm, a_ref, sems, (1,))
        before, here, after = local_rows(p_ref[...], Order(order_l_ref, order_s_ref))
        set_wide(wide_ref, 0, here)
        set_wide(local_ref, 0, before)
        set_wide(local_ref, 1, after)

    next_groups(a_hbm, a_ref, sems, (1,), ib, group_ref)
    sub, lane = iota((8, 128), 0), iota((8, 128), 1)
    lower, upper = halves(ib)

    def one_group(g, carry):
        tile = jnp.where(g == 2, 1, 0)
        second = (g == 1) | ((g == 2) & (lane >= TILE))
        diag = jnp.zeros((8, 128), F32)
        for i in range(8):
            entry = jnp.where(second, group_ref[g, 0, i, upper, :], group_ref[g, 0, i, lower, :])
            diag = jnp.where(sub == i, entry, diag)
        scale = 0.6 * (1.0 / diag)
        scale_ref[ib, g] = scale
        for half in (0, 1):
            columns = [3 * half + c for c in range(3)]
            sums = contracted(group_ref, wide_ref, g, tile, [(0, 0)], columns)
            for c, total in zip(columns, sums):
                own = jnp.where(second, wide_ref[tile, 0, c, upper, :], wide_ref[tile, 0, c, lower, :])
                out_ref[g, c] = own - scale * total
        return carry

    lax.fori_loop(0, 3, one_group, 0)
    rows = pl.ds(pl.multiple_of(16 * ib, 16), 16)
    for index in range(6):
        mid_ref[index, rows, :] = ungrouped(out_ref, index).astype(BF16)


def smooth_kernel(
    me_ref, order_l_ref, order_s_ref, a_hbm, mid_ref, scale_ref, local_ref, far_ref, away_ref, near_ref,
    s_ref, far_out, away_out, near_out, a_ref, sems, group_ref, wide_ref, out_ref,
):
    ib = pl.program_id(0)
    me = me_ref[0]

    @pl.when(ib == 0)
    def _():
        start_copies(a_hbm, a_ref, sems, (0, 2))
        r = Order(order_l_ref, order_s_ref)
        for k, value in enumerate(rim_rows(near_ref[...], away_ref[...], far_ref[...], r, me)):
            set_wide(wide_ref, k, value)
        wide_ref[...] += local_ref[...]
        s_ref[6:12] = mid_ref[...]

    next_groups(a_hbm, a_ref, sems, (0, 2), ib, group_ref)

    def one_group(g, carry):
        tile = jnp.where(g == 2, 1, 0)
        scale = 0.0 - scale_ref[ib, g]
        for k in range(2):
            for half in (0, 1):
                columns = [3 * half + c for c in range(3)]
                sums = contracted(group_ref, wide_ref, g, tile, [(k, 0)], columns)
                for c, total in zip(columns, sums):
                    out_ref[g, 6 * k + c] = scale * total
        return carry

    lax.fori_loop(0, 3, one_group, 0)
    rows = pl.ds(pl.multiple_of(16 * ib, 16), 16)
    for index in range(12):
        s_ref[index if index < 6 else index + 6, rows, :] = ungrouped(out_ref, index).astype(BF16)

    @pl.when(ib == pl.num_programs(0) - 1)
    def _():
        r = Order(order_l_ref, order_s_ref)
        flat = s_ref[...].reshape(COLS, ROWS)
        for ref, rim in zip((far_out, away_out, near_out), rims_of(flat, r, me)):
            ref[...] = rim


def slot_grid(width):
    spot = iota((MEMBERS * SLOTS, width), 0)
    return (spot // SLOTS).astype(F32), (spot % SLOTS).astype(F32)


def pack_kernel(order_l_ref, s_ref, out_ref):
    member, slot = slot_grid(ROWS)
    owner, rank = order_l_ref[0:1, :ROWS], order_l_ref[1:2, :ROWS]
    mine = owner == member
    pick = ones_where(mine & (rank == slot))
    count = jnp.sum(jnp.where(mine, 1.0, 0.0), 1, keepdims=True)
    for block in range(COLS // 128):
        value = lax.dot_general(
            pick, s_ref[128 * block : 128 * (block + 1), :], NT, preferred_element_type=F32
        ).reshape(MEMBERS, SLOTS, 128)
        out_ref[:, 6 * block : 6 * block + 6, :] = value[:, :6, :].astype(BF16)
    counts = jnp.broadcast_to(count, (MEMBERS * SLOTS, 128)).reshape(MEMBERS, SLOTS, 128)
    out_ref[:, 54:56, :] = counts[:, :2, :].astype(BF16)


OFFSETS = [[(k, 6 * (e - k)) for k in range(3) if 0 <= e - k <= 2] for e in range(5)]


def spare_lanes(axis):
    entry, spare = iota((WIDE, WIDE), axis), iota((WIDE, WIDE), 1 - axis) - 252
    return ones_where((spare >= 0) & (entry == 108 + 7 * spare))


def product_kernel(
    me_ref, order_l_ref, order_s_ref, a_hbm, s_ref, far_ref, away_ref, near_ref,
    out_ref, far_out, a_ref, sems, group_ref, wide_ref, ap_ref, own_ref, term_ref,
):
    ib = pl.program_id(0)
    me = me_ref[0]

    @pl.when(ib == 0)
    def _():
        start_copies(a_hbm, a_ref, sems, (0, 1, 2))
        r = Order(order_l_ref, order_s_ref)
        before, here, after = local_rows(s_ref[...], r)
        left, right = rim_rows(near_ref[...], away_ref[...], far_ref[...], r, me)
        for k, value in enumerate((before + left, here, after + right)):
            set_wide(wide_ref, k, value)
        term_ref[...] = jnp.zeros_like(term_ref)

    next_groups(a_hbm, a_ref, sems, (0, 1, 2), ib, group_ref)
    lane = iota((8, 128), 1)

    def one_group(step, carry):
        g, half = step // 2, step % 2
        tile = jnp.where(g == 2, 1, 0)
        for e in range(5):
            columns = [3 * half + c for c in range(3)]
            sums = contracted(group_ref, wide_ref, g, tile, OFFSETS[e], columns)
            for c, total in zip(columns, sums):
                ap_ref[g, ib, 6 * e + c] = total.astype(BF16).astype(F32)
        second = (g == 1) | ((g == 2) & (lane >= TILE))
        lower, upper = pl.ds(pl.multiple_of(16 * ib, 8), 8), pl.ds(pl.multiple_of(16 * ib + 8, 8), 8)
        for c in range(9):
            column = 9 * half + c
            own_ref[g, ib, column] = jnp.where(
                second, wide_ref[tile, 1, column, upper, :], wide_ref[tile, 1, column, lower, :]
            )
        return carry

    lax.fori_loop(0, 6, one_group, 0)

    @pl.when(ib == pl.num_programs(0) - 1)
    def _():
        def one_pair(step, carry):
            k, e = step // 5, step % 5
            for c in range(6):
                near, far = [None] * 6, [None] * 6
                for block in range(TILE // 16):
                    for g in range(3):
                        x = own_ref[g, block, 6 * k + c]
                        for d in range(6):
                            term = x * ap_ref[g, block, 6 * e + d]
                            sums = far if g == 2 else near
                            sums[d] = term if sums[d] is None else sums[d] + term
                for d in range(6):
                    row = slice(6 * c + d, 6 * c + d + 1)
                    tail = jnp.sum(far[d], 0, keepdims=True)
                    term_ref[step, row, 0:128] = jnp.sum(near[d], 0, keepdims=True)
                    term_ref[step, row, 128:ROWS] = tail[:, :TILE] + tail[:, TILE:]
            return carry

        lax.fori_loop(0, 15, one_pair, 0)
        r = Order(order_l_ref, order_s_ref)
        owner, rank, after = (x[:, :ROWS] for x in (r.owner_l, r.rank_l, r.after_l))
        member, slot = slot_grid(ROWS)
        mine, row_slot = owner == member, slot < 6.0
        here = ones_where(mine & (rank == slot))
        back_to = member + jnp.where(me == 0, 1.0, 0.0)
        on_to = member - jnp.where(me == MEMBERS - 1, 1.0, 0.0)
        back = (mine & row_slot & (rank == slot + 1.0)) | ((slot == 6.0) & (owner == back_to) & (rank == 0.0))
        on = (mine & row_slot & (rank == slot - 1.0) & (after > 0.0)) | (
            (slot == 7.0) & (owner == on_to) & (after == 0.0)
        )
        picks = [ones_where(back), here, ones_where(on)]
        terms = []
        for k in range(3):
            pieces = [term_ref[5 * k + e][:36, :ROWS] for e in range(5)]
            pieces.append(jnp.zeros((4 + 36 * k, ROWS), F32))
            if k < 2:
                pieces.insert(0, jnp.zeros((72 - 36 * k, ROWS), F32))
            terms.append(jnp.concatenate(pieces, 0))
        total = None
        for k in range(3):
            prod = exact_dot(picks[k], terms[k], NT, True)
            total = prod if total is None else total + prod
        high = total.astype(BF16).astype(F32)
        rest = dot((total - high).astype(BF16), spare_lanes(0))
        out_ref[...] = (high + rest).astype(BF16)
        head, tail = far_pick(r, me, ROWS)
        far_out[...] = exact_dot(head, terms[0], NT, True) + exact_dot(tail, terms[2], NT, True)


def unpack_smooth_kernel(recv_ref, out_ref, pick_out):
    size = MEMBERS * SLOTS
    count = jnp.broadcast_to(recv_ref[:, 54:55, :].astype(F32), (MEMBERS, SLOTS, 128)).reshape(size, 128)
    source, other = iota((size, size), 0) // SLOTS, iota((size, size), 1) // SLOTS
    first_slot = iota((size, size), 1) % SLOTS == 0
    earlier = ones_where((other < source) & first_slot)
    start = dot(earlier, count.astype(BF16))[:, :1]
    count = count[:, :1]
    slot = (iota((size, 1), 0) % SLOTS).astype(F32)
    place = jnp.where(slot < count, start + slot, -1.0)
    column = iota((size, ROWS), 1).astype(F32)
    pick = ones_where(place == column)
    for block in range(COLS // 128):
        rows = recv_ref[:, 6 * block : 6 * block + 6, :].astype(F32)
        rows = jnp.concatenate([rows, jnp.zeros((MEMBERS, 2, 128), F32)], 1).reshape(size, 128)
        value = lax.dot_general(rows.astype(BF16), pick, TN, preferred_element_type=F32)
        out_ref[128 * block : 128 * (block + 1), :] = value.astype(BF16)
    place = jnp.where(slot == 6.0, jnp.where(start == 0.0, ROWS - 1.0, start - 1.0), place)
    stop = start + count
    place = jnp.where(slot == 7.0, jnp.where(stop == float(ROWS), 0.0, stop), place)
    column = iota((size, WIDE), 1).astype(F32)
    pick_out[...] = jnp.where(place == column, 1.0, 0.0).T[:ROWS].astype(BF16)


def unpack_coarse_kernel(me_ref, pick_ref, sums_ref, far_ref, out_ref):
    me = me_ref[0]
    total = dot(pick_ref[...], sums_ref[...])
    total = total + dot(total.astype(BF16), spare_lanes(1))
    row = iota((ROWS, WIDE), 0)
    edge = jnp.where(me == 0, 0, ROWS - 1)
    far = jnp.broadcast_to(far_ref[0:1, :], (ROWS, WIDE))
    total = total + jnp.where(row == edge, far, 0.0)
    out_ref[...] = total[:, :252]


def call(kernel, outs, args, grid=None, in_specs=None, scratch=(), flops=0, mib=16, name=None):
    whole = lambda shape: pl.BlockSpec(shape, lambda *_: (0,) * len(shape))
    specs = []
    for n, arg in enumerate(args):
        spec = None if in_specs is None else in_specs.get(n)
        if spec is None:
            spec = pl.BlockSpec(memory_space=pltpu.SMEM) if arg.shape == (1,) else whole(arg.shape)
        specs.append(spec)
    moved = sum(a.size * a.dtype.itemsize for a in args) + sum(o.size * o.dtype.itemsize for o in outs)
    return pl.pallas_call(
        kernel,
        grid=(1,) if grid is None else grid,
        in_specs=specs,
        out_specs=[whole(o.shape) for o in outs],
        out_shape=outs,
        scratch_shapes=list(scratch),
        compiler_params=pltpu.CompilerParams(vmem_limit_bytes=mib * MIB),
        cost_estimate=pl.CostEstimate(flops=flops, bytes_accessed=moved, transcendentals=0),
        name=name,
    )(*args)


def shaped(shape, dtype=BF16):
    return jax.ShapeDtypeStruct(shape, dtype)


def swaps(groups):
    ring, axes = MEMBERS, range(groups)
    both = lambda pairs: [q for a, b in pairs for q in ((a, b), (b, a))]
    across = both([(g * ring - 1, g * ring) for g in range(1, groups)])
    away = both([(g * ring + i, g * ring + (i + 1) % ring) for g in axes for i in range(1, ring, 2)])
    near = both([(g * ring + i, g * ring + i + 1) for g in axes for i in range(0, ring, 2)])
    return across, away, near


def per_device(a_band, p_tent, new_owner):
    axes = ("group", "member")
    across, away_pairs, near_pairs = swaps(lax.axis_size("group"))
    me = lax.axis_index("member").astype(jnp.int32).reshape(1)
    a = a_band.transpose(1, 2, 3, 0)
    p = p_tent.transpose(1, 2, 0).reshape(MODES * TILE, ROWS)
    a_spec = pl.BlockSpec(memory_space=pltpu.HBM)
    grid = (TILE // 16,)

    def a_scratch(planes):
        return [
            pltpu.VMEM((planes, TILE, TILE, ROWS), BF16),
            pltpu.SemaphoreType.DMA((planes, TILE // 16)),
            pltpu.VMEM((3, planes, 8, TILE, 128), F32),
        ]

    def exchanged(far, away, near):
        far = lax.ppermute(far, axes, across)
        away = lax.ppermute(away, axes, away_pairs)
        return far, away, lax.ppermute(near, axes, near_pairs)

    def rims(length):
        return [shaped((8, length)), shaped((length // 2, 128)), shaped((length // 2, 128))]

    order_l, order_s, p, *sent = call(
        first_kernel,
        [shaped((8, WIDE), F32), shaped((ROWS, 128), F32), shaped(p.shape)] + rims(MODES * TILE),
        (me, new_owner.reshape(1, ROWS), p),
        name="rims",
    )
    got = exchanged(*sent)
    local = shaped((2, 2, MODES, TILE, 128), F32)
    parts = call(
        middle_kernel,
        [shaped((MODES, TILE, ROWS)), shaped((TILE // 16, 3, 8, 128), F32), local],
        (order_l, order_s, a, p),
        grid=grid,
        in_specs={2: a_spec},
        scratch=[
            *a_scratch(1),
            pltpu.VMEM((2, 1, MODES, TILE, 128), F32),
            pltpu.VMEM((3, MODES, 8, 128), F32),
        ],
        flops=10**9,
        mib=50,
        name="middle",
    )
    s, *sent = call(
        smooth_kernel,
        [shaped((18, TILE, ROWS))] + rims(COLS),
        (me, order_l, order_s, a, *parts, *got),
        grid=grid,
        in_specs={3: a_spec},
        scratch=[*a_scratch(2), pltpu.VMEM(local.shape, F32), pltpu.VMEM((3, 12, 8, 128), F32)],
        flops=10**9,
        mib=50,
        name="smooth",
    )
    got = exchanged(*sent)
    s = s.reshape(COLS, ROWS)
    (packed,) = call(pack_kernel, [shaped((MEMBERS, PACKED, 128))], (order_l, s), name="pack")
    packed, *got = lax.optimization_barrier((packed, *got))
    recv = lax.all_to_all(packed, "member", split_axis=0, concat_axis=0, tiled=True)

    sums, far = call(
        product_kernel,
        [shaped((MEMBERS * SLOTS, WIDE)), shaped((8, WIDE), F32)],
        (me, order_l, order_s, a, s, *got),
        grid=grid,
        in_specs={3: a_spec},
        scratch=[
            *a_scratch(3),
            pltpu.VMEM((2, 3, 18, TILE, 128), F32),
            pltpu.VMEM((3, TILE // 16, 30, 8, 128), F32),
            pltpu.VMEM((3, TILE // 16, 18, 8, 128), F32),
            pltpu.VMEM((15, 40, WIDE), F32),
        ],
        flops=10**10,
        mib=50,
        name="product",
    )
    far = lax.ppermute(far, axes, across)
    sums = lax.all_to_all(
        sums.reshape(MEMBERS, SLOTS, WIDE), "member", split_axis=0, concat_axis=0, tiled=True
    ).reshape(MEMBERS * SLOTS, WIDE)
    smooth, pick = call(
        unpack_smooth_kernel,
        [shaped((COLS, ROWS)), shaped((ROWS, MEMBERS * SLOTS))],
        (recv,),
        flops=10**9,
        name="unpack_smooth",
    )
    (coarse,) = call(
        unpack_coarse_kernel, [shaped((ROWS, 252), F32)], (me, pick, sums, far), name="unpack_coarse"
    )
    return smooth.reshape(3, MODES, TILE, ROWS).transpose(3, 0, 1, 2), coarse


def solution(mesh):
    in_specs = (
        P(("group", "member"), None, None, None),
        P(("group", "member"), None, None),
        P(("group", "member")),
    )
    out_specs = (P(("group", "member"), None, None, None), P(("group", "member"), None))
    return jax.shard_map(
        per_device, mesh=mesh, in_specs=in_specs, out_specs=out_specs, check_vma=False
    )
```

```python
import jax
import jax.numpy as jnp
from jax import lax
from jax.experimental import pallas as pl
from jax.experimental.pallas import tpu as pltpu
from jax.sharding import PartitionSpec as P

ROWS = 192
WIDE = 256
TILE = 64
MODES = 6
MEMBERS = 64
SLOTS = 8
COLS = 3 * MODES * TILE
F32 = jnp.float32
BF16 = jnp.bfloat16
NT = (((1,), (1,)), ((), ()))
TN = (((0,), (0,)), ((), ()))
MIB = 1024 * 1024
PACKED = 56


def iota(shape, axis):
    return lax.broadcasted_iota(jnp.int32, shape, axis)


def ones_where(mask):
    return jnp.where(mask, 1.0, 0.0).astype(BF16)


def dot(a, b):
    return jnp.dot(a, b, preferred_element_type=F32)


def parts_of(x):
    high = x.astype(BF16)
    rest = x - high.astype(F32)
    mid = rest.astype(BF16)
    low = (rest - mid.astype(F32)).astype(BF16)
    return high, mid, low


def exact_dot(pick, x, dims, pick_first):
    total = None
    for part in parts_of(x):
        ab = (pick, part) if pick_first else (part, pick)
        prod = lax.dot_general(*ab, dims, preferred_element_type=F32)
        total = prod if total is None else total + prod
    return total


def rank_arrays(owner_row):
    owner_row = owner_row.astype(F32)
    owner_row = jnp.concatenate([owner_row, owner_row[:, 128:]], 1)
    wide = jnp.broadcast_to(owner_row, (WIDE, WIDE))
    tall = wide.T[:ROWS]
    wide = wide[:ROWS]
    lane = iota((ROWS, WIDE), 1)
    row_l = jnp.where(lane < ROWS, lane, lane - TILE)
    row_s = iota((ROWS, WIDE), 0)
    one = jnp.where(wide == tall, 1.0, 0.0)
    less, more = row_s < row_l, row_s > row_l
    rank_l = jnp.sum(jnp.where(less, one, 0.0), 0, keepdims=True)
    after_l = jnp.sum(jnp.where(more, one, 0.0), 0, keepdims=True)
    once = jnp.where(lane < ROWS, one, 0.0)
    rank_s = jnp.sum(jnp.where(more, once, 0.0), 1, keepdims=True)
    after_s = jnp.sum(jnp.where(less, once, 0.0), 1, keepdims=True)
    return (wide[:1], rank_l, after_l), (tall[:, :1], rank_s, after_s)


class Order:
    def __init__(self, wide_ref, tall_ref):
        self.owner_l, self.rank_l, self.after_l = (wide_ref[n : n + 1, :] for n in range(3))
        self.owner_s, self.rank_s, self.after_s = (tall_ref[:, n : n + 1] for n in range(3))


def rim_picks(r, me):
    lane = iota((ROWS, 128), 1)
    first, last = r.rank_s == 0.0, r.after_s == 0.0
    even = me % 2 == 0
    picks = []
    for half in (0, 1):
        slot = lane - TILE * half
        inside = (slot >= 0) & (slot < TILE)
        to_left = jnp.where(inside, slot + jnp.where(me == 0, 1, 0), -1).astype(F32)
        to_right = jnp.where(inside, slot - jnp.where(me == MEMBERS - 1, 1, 0), -1).astype(F32)
        left = jnp.where((r.owner_s == to_left) & first, 1.0, 0.0)
        right = jnp.where((r.owner_s == to_right) & last, 1.0, 0.0)
        near = jnp.where(even, right, left).astype(BF16)
        far = jnp.where(even, left, right).astype(BF16)
        picks.append((near, far))
    return picks


def far_pick(r, me, width):
    top = iota((8, width), 0) == 0
    owner, rank, after = r.owner_l[:, :width], r.rank_l[:, :width], r.after_l[:, :width]
    head = top & (me == 0) & (owner == 0.0) & (rank == 0.0)
    tail = top & (me == MEMBERS - 1) & (owner == MEMBERS - 1.0) & (after == 0.0)
    return ones_where(head), ones_where(tail)


def rims_of(rows, r, me):
    half = rows.shape[0] // 2
    top, bottom = rim_picks(r, me)
    rims = [(dot(rows[:half], a) + dot(rows[half:], b)).astype(BF16) for a, b in zip(top, bottom)]
    head, tail = far_pick(r, me, ROWS)
    far = lax.dot_general(head + tail, rows, NT, preferred_element_type=F32).astype(BF16)
    return [far] + rims[::-1]


def local_rows(rows, r):
    lane = iota((ROWS, WIDE), 1)
    row_l = jnp.where(lane < ROWS, lane, lane - TILE)
    same = r.owner_l == r.owner_s
    before = ones_where(same & (r.rank_s + 1.0 == r.rank_l))
    after = ones_where(same & (r.rank_s == r.rank_l + 1.0))
    here = ones_where(iota((ROWS, WIDE), 0) == row_l)
    return [dot(rows, pick) for pick in (before, here, after)]


def rim_rows(near, away, far, r, me):
    bucket = iota((128, WIDE), 0)
    even = me % 2 == 0
    result = []
    for rim, edge, end in zip(
        (jnp.where(even, away, near), jnp.where(even, near, away)), (r.rank_l, r.after_l), far_pick(r, me, WIDE)
    ):
        ends = []
        for side in (0, 1):
            want = bucket - TILE * side
            want = jnp.where((want >= 0) & (want < TILE), want, -1).astype(F32)
            ends.append(dot(rim, ones_where((want == r.owner_l) & (edge == 0.0))))
        result.append(jnp.concatenate(ends, 0) + lax.dot_general(far, end, TN, preferred_element_type=F32))
    return result


def set_wide(ref, k, value):
    for tile in (0, 1):
        part = value[:, 128 * tile : 128 * (tile + 1)]
        ref[tile, k] = part.reshape(-1, TILE, 128)


def chunk_copies(a_hbm, a_ref, sems, planes, n):
    rows = pl.ds(16 * n, 16)
    return [
        pltpu.make_async_copy(a_hbm.at[k, rows], a_ref.at[at, rows], sems.at[at, n])
        for at, k in enumerate(planes)
    ]


def start_copies(a_hbm, a_ref, sems, planes):
    for n in range(TILE // 16):
        for copy in chunk_copies(a_hbm, a_ref, sems, planes, n):
            copy.start()


def next_groups(a_hbm, a_ref, sems, planes, ib, group_ref):
    for copy in chunk_copies(a_hbm, a_ref, sems, planes, ib):
        copy.wait()
    for k in range(len(planes)):
        for i in range(8):
            low, high = (a_ref[k, 16 * ib + i + n].astype(F32) for n in (0, 8))
            group_ref[0, k, i] = low[:, :128]
            group_ref[1, k, i] = high[:, :128]
            group_ref[2, k, i] = jnp.concatenate([low[:, 128:], high[:, 128:]], 1)


def folded(terms):
    sub = iota((8, 128), 0)
    for shift in (1, 2, 4):
        keep = (sub & shift) == 0
        terms = [
            jnp.where(keep, x, y) + pltpu.roll(jnp.where(keep, y, x), shift, 0)
            for x, y in zip(terms[::2], terms[1::2])
        ]
    return terms[0]


def contracted(group_ref, wide_ref, g, tile, pairs, columns):
    totals = [[None] * 8 for _ in columns]
    for jb in range(TILE // 8):
        j = pl.ds(8 * jb, 8)
        for k, base in pairs:
            a = [group_ref[g, k, i, j, :] for i in range(8)]
            for n, column in enumerate(columns):
                x = wide_ref[tile, k, base + column, j, :]
                for i in range(8):
                    term = a[i] * x
                    totals[n][i] = term if totals[n][i] is None else totals[n][i] + term
    return [folded(t) for t in totals]


def ungrouped(out_ref, index):
    low, high, both = out_ref[0, index], out_ref[1, index], out_ref[2, index]
    top = jnp.concatenate([low, both[:, :TILE]], 1)
    bottom = jnp.concatenate([high, both[:, TILE:]], 1)
    return jnp.concatenate([top, bottom], 0)


def first_kernel(me_ref, owner_ref, p_ref, wide_ref, tall_ref, p_out, far_out, away_out, near_out):
    rows, columns = rank_arrays(owner_ref[...])
    p_out[...] = p_ref[...]
    wide_ref[...] = jnp.zeros_like(wide_ref)
    for n in range(3):
        wide_ref[n : n + 1, :] = rows[n]
    lane = iota((ROWS, 128), 1)
    tall_ref[...] = jnp.where(lane == 0, columns[0], jnp.where(lane == 1, columns[1], columns[2]))
    r = Order(wide_ref, tall_ref)
    for ref, rim in zip((far_out, away_out, near_out), rims_of(p_ref[...], r, me_ref[0])):
        ref[...] = rim


def halves(ib):
    return pl.ds(pl.multiple_of(16 * ib, 8), 8), pl.ds(pl.multiple_of(16 * ib + 8, 8), 8)


def end_picks(r):
    lane = iota((ROWS, 128), 1)
    bucket = jnp.where(lane < TILE, lane, lane - TILE).astype(F32)
    mine = r.owner_s == bucket
    first = ones_where(mine & (lane < TILE) & (r.rank_s == 0.0))
    last = ones_where(mine & (lane >= TILE) & (r.after_s == 0.0))
    return first, last


def middle_kernel(
    order_l_ref, order_s_ref, a_hbm, p_ref, s_ref, ends_ref, end_scale_ref,
    a_ref, sems, group_ref, wide_ref, out_ref, scale_ref,
):
    ib = pl.program_id(0)
    r = Order(order_l_ref, order_s_ref)

    @pl.when(ib == 0)
    def _():
        start_copies(a_hbm, a_ref, sems, (0, 1, 2))
        for k, value in enumerate(local_rows(p_ref[...], r)):
            set_wide(wide_ref, k, value)

    next_groups(a_hbm, a_ref, sems, (0, 1, 2), ib, group_ref)
    sub, lane = iota((8, 128), 0), iota((8, 128), 1)
    lower, upper = halves(ib)
    rows = pl.ds(pl.multiple_of(16 * ib, 16), 16)
    first, last = end_picks(r)
    ends = dot(a_ref[0, rows].reshape(16 * TILE, ROWS), first) + dot(a_ref[2, rows].reshape(16 * TILE, ROWS), last)
    ends_ref[rows] = ends.reshape(16, TILE, 128).astype(BF16)

    def one_group(g, carry):
        tile = jnp.where(g == 2, 1, 0)
        second = (g == 1) | ((g == 2) & (lane >= TILE))
        diag = jnp.zeros((8, 128), F32)
        for i in range(8):
            entry = jnp.where(second, group_ref[g, 1, i, upper, :], group_ref[g, 1, i, lower, :])
            diag = jnp.where(sub == i, entry, diag)
        scale = 0.6 * (1.0 / diag)
        out_ref[g, 18] = scale
        for k in range(3):
            for half in (0, 1):
                columns = [3 * half + c for c in range(3)]
                sums = contracted(group_ref, wide_ref, g, tile, [(k, 0)], columns)
                for c, total in zip(columns, sums):
                    value = scale * total
                    if k == 1:
                        own = jnp.where(second, wide_ref[tile, 1, c, upper, :], wide_ref[tile, 1, c, lower, :])
                        value = own - value
                    else:
                        value = 0.0 - value
                    out_ref[g, 6 * k + c] = value
        return carry

    lax.fori_loop(0, 3, one_group, 0)
    for index in range(18):
        s_ref[index, rows, :] = ungrouped(out_ref, index).astype(BF16)
    scale_ref[rows, :] = ungrouped(out_ref, 18)

    @pl.when(ib == pl.num_programs(0) - 1)
    def _():
        end_scale_ref[...] = exact_dot(first + last, scale_ref[...], (((1,), (0,)), ((), ())), False)


def smooth_kernel(
    me_ref, order_l_ref, order_s_ref, part_ref, ends_ref, end_scale_ref, far_ref, away_ref, near_ref,
    s_ref, far_out, away_out, near_out, group_ref, wide_ref, end_ref,
):
    me = me_ref[0]
    even = me % 2 == 0
    near, away = near_ref[...].astype(F32), away_ref[...].astype(F32)
    left, right = jnp.where(even, away, near), jnp.where(even, near, away)
    top = jnp.concatenate([left[:, :TILE], right[:, :TILE]], 1)
    bottom = jnp.concatenate([left[:, TILE:], right[:, TILE:]], 1)
    row, lane = iota((8, 128), 0), iota((8, 128), 1)
    spot = ((me == 0) & (lane == 0)) | ((me == MEMBERS - 1) & (lane == 127))
    across = lax.dot_general(far_ref[...], ones_where((row == 0) & spot), TN, preferred_element_type=F32)
    wide_ref[0, 0] = (jnp.concatenate([top, bottom], 0) + across).reshape(MODES, TILE, 128)

    def one_group(g, carry):
        rows = pl.ds(pl.multiple_of(8 * g, 8), 8)
        for i in range(8):
            group_ref[0, 0, i] = ends_ref[8 * g + i].astype(F32)
        for half in (0, 1):
            columns = [3 * half + c for c in range(3)]
            sums = contracted(group_ref, wide_ref, 0, 0, [(0, 0)], columns)
            for c, total in zip(columns, sums):
                end_ref[c, rows, :] = 0.0 - end_scale_ref[rows, :] * total
        return carry

    lax.fori_loop(0, TILE // 8, one_group, 0)
    r = Order(order_l_ref, order_s_ref)
    bucket = iota((128, ROWS), 0).astype(F32)
    owner = r.owner_l[:, :ROWS]
    first = ones_where((owner == bucket) & (r.rank_l[:, :ROWS] == 0.0))
    last = ones_where((owner + float(TILE) == bucket) & (r.after_l[:, :ROWS] == 0.0))
    found = end_ref[...].astype(BF16).reshape(MODES * TILE, 128)
    s_ref[MODES : 2 * MODES] = part_ref[MODES : 2 * MODES]
    for k, pick in ((0, first), (2, last)):
        at = slice(MODES * k, MODES * (k + 1))
        value = dot(found, pick).reshape(MODES, TILE, ROWS) + part_ref[at].astype(F32)
        s_ref[at] = value.astype(BF16)
    flat = s_ref[...].reshape(COLS, ROWS)
    for ref, rim in zip((far_out, away_out, near_out), rims_of(flat, r, me)):
        ref[...] = rim


def slot_grid(width):
    spot = iota((MEMBERS * SLOTS, width), 0)
    return (spot // SLOTS).astype(F32), (spot % SLOTS).astype(F32)


def pack_kernel(order_l_ref, s_ref, out_ref):
    member, slot = slot_grid(ROWS)
    owner, rank = order_l_ref[0:1, :ROWS], order_l_ref[1:2, :ROWS]
    mine = owner == member
    pick = ones_where(mine & (rank == slot))
    count = jnp.sum(jnp.where(mine, 1.0, 0.0), 1, keepdims=True)
    for block in range(COLS // 128):
        value = lax.dot_general(
            pick, s_ref[128 * block : 128 * (block + 1), :], NT, preferred_element_type=F32
        ).reshape(MEMBERS, SLOTS, 128)
        out_ref[:, 6 * block : 6 * block + 6, :] = value[:, :6, :].astype(BF16)
    counts = jnp.broadcast_to(count, (MEMBERS * SLOTS, 128)).reshape(MEMBERS, SLOTS, 128)
    out_ref[:, 54:56, :] = counts[:, :2, :].astype(BF16)


OFFSETS = [[(k, 6 * (e - k)) for k in range(3) if 0 <= e - k <= 2] for e in range(5)]


def spare_lanes(axis):
    entry, spare = iota((WIDE, WIDE), axis), iota((WIDE, WIDE), 1 - axis) - 252
    return ones_where((spare >= 0) & (entry == 108 + 7 * spare))


def product_kernel(
    me_ref, order_l_ref, order_s_ref, a_hbm, s_ref, far_ref, away_ref, near_ref,
    out_ref, far_out, a_ref, sems, group_ref, wide_ref, ap_ref, own_ref, term_ref,
):
    ib = pl.program_id(0)
    me = me_ref[0]

    @pl.when(ib == 0)
    def _():
        start_copies(a_hbm, a_ref, sems, (0, 1, 2))
        r = Order(order_l_ref, order_s_ref)
        before, here, after = local_rows(s_ref[...], r)
        left, right = rim_rows(near_ref[...], away_ref[...], far_ref[...], r, me)
        for k, value in enumerate((before + left, here, after + right)):
            set_wide(wide_ref, k, value)
        term_ref[...] = jnp.zeros_like(term_ref)

    next_groups(a_hbm, a_ref, sems, (0, 1, 2), ib, group_ref)
    lane = iota((8, 128), 1)

    def one_group(step, carry):
        g, half = step // 2, step % 2
        tile = jnp.where(g == 2, 1, 0)
        for e in range(5):
            columns = [3 * half + c for c in range(3)]
            sums = contracted(group_ref, wide_ref, g, tile, OFFSETS[e], columns)
            for c, total in zip(columns, sums):
                ap_ref[g, ib, 6 * e + c] = total.astype(BF16).astype(F32)
        second = (g == 1) | ((g == 2) & (lane >= TILE))
        lower, upper = pl.ds(pl.multiple_of(16 * ib, 8), 8), pl.ds(pl.multiple_of(16 * ib + 8, 8), 8)
        for c in range(9):
            column = 9 * half + c
            own_ref[g, ib, column] = jnp.where(
                second, wide_ref[tile, 1, column, upper, :], wide_ref[tile, 1, column, lower, :]
            )
        return carry

    lax.fori_loop(0, 6, one_group, 0)

    @pl.when(ib == pl.num_programs(0) - 1)
    def _():
        def one_pair(step, carry):
            k, e = step // 5, step % 5
            for c in range(6):
                near, far = [None] * 6, [None] * 6
                for block in range(TILE // 16):
                    for g in range(3):
                        x = own_ref[g, block, 6 * k + c]
                        for d in range(6):
                            term = x * ap_ref[g, block, 6 * e + d]
                            sums = far if g == 2 else near
                            sums[d] = term if sums[d] is None else sums[d] + term
                for d in range(6):
                    row = slice(6 * c + d, 6 * c + d + 1)
                    tail = jnp.sum(far[d], 0, keepdims=True)
                    term_ref[step, row, 0:128] = jnp.sum(near[d], 0, keepdims=True)
                    term_ref[step, row, 128:ROWS] = tail[:, :TILE] + tail[:, TILE:]
            return carry

        lax.fori_loop(0, 15, one_pair, 0)
        r = Order(order_l_ref, order_s_ref)
        owner, rank, after = (x[:, :ROWS] for x in (r.owner_l, r.rank_l, r.after_l))
        member, slot = slot_grid(ROWS)
        mine, row_slot = owner == member, slot < 6.0
        here = ones_where(mine & (rank == slot))
        back_to = member + jnp.where(me == 0, 1.0, 0.0)
        on_to = member - jnp.where(me == MEMBERS - 1, 1.0, 0.0)
        back = (mine & row_slot & (rank == slot + 1.0)) | ((slot == 6.0) & (owner == back_to) & (rank == 0.0))
        on = (mine & row_slot & (rank == slot - 1.0) & (after > 0.0)) | (
            (slot == 7.0) & (owner == on_to) & (after == 0.0)
        )
        picks = [ones_where(back), here, ones_where(on)]
        terms = []
        for k in range(3):
            pieces = [term_ref[5 * k + e][:36, :ROWS] for e in range(5)]
            pieces.append(jnp.zeros((4 + 36 * k, ROWS), F32))
            if k < 2:
                pieces.insert(0, jnp.zeros((72 - 36 * k, ROWS), F32))
            terms.append(jnp.concatenate(pieces, 0))
        total = None
        for k in range(3):
            prod = exact_dot(picks[k], terms[k], NT, True)
            total = prod if total is None else total + prod
        high = total.astype(BF16).astype(F32)
        rest = dot((total - high).astype(BF16), spare_lanes(0))
        out_ref[...] = (high + rest).astype(BF16)
        head, tail = far_pick(r, me, ROWS)
        far_out[...] = exact_dot(head, terms[0], NT, True) + exact_dot(tail, terms[2], NT, True)


def unpack_smooth_kernel(recv_ref, out_ref, pick_out):
    size = MEMBERS * SLOTS
    count = jnp.broadcast_to(recv_ref[:, 54:55, :].astype(F32), (MEMBERS, SLOTS, 128)).reshape(size, 128)
    source, other = iota((size, size), 0) // SLOTS, iota((size, size), 1) // SLOTS
    first_slot = iota((size, size), 1) % SLOTS == 0
    earlier = ones_where((other < source) & first_slot)
    start = dot(earlier, count.astype(BF16))[:, :1]
    count = count[:, :1]
    slot = (iota((size, 1), 0) % SLOTS).astype(F32)
    place = jnp.where(slot < count, start + slot, -1.0)
    column = iota((size, ROWS), 1).astype(F32)
    pick = ones_where(place == column)
    for block in range(COLS // 128):
        rows = recv_ref[:, 6 * block : 6 * block + 6, :].astype(F32)
        rows = jnp.concatenate([rows, jnp.zeros((MEMBERS, 2, 128), F32)], 1).reshape(size, 128)
        value = lax.dot_general(rows.astype(BF16), pick, TN, preferred_element_type=F32)
        out_ref[128 * block : 128 * (block + 1), :] = value.astype(BF16)
    place = jnp.where(slot == 6.0, jnp.where(start == 0.0, ROWS - 1.0, start - 1.0), place)
    stop = start + count
    place = jnp.where(slot == 7.0, jnp.where(stop == float(ROWS), 0.0, stop), place)
    column = iota((size, WIDE), 1).astype(F32)
    pick_out[...] = jnp.where(place == column, 1.0, 0.0).T[:ROWS].astype(BF16)


def unpack_coarse_kernel(me_ref, pick_ref, sums_ref, far_ref, out_ref):
    me = me_ref[0]
    total = dot(pick_ref[...], sums_ref[...])
    total = total + dot(total.astype(BF16), spare_lanes(1))
    row = iota((ROWS, WIDE), 0)
    edge = jnp.where(me == 0, 0, ROWS - 1)
    far = jnp.broadcast_to(far_ref[0:1, :], (ROWS, WIDE))
    total = total + jnp.where(row == edge, far, 0.0)
    out_ref[...] = total[:, :252]


def call(kernel, outs, args, grid=None, in_specs=None, scratch=(), flops=0, mib=16, name=None):
    whole = lambda shape: pl.BlockSpec(shape, lambda *_: (0,) * len(shape))
    specs = []
    for n, arg in enumerate(args):
        spec = None if in_specs is None else in_specs.get(n)
        if spec is None:
            spec = pl.BlockSpec(memory_space=pltpu.SMEM) if arg.shape == (1,) else whole(arg.shape)
        specs.append(spec)
    moved = sum(a.size * a.dtype.itemsize for a in args) + sum(o.size * o.dtype.itemsize for o in outs)
    return pl.pallas_call(
        kernel,
        grid=(1,) if grid is None else grid,
        in_specs=specs,
        out_specs=[whole(o.shape) for o in outs],
        out_shape=outs,
        scratch_shapes=list(scratch),
        compiler_params=pltpu.CompilerParams(vmem_limit_bytes=mib * MIB),
        cost_estimate=pl.CostEstimate(flops=flops, bytes_accessed=moved, transcendentals=0),
        name=name,
    )(*args)


def shaped(shape, dtype=BF16):
    return jax.ShapeDtypeStruct(shape, dtype)


def swaps(groups):
    ring, axes = MEMBERS, range(groups)
    both = lambda pairs: [q for a, b in pairs for q in ((a, b), (b, a))]
    across = both([(g * ring - 1, g * ring) for g in range(1, groups)])
    away = both([(g * ring + i, g * ring + (i + 1) % ring) for g in axes for i in range(1, ring, 2)])
    near = both([(g * ring + i, g * ring + i + 1) for g in axes for i in range(0, ring, 2)])
    return across, away, near


def per_device(a_band, p_tent, new_owner):
    axes = ("group", "member")
    across, away_pairs, near_pairs = swaps(lax.axis_size("group"))
    me = lax.axis_index("member").astype(jnp.int32).reshape(1)
    a = a_band.transpose(1, 2, 3, 0)
    p = p_tent.transpose(1, 2, 0).reshape(MODES * TILE, ROWS)
    a_spec = pl.BlockSpec(memory_space=pltpu.HBM)
    grid = (TILE // 16,)

    def a_scratch(planes):
        return [
            pltpu.VMEM((planes, TILE, TILE, ROWS), BF16),
            pltpu.SemaphoreType.DMA((planes, TILE // 16)),
            pltpu.VMEM((3, planes, 8, TILE, 128), F32),
        ]

    def exchanged(far, away, near):
        far = lax.ppermute(far, axes, across)
        away = lax.ppermute(away, axes, away_pairs)
        return far, away, lax.ppermute(near, axes, near_pairs)

    def rims(length):
        return [shaped((8, length)), shaped((length // 2, 128)), shaped((length // 2, 128))]

    order_l, order_s, p, *sent = call(
        first_kernel,
        [shaped((8, WIDE), F32), shaped((ROWS, 128), F32), shaped(p.shape)] + rims(MODES * TILE),
        (me, new_owner.reshape(1, ROWS), p),
        name="rims",
    )
    got = exchanged(*sent)
    parts = call(
        middle_kernel,
        [shaped((18, TILE, ROWS)), shaped((TILE, TILE, 128)), shaped((TILE, 128), F32)],
        (order_l, order_s, a, p),
        grid=grid,
        in_specs={2: a_spec},
        scratch=[
            *a_scratch(3),
            pltpu.VMEM((2, 3, MODES, TILE, 128), F32),
            pltpu.VMEM((3, 19, 8, 128), F32),
            pltpu.VMEM((TILE, ROWS), F32),
        ],
        flops=10**9,
        mib=50,
        name="middle",
    )
    s, *sent = call(
        smooth_kernel,
        [shaped((18, TILE, ROWS))] + rims(COLS),
        (me, order_l, order_s, *parts, *got),
        scratch=[
            pltpu.VMEM((1, 1, 8, TILE, 128), F32),
            pltpu.VMEM((1, 1, MODES, TILE, 128), F32),
            pltpu.VMEM((MODES, TILE, 128), F32),
        ],
        flops=10**9,
        mib=24,
        name="smooth",
    )
    got = exchanged(*sent)
    s = s.reshape(COLS, ROWS)
    (packed,) = call(pack_kernel, [shaped((MEMBERS, PACKED, 128))], (order_l, s), name="pack")
    packed, *got = lax.optimization_barrier((packed, *got))
    recv = lax.all_to_all(packed, "member", split_axis=0, concat_axis=0, tiled=True)

    sums, far = call(
        product_kernel,
        [shaped((MEMBERS * SLOTS, WIDE)), shaped((8, WIDE), F32)],
        (me, order_l, order_s, a, s, *got),
        grid=grid,
        in_specs={3: a_spec},
        scratch=[
            *a_scratch(3),
            pltpu.VMEM((2, 3, 18, TILE, 128), F32),
            pltpu.VMEM((3, TILE // 16, 30, 8, 128), F32),
            pltpu.VMEM((3, TILE // 16, 18, 8, 128), F32),
            pltpu.VMEM((15, 40, WIDE), F32),
        ],
        flops=10**10,
        mib=50,
        name="product",
    )
    far = lax.ppermute(far, axes, across)
    sums = lax.all_to_all(
        sums.reshape(MEMBERS, SLOTS, WIDE), "member", split_axis=0, concat_axis=0, tiled=True
    ).reshape(MEMBERS * SLOTS, WIDE)
    smooth, pick = call(
        unpack_smooth_kernel,
        [shaped((COLS, ROWS)), shaped((ROWS, MEMBERS * SLOTS))],
        (recv,),
        flops=10**9,
        name="unpack_smooth",
    )
    (coarse,) = call(
        unpack_coarse_kernel, [shaped((ROWS, 252), F32)], (me, pick, sums, far), name="unpack_coarse"
    )
    return smooth.reshape(3, MODES, TILE, ROWS).transpose(3, 0, 1, 2), coarse


def solution(mesh):
    in_specs = (
        P(("group", "member"), None, None, None),
        P(("group", "member"), None, None),
        P(("group", "member")),
    )
    out_specs = (P(("group", "member"), None, None, None), P(("group", "member"), None))
    return jax.shard_map(
        per_device, mesh=mesh, in_specs=in_specs, out_specs=out_specs, check_vma=False
    )
```

```python
import jax
import jax.numpy as jnp
from jax import lax
from jax.experimental import pallas as pl
from jax.experimental.pallas import tpu as pltpu
from jax.sharding import PartitionSpec as P

ROWS = 192
WIDE = 256
TILE = 64
MODES = 6
MEMBERS = 64
SLOTS = 8
COLS = 3 * MODES * TILE
F32 = jnp.float32
BF16 = jnp.bfloat16
NT = (((1,), (1,)), ((), ()))
TN = (((0,), (0,)), ((), ()))
MIB = 1024 * 1024
BACK = 3328
PACKED = 56


def iota(shape, axis):
    return lax.broadcasted_iota(jnp.int32, shape, axis)


def ones_where(mask):
    return jnp.where(mask, 1.0, 0.0).astype(BF16)


def dot(a, b):
    return jnp.dot(a, b, preferred_element_type=F32)


def parts_of(x):
    high = x.astype(BF16)
    rest = x - high.astype(F32)
    mid = rest.astype(BF16)
    low = (rest - mid.astype(F32)).astype(BF16)
    return high, mid, low


def exact_dot(pick, x, dims, pick_first):
    total = None
    for part in parts_of(x):
        ab = (pick, part) if pick_first else (part, pick)
        prod = lax.dot_general(*ab, dims, preferred_element_type=F32)
        total = prod if total is None else total + prod
    return total


def rank_arrays(owner_row):
    owner_row = owner_row.astype(F32)
    owner_row = jnp.concatenate([owner_row, owner_row[:, 128:]], 1)
    wide = jnp.broadcast_to(owner_row, (WIDE, WIDE))
    tall = wide.T[:ROWS]
    wide = wide[:ROWS]
    lane = iota((ROWS, WIDE), 1)
    row_l = jnp.where(lane < ROWS, lane, lane - TILE)
    row_s = iota((ROWS, WIDE), 0)
    one = jnp.where(wide == tall, 1.0, 0.0)
    less, more = row_s < row_l, row_s > row_l
    rank_l = jnp.sum(jnp.where(less, one, 0.0), 0, keepdims=True)
    after_l = jnp.sum(jnp.where(more, one, 0.0), 0, keepdims=True)
    once = jnp.where(lane < ROWS, one, 0.0)
    rank_s = jnp.sum(jnp.where(more, once, 0.0), 1, keepdims=True)
    after_s = jnp.sum(jnp.where(less, once, 0.0), 1, keepdims=True)
    return (wide[:1], rank_l, after_l), (tall[:, :1], rank_s, after_s)


class Order:
    def __init__(self, wide_ref, tall_ref):
        self.owner_l, self.rank_l, self.after_l = (wide_ref[n : n + 1, :] for n in range(3))
        self.owner_s, self.rank_s, self.after_s = (tall_ref[:, n : n + 1] for n in range(3))


def rim_picks(r, me):
    lane = iota((ROWS, 128), 1)
    first, last = r.rank_s == 0.0, r.after_s == 0.0
    even = me % 2 == 0
    picks = []
    for half in (0, 1):
        slot = lane - TILE * half
        inside = (slot >= 0) & (slot < TILE)
        to_left = jnp.where(inside, slot + jnp.where(me == 0, 1, 0), -1).astype(F32)
        to_right = jnp.where(inside, slot - jnp.where(me == MEMBERS - 1, 1, 0), -1).astype(F32)
        left = jnp.where((r.owner_s == to_left) & first, 1.0, 0.0)
        right = jnp.where((r.owner_s == to_right) & last, 1.0, 0.0)
        near = jnp.where(even, right, left).astype(BF16)
        far = jnp.where(even, left, right).astype(BF16)
        picks.append((near, far))
    return picks


def far_pick(r, me, width):
    top = iota((8, width), 0) == 0
    owner, rank, after = r.owner_l[:, :width], r.rank_l[:, :width], r.after_l[:, :width]
    head = top & (me == 0) & (owner == 0.0) & (rank == 0.0)
    tail = top & (me == MEMBERS - 1) & (owner == MEMBERS - 1.0) & (after == 0.0)
    return ones_where(head), ones_where(tail)


def rims_of(rows, r, me):
    half = rows.shape[0] // 2
    top, bottom = rim_picks(r, me)
    rims = [(dot(rows[:half], a) + dot(rows[half:], b)).astype(BF16) for a, b in zip(top, bottom)]
    head, tail = far_pick(r, me, ROWS)
    far = lax.dot_general(head + tail, rows, NT, preferred_element_type=F32).astype(BF16)
    return [far] + rims[::-1]


def local_rows(rows, r):
    lane = iota((ROWS, WIDE), 1)
    row_l = jnp.where(lane < ROWS, lane, lane - TILE)
    same = r.owner_l == r.owner_s
    before = ones_where(same & (r.rank_s + 1.0 == r.rank_l))
    after = ones_where(same & (r.rank_s == r.rank_l + 1.0))
    here = ones_where(iota((ROWS, WIDE), 0) == row_l)
    return [dot(rows, pick) for pick in (before, here, after)]


def rim_rows(near, away, far, r, me):
    bucket = iota((128, WIDE), 0)
    even = me % 2 == 0
    result = []
    for rim, edge, end in zip(
        (jnp.where(even, away, near), jnp.where(even, near, away)), (r.rank_l, r.after_l), far_pick(r, me, WIDE)
    ):
        ends = []
        for side in (0, 1):
            want = bucket - TILE * side
            want = jnp.where((want >= 0) & (want < TILE), want, -1).astype(F32)
            ends.append(dot(rim, ones_where((want == r.owner_l) & (edge == 0.0))))
        result.append(jnp.concatenate(ends, 0) + lax.dot_general(far, end, TN, preferred_element_type=F32))
    return result


def set_wide(ref, k, value):
    for tile in (0, 1):
        part = value[:, 128 * tile : 128 * (tile + 1)]
        ref[tile, k] = part.reshape(-1, TILE, 128)


def chunk_copies(a_hbm, a_ref, sems, planes, n):
    rows = pl.ds(16 * n, 16)
    return [
        pltpu.make_async_copy(a_hbm.at[k, rows], a_ref.at[at, rows], sems.at[at, n])
        for at, k in enumerate(planes)
    ]


def start_copies(a_hbm, a_ref, sems, planes):
    for n in range(TILE // 16):
        for copy in chunk_copies(a_hbm, a_ref, sems, planes, n):
            copy.start()


def next_groups(a_hbm, a_ref, sems, planes, ib, group_ref):
    for copy in chunk_copies(a_hbm, a_ref, sems, planes, ib):
        copy.wait()
    for k in range(len(planes)):
        for i in range(8):
            low, high = (a_ref[k, 16 * ib + i + n].astype(F32) for n in (0, 8))
            group_ref[0, k, i] = low[:, :128]
            group_ref[1, k, i] = high[:, :128]
            group_ref[2, k, i] = jnp.concatenate([low[:, 128:], high[:, 128:]], 1)


def folded(terms):
    sub = iota((8, 128), 0)
    for shift in (1, 2, 4):
        keep = (sub & shift) == 0
        terms = [
            jnp.where(keep, x, y) + pltpu.roll(jnp.where(keep, y, x), shift, 0)
            for x, y in zip(terms[::2], terms[1::2])
        ]
    return terms[0]


def contracted(group_ref, wide_ref, g, tile, pairs, columns):
    totals = [[None] * 8 for _ in columns]
    for jb in range(TILE // 8):
        j = pl.ds(8 * jb, 8)
        for k, base in pairs:
            a = [group_ref[g, k, i, j, :] for i in range(8)]
            for n, column in enumerate(columns):
                x = wide_ref[tile, k, base + column, j, :]
                for i in range(8):
                    term = a[i] * x
                    totals[n][i] = term if totals[n][i] is None else totals[n][i] + term
    return [folded(t) for t in totals]


def ungrouped(out_ref, index):
    low, high, both = out_ref[0, index], out_ref[1, index], out_ref[2, index]
    top = jnp.concatenate([low, both[:, :TILE]], 1)
    bottom = jnp.concatenate([high, both[:, TILE:]], 1)
    return jnp.concatenate([top, bottom], 0)


def first_kernel(me_ref, owner_ref, p_ref, wide_ref, tall_ref, p_out, back_out, far_out, away_out, near_out):
    rows, columns = rank_arrays(owner_ref[...])
    p_out[...] = p_ref[...]
    wide_ref[...] = jnp.zeros_like(wide_ref)
    for n in range(3):
        wide_ref[n : n + 1, :] = rows[n]
    lane = iota((ROWS, 128), 1)
    tall_ref[...] = jnp.where(lane == 0, columns[0], jnp.where(lane == 1, columns[1], columns[2]))
    r = Order(wide_ref, tall_ref)
    for ref, rim in zip((far_out, away_out, near_out), rims_of(p_ref[...], r, me_ref[0])):
        ref[...] = rim
    back_out[...] = jnp.zeros_like(back_out)
    back_out[:, : MODES * TILE] = far_out[...]


def halves(ib):
    return pl.ds(pl.multiple_of(16 * ib, 8), 8), pl.ds(pl.multiple_of(16 * ib + 8, 8), 8)


def middle_kernel(
    order_l_ref, order_s_ref, a_hbm, p_ref, mid_ref, scale_ref, local_ref,
    a_ref, sems, group_ref, wide_ref, out_ref,
):
    ib = pl.program_id(0)

    @pl.when(ib == 0)
    def _():
        start_copies(a_hbm, a_ref, sems, (1,))
        before, here, after = local_rows(p_ref[...], Order(order_l_ref, order_s_ref))
        set_wide(wide_ref, 0, here)
        set_wide(local_ref, 0, before)
        set_wide(local_ref, 1, after)

    next_groups(a_hbm, a_ref, sems, (1,), ib, group_ref)
    sub, lane = iota((8, 128), 0), iota((8, 128), 1)
    lower, upper = halves(ib)

    def one_group(g, carry):
        tile = jnp.where(g == 2, 1, 0)
        second = (g == 1) | ((g == 2) & (lane >= TILE))
        diag = jnp.zeros((8, 128), F32)
        for i in range(8):
            entry = jnp.where(second, group_ref[g, 0, i, upper, :], group_ref[g, 0, i, lower, :])
            diag = jnp.where(sub == i, entry, diag)
        scale = 0.6 * (1.0 / diag)
        scale_ref[ib, g] = scale
        for half in (0, 1):
            columns = [3 * half + c for c in range(3)]
            sums = contracted(group_ref, wide_ref, g, tile, [(0, 0)], columns)
            for c, total in zip(columns, sums):
                own = jnp.where(second, wide_ref[tile, 0, c, upper, :], wide_ref[tile, 0, c, lower, :])
                out_ref[g, c] = own - scale * total
        return carry

    lax.fori_loop(0, 3, one_group, 0)
    rows = pl.ds(pl.multiple_of(16 * ib, 16), 16)
    for index in range(6):
        mid_ref[index, rows, :] = ungrouped(out_ref, index).astype(BF16)


def smooth_kernel(
    me_ref, order_l_ref, order_s_ref, a_hbm, mid_ref, scale_ref, local_ref, on_ref, away_ref, near_ref, back_ref,
    s_ref, far_out, away_out, near_out, a_ref, sems, group_ref, wide_ref, out_ref,
):
    ib = pl.program_id(0)
    me = me_ref[0]

    @pl.when(ib == 0)
    def _():
        start_copies(a_hbm, a_ref, sems, (0, 2))
        r = Order(order_l_ref, order_s_ref)
        for k, value in enumerate(rim_rows(near_ref[...], away_ref[...], on_ref[...] + back_ref[:, : MODES * TILE], r, me)):
            set_wide(wide_ref, k, value)
        wide_ref[...] += local_ref[...]
        s_ref[6:12] = mid_ref[...]

    next_groups(a_hbm, a_ref, sems, (0, 2), ib, group_ref)

    def one_group(g, carry):
        tile = jnp.where(g == 2, 1, 0)
        scale = 0.0 - scale_ref[ib, g]
        for k in range(2):
            for half in (0, 1):
                columns = [3 * half + c for c in range(3)]
                sums = contracted(group_ref, wide_ref, g, tile, [(k, 0)], columns)
                for c, total in zip(columns, sums):
                    out_ref[g, 6 * k + c] = scale * total
        return carry

    lax.fori_loop(0, 3, one_group, 0)
    rows = pl.ds(pl.multiple_of(16 * ib, 16), 16)
    for index in range(12):
        s_ref[index if index < 6 else index + 6, rows, :] = ungrouped(out_ref, index).astype(BF16)

    @pl.when(ib == pl.num_programs(0) - 1)
    def _():
        r = Order(order_l_ref, order_s_ref)
        flat = s_ref[...].reshape(COLS, ROWS)
        for ref, rim in zip((far_out, away_out, near_out), rims_of(flat, r, me)):
            ref[...] = rim


def slot_grid(width):
    spot = iota((MEMBERS * SLOTS, width), 0)
    return (spot // SLOTS).astype(F32), (spot % SLOTS).astype(F32)


def pack_kernel(order_l_ref, s_ref, out_ref):
    member, slot = slot_grid(ROWS)
    owner, rank = order_l_ref[0:1, :ROWS], order_l_ref[1:2, :ROWS]
    mine = owner == member
    pick = ones_where(mine & (rank == slot))
    count = jnp.sum(jnp.where(mine, 1.0, 0.0), 1, keepdims=True)
    for block in range(COLS // 128):
        value = lax.dot_general(
            pick, s_ref[128 * block : 128 * (block + 1), :], NT, preferred_element_type=F32
        ).reshape(MEMBERS, SLOTS, 128)
        out_ref[:, 6 * block : 6 * block + 6, :] = value[:, :6, :].astype(BF16)
    counts = jnp.broadcast_to(count, (MEMBERS * SLOTS, 128)).reshape(MEMBERS, SLOTS, 128)
    out_ref[:, 54:56, :] = counts[:, :2, :].astype(BF16)


OFFSETS = [[(k, 6 * (e - k)) for k in range(3) if 0 <= e - k <= 2] for e in range(5)]


def spare_lanes(axis):
    entry, spare = iota((WIDE, WIDE), axis), iota((WIDE, WIDE), 1 - axis) - 252
    return ones_where((spare >= 0) & (entry == 108 + 7 * spare))


def product_kernel(
    me_ref, order_l_ref, order_s_ref, a_hbm, s_ref, far_ref, away_ref, near_ref,
    out_ref, far_out, a_ref, sems, group_ref, wide_ref, ap_ref, own_ref, term_ref,
):
    ib = pl.program_id(0)
    me = me_ref[0]

    @pl.when(ib == 0)
    def _():
        start_copies(a_hbm, a_ref, sems, (0, 1, 2))
        r = Order(order_l_ref, order_s_ref)
        before, here, after = local_rows(s_ref[...], r)
        left, right = rim_rows(near_ref[...], away_ref[...], far_ref[...], r, me)
        for k, value in enumerate((before + left, here, after + right)):
            set_wide(wide_ref, k, value)
        term_ref[...] = jnp.zeros_like(term_ref)

    next_groups(a_hbm, a_ref, sems, (0, 1, 2), ib, group_ref)
    lane = iota((8, 128), 1)

    def one_group(step, carry):
        g, half = step // 2, step % 2
        tile = jnp.where(g == 2, 1, 0)
        for e in range(5):
            columns = [3 * half + c for c in range(3)]
            sums = contracted(group_ref, wide_ref, g, tile, OFFSETS[e], columns)
            for c, total in zip(columns, sums):
                ap_ref[g, ib, 6 * e + c] = total.astype(BF16).astype(F32)
        second = (g == 1) | ((g == 2) & (lane >= TILE))
        lower, upper = pl.ds(pl.multiple_of(16 * ib, 8), 8), pl.ds(pl.multiple_of(16 * ib + 8, 8), 8)
        for c in range(9):
            column = 9 * half + c
            own_ref[g, ib, column] = jnp.where(
                second, wide_ref[tile, 1, column, upper, :], wide_ref[tile, 1, column, lower, :]
            )
        return carry

    lax.fori_loop(0, 6, one_group, 0)

    @pl.when(ib == pl.num_programs(0) - 1)
    def _():
        def one_pair(step, carry):
            k, e = step // 5, step % 5
            for c in range(6):
                near, far = [None] * 6, [None] * 6
                for block in range(TILE // 16):
                    for g in range(3):
                        x = own_ref[g, block, 6 * k + c]
                        for d in range(6):
                            term = x * ap_ref[g, block, 6 * e + d]
                            sums = far if g == 2 else near
                            sums[d] = term if sums[d] is None else sums[d] + term
                for d in range(6):
                    row = slice(6 * c + d, 6 * c + d + 1)
                    tail = jnp.sum(far[d], 0, keepdims=True)
                    term_ref[step, row, 0:128] = jnp.sum(near[d], 0, keepdims=True)
                    term_ref[step, row, 128:ROWS] = tail[:, :TILE] + tail[:, TILE:]
            return carry

        lax.fori_loop(0, 15, one_pair, 0)
        r = Order(order_l_ref, order_s_ref)
        owner, rank, after = (x[:, :ROWS] for x in (r.owner_l, r.rank_l, r.after_l))
        member, slot = slot_grid(ROWS)
        mine, row_slot = owner == member, slot < 6.0
        here = ones_where(mine & (rank == slot))
        back_to = member + jnp.where(me == 0, 1.0, 0.0)
        on_to = member - jnp.where(me == MEMBERS - 1, 1.0, 0.0)
        back = (mine & row_slot & (rank == slot + 1.0)) | ((slot == 6.0) & (owner == back_to) & (rank == 0.0))
        on = (mine & row_slot & (rank == slot - 1.0) & (after > 0.0)) | (
            (slot == 7.0) & (owner == on_to) & (after == 0.0)
        )
        picks = [ones_where(back), here, ones_where(on)]
        terms = []
        for k in range(3):
            pieces = [term_ref[5 * k + e][:36, :ROWS] for e in range(5)]
            pieces.append(jnp.zeros((4 + 36 * k, ROWS), F32))
            if k < 2:
                pieces.insert(0, jnp.zeros((72 - 36 * k, ROWS), F32))
            terms.append(jnp.concatenate(pieces, 0))
        total = None
        for k in range(3):
            prod = exact_dot(picks[k], terms[k], NT, True)
            total = prod if total is None else total + prod
        high = total.astype(BF16).astype(F32)
        rest = dot((total - high).astype(BF16), spare_lanes(0))
        out_ref[...] = (high + rest).astype(BF16)
        head, tail = far_pick(r, me, ROWS)
        far_out[...] = exact_dot(head, terms[0], NT, True) + exact_dot(tail, terms[2], NT, True)


def unpack_smooth_kernel(recv_ref, out_ref, pick_out):
    size = MEMBERS * SLOTS
    count = jnp.broadcast_to(recv_ref[:, 54:55, :].astype(F32), (MEMBERS, SLOTS, 128)).reshape(size, 128)
    source, other = iota((size, size), 0) // SLOTS, iota((size, size), 1) // SLOTS
    first_slot = iota((size, size), 1) % SLOTS == 0
    earlier = ones_where((other < source) & first_slot)
    start = dot(earlier, count.astype(BF16))[:, :1]
    count = count[:, :1]
    slot = (iota((size, 1), 0) % SLOTS).astype(F32)
    place = jnp.where(slot < count, start + slot, -1.0)
    column = iota((size, ROWS), 1).astype(F32)
    pick = ones_where(place == column)
    for block in range(COLS // 128):
        rows = recv_ref[:, 6 * block : 6 * block + 6, :].astype(F32)
        rows = jnp.concatenate([rows, jnp.zeros((MEMBERS, 2, 128), F32)], 1).reshape(size, 128)
        value = lax.dot_general(rows.astype(BF16), pick, TN, preferred_element_type=F32)
        out_ref[128 * block : 128 * (block + 1), :] = value.astype(BF16)
    place = jnp.where(slot == 6.0, jnp.where(start == 0.0, ROWS - 1.0, start - 1.0), place)
    stop = start + count
    place = jnp.where(slot == 7.0, jnp.where(stop == float(ROWS), 0.0, stop), place)
    column = iota((size, WIDE), 1).astype(F32)
    pick_out[...] = jnp.where(place == column, 1.0, 0.0).T[:ROWS].astype(BF16)


def unpack_coarse_kernel(me_ref, pick_ref, sums_ref, far_ref, out_ref):
    me = me_ref[0]
    total = dot(pick_ref[...], sums_ref[...])
    total = total + dot(total.astype(BF16), spare_lanes(1))
    row = iota((ROWS, WIDE), 0)
    edge = jnp.where(me == 0, 0, ROWS - 1)
    far = jnp.broadcast_to(far_ref[0:1, :], (ROWS, WIDE))
    total = total + jnp.where(row == edge, far, 0.0)
    out_ref[...] = total[:, :252]


def call(kernel, outs, args, grid=None, in_specs=None, scratch=(), flops=0, mib=16, name=None):
    whole = lambda shape: pl.BlockSpec(shape, lambda *_: (0,) * len(shape))
    specs = []
    for n, arg in enumerate(args):
        spec = None if in_specs is None else in_specs.get(n)
        if spec is None:
            spec = pl.BlockSpec(memory_space=pltpu.SMEM) if arg.shape == (1,) else whole(arg.shape)
        specs.append(spec)
    moved = sum(a.size * a.dtype.itemsize for a in args) + sum(o.size * o.dtype.itemsize for o in outs)
    return pl.pallas_call(
        kernel,
        grid=(1,) if grid is None else grid,
        in_specs=specs,
        out_specs=[whole(o.shape) for o in outs],
        out_shape=outs,
        scratch_shapes=list(scratch),
        compiler_params=pltpu.CompilerParams(vmem_limit_bytes=mib * MIB),
        cost_estimate=pl.CostEstimate(flops=flops, bytes_accessed=moved, transcendentals=0),
        name=name,
    )(*args)


def shaped(shape, dtype=BF16):
    return jax.ShapeDtypeStruct(shape, dtype)


def swaps(groups):
    ring, axes = MEMBERS, range(groups)
    both = lambda pairs: [q for a, b in pairs for q in ((a, b), (b, a))]
    across = both([(g * ring - 1, g * ring) for g in range(1, groups)])
    away = both([(g * ring + i, g * ring + (i + 1) % ring) for g in axes for i in range(1, ring, 2)])
    near = both([(g * ring + i, g * ring + i + 1) for g in axes for i in range(0, ring, 2)])
    return across, away, near


def per_device(a_band, p_tent, new_owner):
    axes = ("group", "member")
    across, away_pairs, near_pairs = swaps(lax.axis_size("group"))
    me = lax.axis_index("member").astype(jnp.int32).reshape(1)
    a = a_band.transpose(1, 2, 3, 0)
    p = p_tent.transpose(1, 2, 0).reshape(MODES * TILE, ROWS)
    a_spec = pl.BlockSpec(memory_space=pltpu.HBM)
    grid = (TILE // 16,)

    def a_scratch(planes):
        return [
            pltpu.VMEM((planes, TILE, TILE, ROWS), BF16),
            pltpu.SemaphoreType.DMA((planes, TILE // 16)),
            pltpu.VMEM((3, planes, 8, TILE, 128), F32),
        ]

    def exchanged(far, away, near):
        far = lax.ppermute(far, axes, across)
        away = lax.ppermute(away, axes, away_pairs)
        return far, away, lax.ppermute(near, axes, near_pairs)

    def rims(length):
        return [shaped((8, length)), shaped((length // 2, 128)), shaped((length // 2, 128))]

    order_l, order_s, p, back, *sent = call(
        first_kernel,
        [shaped((8, WIDE), F32), shaped((ROWS, 128), F32), shaped(p.shape), shaped((8, BACK))] + rims(MODES * TILE),
        (me, new_owner.reshape(1, ROWS), p),
        name="rims",
    )
    far, away, near = sent
    on = lax.ppermute(far, axes, across[::2])
    away = lax.ppermute(away, axes, away_pairs)
    near = lax.ppermute(near, axes, near_pairs)
    back = lax.ppermute(back, axes, across[1::2])
    got = on, away, near, back
    local = shaped((2, 2, MODES, TILE, 128), F32)
    parts = call(
        middle_kernel,
        [shaped((MODES, TILE, ROWS)), shaped((TILE // 16, 3, 8, 128), F32), local],
        (order_l, order_s, a, p),
        grid=grid,
        in_specs={2: a_spec},
        scratch=[
            *a_scratch(1),
            pltpu.VMEM((2, 1, MODES, TILE, 128), F32),
            pltpu.VMEM((3, MODES, 8, 128), F32),
        ],
        flops=10**9,
        mib=50,
        name="middle",
    )
    s, *sent = call(
        smooth_kernel,
        [shaped((18, TILE, ROWS))] + rims(COLS),
        (me, order_l, order_s, a, *parts, *got),
        grid=grid,
        in_specs={3: a_spec},
        scratch=[*a_scratch(2), pltpu.VMEM(local.shape, F32), pltpu.VMEM((3, 12, 8, 128), F32)],
        flops=10**9,
        mib=50,
        name="smooth",
    )
    got = exchanged(*sent)
    s = s.reshape(COLS, ROWS)
    (packed,) = call(pack_kernel, [shaped((MEMBERS, PACKED, 128))], (order_l, s), name="pack")
    packed, *got = lax.optimization_barrier((packed, *got))
    recv = lax.all_to_all(packed, "member", split_axis=0, concat_axis=0, tiled=True)

    sums, far = call(
        product_kernel,
        [shaped((MEMBERS * SLOTS, WIDE)), shaped((8, WIDE), F32)],
        (me, order_l, order_s, a, s, *got),
        grid=grid,
        in_specs={3: a_spec},
        scratch=[
            *a_scratch(3),
            pltpu.VMEM((2, 3, 18, TILE, 128), F32),
            pltpu.VMEM((3, TILE // 16, 30, 8, 128), F32),
            pltpu.VMEM((3, TILE // 16, 18, 8, 128), F32),
            pltpu.VMEM((15, 40, WIDE), F32),
        ],
        flops=10**10,
        mib=50,
        name="product",
    )
    far = lax.ppermute(far, axes, across)
    sums = lax.all_to_all(
        sums.reshape(MEMBERS, SLOTS, WIDE), "member", split_axis=0, concat_axis=0, tiled=True
    ).reshape(MEMBERS * SLOTS, WIDE)
    smooth, pick = call(
        unpack_smooth_kernel,
        [shaped((COLS, ROWS)), shaped((ROWS, MEMBERS * SLOTS))],
        (recv,),
        flops=10**9,
        name="unpack_smooth",
    )
    (coarse,) = call(
        unpack_coarse_kernel, [shaped((ROWS, 252), F32)], (me, pick, sums, far), name="unpack_coarse"
    )
    return smooth.reshape(3, MODES, TILE, ROWS).transpose(3, 0, 1, 2), coarse


def solution(mesh):
    in_specs = (
        P(("group", "member"), None, None, None),
        P(("group", "member"), None, None),
        P(("group", "member")),
    )
    out_specs = (P(("group", "member"), None, None, None), P(("group", "member"), None))
    return jax.shard_map(
        per_device, mesh=mesh, in_specs=in_specs, out_specs=out_specs, check_vma=False
    )
```

```python
import jax
import jax.numpy as jnp
from jax import lax
from jax.experimental import pallas as pl
from jax.experimental.pallas import tpu as pltpu
from jax.sharding import PartitionSpec as P

ROWS = 192
WIDE = 256
TILE = 64
MODES = 6
MEMBERS = 64
SLOTS = 8
COLS = 3 * MODES * TILE
F32 = jnp.float32
BF16 = jnp.bfloat16
NT = (((1,), (1,)), ((), ()))
TN = (((0,), (0,)), ((), ()))
MIB = 1024 * 1024
BACK = 3328
PACKED = 56


def iota(shape, axis):
    return lax.broadcasted_iota(jnp.int32, shape, axis)


def ones_where(mask):
    return jnp.where(mask, 1.0, 0.0).astype(BF16)


def dot(a, b):
    return jnp.dot(a, b, preferred_element_type=F32)


def parts_of(x):
    high = x.astype(BF16)
    rest = x - high.astype(F32)
    mid = rest.astype(BF16)
    low = (rest - mid.astype(F32)).astype(BF16)
    return high, mid, low


def exact_dot(pick, x, dims, pick_first):
    total = None
    for part in parts_of(x):
        ab = (pick, part) if pick_first else (part, pick)
        prod = lax.dot_general(*ab, dims, preferred_element_type=F32)
        total = prod if total is None else total + prod
    return total


def rank_arrays(owner_row):
    owner_row = owner_row.astype(F32)
    owner_row = jnp.concatenate([owner_row, owner_row[:, 128:]], 1)
    wide = jnp.broadcast_to(owner_row, (WIDE, WIDE))
    tall = wide.T[:ROWS]
    wide = wide[:ROWS]
    lane = iota((ROWS, WIDE), 1)
    row_l = jnp.where(lane < ROWS, lane, lane - TILE)
    row_s = iota((ROWS, WIDE), 0)
    one = jnp.where(wide == tall, 1.0, 0.0)
    less, more = row_s < row_l, row_s > row_l
    rank_l = jnp.sum(jnp.where(less, one, 0.0), 0, keepdims=True)
    after_l = jnp.sum(jnp.where(more, one, 0.0), 0, keepdims=True)
    once = jnp.where(lane < ROWS, one, 0.0)
    rank_s = jnp.sum(jnp.where(more, once, 0.0), 1, keepdims=True)
    after_s = jnp.sum(jnp.where(less, once, 0.0), 1, keepdims=True)
    return (wide[:1], rank_l, after_l), (tall[:, :1], rank_s, after_s)


class Order:
    def __init__(self, wide_ref, tall_ref):
        self.owner_l, self.rank_l, self.after_l = (wide_ref[n : n + 1, :] for n in range(3))
        self.owner_s, self.rank_s, self.after_s = (tall_ref[:, n : n + 1] for n in range(3))


def rim_picks(r, me):
    lane = iota((ROWS, 128), 1)
    first, last = r.rank_s == 0.0, r.after_s == 0.0
    even = me % 2 == 0
    picks = []
    for half in (0, 1):
        slot = lane - TILE * half
        inside = (slot >= 0) & (slot < TILE)
        to_left = jnp.where(inside, slot + jnp.where(me == 0, 1, 0), -1).astype(F32)
        to_right = jnp.where(inside, slot - jnp.where(me == MEMBERS - 1, 1, 0), -1).astype(F32)
        left = jnp.where((r.owner_s == to_left) & first, 1.0, 0.0)
        right = jnp.where((r.owner_s == to_right) & last, 1.0, 0.0)
        near = jnp.where(even, right, left).astype(BF16)
        far = jnp.where(even, left, right).astype(BF16)
        picks.append((near, far))
    return picks


def far_pick(r, me, width):
    top = iota((8, width), 0) == 0
    owner, rank, after = r.owner_l[:, :width], r.rank_l[:, :width], r.after_l[:, :width]
    head = top & (me == 0) & (owner == 0.0) & (rank == 0.0)
    tail = top & (me == MEMBERS - 1) & (owner == MEMBERS - 1.0) & (after == 0.0)
    return ones_where(head), ones_where(tail)


def rims_of(rows, r, me):
    half = rows.shape[0] // 2
    top, bottom = rim_picks(r, me)
    rims = [(dot(rows[:half], a) + dot(rows[half:], b)).astype(BF16) for a, b in zip(top, bottom)]
    head, tail = far_pick(r, me, ROWS)
    far = lax.dot_general(head + tail, rows, NT, preferred_element_type=F32).astype(BF16)
    return [far] + rims[::-1]


def local_rows(rows, r):
    lane = iota((ROWS, WIDE), 1)
    row_l = jnp.where(lane < ROWS, lane, lane - TILE)
    same = r.owner_l == r.owner_s
    before = ones_where(same & (r.rank_s + 1.0 == r.rank_l))
    after = ones_where(same & (r.rank_s == r.rank_l + 1.0))
    here = ones_where(iota((ROWS, WIDE), 0) == row_l)
    return [dot(rows, pick) for pick in (before, here, after)]


def rim_rows(near, away, far, r, me):
    bucket = iota((128, WIDE), 0)
    even = me % 2 == 0
    result = []
    for rim, edge, end in zip(
        (jnp.where(even, away, near), jnp.where(even, near, away)), (r.rank_l, r.after_l), far_pick(r, me, WIDE)
    ):
        ends = []
        for side in (0, 1):
            want = bucket - TILE * side
            want = jnp.where((want >= 0) & (want < TILE), want, -1).astype(F32)
            ends.append(dot(rim, ones_where((want == r.owner_l) & (edge == 0.0))))
        result.append(jnp.concatenate(ends, 0) + lax.dot_general(far, end, TN, preferred_element_type=F32))
    return result


def set_wide(ref, k, value):
    for tile in (0, 1):
        part = value[:, 128 * tile : 128 * (tile + 1)]
        ref[tile, k] = part.reshape(-1, TILE, 128)


def chunk_copies(a_hbm, a_ref, sems, planes, n):
    rows = pl.ds(16 * n, 16)
    return [
        pltpu.make_async_copy(a_hbm.at[k, rows], a_ref.at[at, rows], sems.at[at, n])
        for at, k in enumerate(planes)
    ]


def start_copies(a_hbm, a_ref, sems, planes):
    for n in range(TILE // 16):
        for copy in chunk_copies(a_hbm, a_ref, sems, planes, n):
            copy.start()


def next_groups(a_hbm, a_ref, sems, planes, ib, group_ref):
    for copy in chunk_copies(a_hbm, a_ref, sems, planes, ib):
        copy.wait()
    set_groups(a_ref, ib, group_ref)


def set_groups(a_ref, ib, group_ref):
    for k in range(a_ref.shape[0]):
        for i in range(8):
            low, high = (a_ref[k, 16 * ib + i + n].astype(F32) for n in (0, 8))
            group_ref[0, k, i] = low[:, :128]
            group_ref[1, k, i] = high[:, :128]
            group_ref[2, k, i] = jnp.concatenate([low[:, 128:], high[:, 128:]], 1)


def folded(terms):
    sub = iota((8, 128), 0)
    for shift in (1, 2, 4):
        keep = (sub & shift) == 0
        terms = [
            jnp.where(keep, x, y) + pltpu.roll(jnp.where(keep, y, x), shift, 0)
            for x, y in zip(terms[::2], terms[1::2])
        ]
    return terms[0]


def contracted(group_ref, wide_ref, g, tile, pairs, columns):
    totals = [[None] * 8 for _ in columns]
    for jb in range(TILE // 8):
        j = pl.ds(8 * jb, 8)
        for k, base in pairs:
            a = [group_ref[g, k, i, j, :] for i in range(8)]
            for n, column in enumerate(columns):
                x = wide_ref[tile, k, base + column, j, :]
                for i in range(8):
                    term = a[i] * x
                    totals[n][i] = term if totals[n][i] is None else totals[n][i] + term
    return [folded(t) for t in totals]


def ungrouped(out_ref, index):
    low, high, both = out_ref[0, index], out_ref[1, index], out_ref[2, index]
    top = jnp.concatenate([low, both[:, :TILE]], 1)
    bottom = jnp.concatenate([high, both[:, TILE:]], 1)
    return jnp.concatenate([top, bottom], 0)


def first_kernel(me_ref, owner_ref, p_ref, wide_ref, tall_ref, p_out, back_out, far_out, away_out, near_out):
    rows, columns = rank_arrays(owner_ref[...])
    p_out[...] = p_ref[...]
    wide_ref[...] = jnp.zeros_like(wide_ref)
    for n in range(3):
        wide_ref[n : n + 1, :] = rows[n]
    lane = iota((ROWS, 128), 1)
    tall_ref[...] = jnp.where(lane == 0, columns[0], jnp.where(lane == 1, columns[1], columns[2]))
    r = Order(wide_ref, tall_ref)
    for ref, rim in zip((far_out, away_out, near_out), rims_of(p_ref[...], r, me_ref[0])):
        ref[...] = rim
    back_out[...] = jnp.zeros_like(back_out)
    back_out[:, : MODES * TILE] = far_out[...]


def halves(ib):
    return pl.ds(pl.multiple_of(16 * ib, 8), 8), pl.ds(pl.multiple_of(16 * ib + 8, 8), 8)


def middle_kernel(
    order_l_ref, order_s_ref, a_hbm, p_ref, mid_ref, scale_ref, local_ref, outer_ref,
    a_ref, sems, outer_sem, group_ref, wide_ref, out_ref,
):
    ib = pl.program_id(0)

    @pl.when(ib == 0)
    def _():
        start_copies(a_hbm, a_ref, sems, (1,))
        for at in range(2):
            pltpu.make_async_copy(a_hbm.at[2 * at], outer_ref.at[at], outer_sem.at[at]).start()
        before, here, after = local_rows(p_ref[...], Order(order_l_ref, order_s_ref))
        set_wide(wide_ref, 0, here)
        set_wide(local_ref, 0, before)
        set_wide(local_ref, 1, after)

    next_groups(a_hbm, a_ref, sems, (1,), ib, group_ref)
    sub, lane = iota((8, 128), 0), iota((8, 128), 1)
    lower, upper = halves(ib)

    def one_group(g, carry):
        tile = jnp.where(g == 2, 1, 0)
        second = (g == 1) | ((g == 2) & (lane >= TILE))
        diag = jnp.zeros((8, 128), F32)
        for i in range(8):
            entry = jnp.where(second, group_ref[g, 0, i, upper, :], group_ref[g, 0, i, lower, :])
            diag = jnp.where(sub == i, entry, diag)
        scale = 0.6 * (1.0 / diag)
        scale_ref[ib, g] = scale
        for half in (0, 1):
            columns = [3 * half + c for c in range(3)]
            sums = contracted(group_ref, wide_ref, g, tile, [(0, 0)], columns)
            for c, total in zip(columns, sums):
                own = jnp.where(second, wide_ref[tile, 0, c, upper, :], wide_ref[tile, 0, c, lower, :])
                out_ref[g, c] = own - scale * total
        return carry

    lax.fori_loop(0, 3, one_group, 0, unroll=True)
    rows = pl.ds(pl.multiple_of(16 * ib, 16), 16)
    for index in range(6):
        mid_ref[index, rows, :] = ungrouped(out_ref, index).astype(BF16)

    @pl.when(ib == pl.num_programs(0) - 1)
    def _():
        for at in range(2):
            pltpu.make_async_copy(a_hbm.at[2 * at], outer_ref.at[at], outer_sem.at[at]).wait()


def smooth_kernel(
    me_ref, order_l_ref, order_s_ref, mid_ref, scale_ref, local_ref, outer_ref, on_ref, away_ref, near_ref, back_ref,
    s_ref, far_out, away_out, near_out, group_ref, wide_ref, out_ref,
):
    ib = pl.program_id(0)
    me = me_ref[0]

    @pl.when(ib == 0)
    def _():
        r = Order(order_l_ref, order_s_ref)
        for k, value in enumerate(rim_rows(near_ref[...], away_ref[...], on_ref[...] + back_ref[:, : MODES * TILE], r, me)):
            set_wide(wide_ref, k, value)
        wide_ref[...] += local_ref[...]
        s_ref[6:12] = mid_ref[...]

    set_groups(outer_ref, ib, group_ref)

    def one_group(g, carry):
        tile = jnp.where(g == 2, 1, 0)
        scale = 0.0 - scale_ref[ib, g]
        for k in range(2):
            for half in (0, 1):
                columns = [3 * half + c for c in range(3)]
                sums = contracted(group_ref, wide_ref, g, tile, [(k, 0)], columns)
                for c, total in zip(columns, sums):
                    out_ref[g, 6 * k + c] = scale * total
        return carry

    lax.fori_loop(0, 3, one_group, 0, unroll=True)
    rows = pl.ds(pl.multiple_of(16 * ib, 16), 16)
    for index in range(12):
        s_ref[index if index < 6 else index + 6, rows, :] = ungrouped(out_ref, index).astype(BF16)

    @pl.when(ib == pl.num_programs(0) - 1)
    def _():
        r = Order(order_l_ref, order_s_ref)
        flat = s_ref[...].reshape(COLS, ROWS)
        for ref, rim in zip((far_out, away_out, near_out), rims_of(flat, r, me)):
            ref[...] = rim


def slot_grid(width):
    spot = iota((MEMBERS * SLOTS, width), 0)
    return (spot // SLOTS).astype(F32), (spot % SLOTS).astype(F32)


def pack_kernel(order_l_ref, s_ref, out_ref):
    member, slot = slot_grid(ROWS)
    owner, rank = order_l_ref[0:1, :ROWS], order_l_ref[1:2, :ROWS]
    mine = owner == member
    pick = ones_where(mine & (rank == slot))
    count = jnp.sum(jnp.where(mine, 1.0, 0.0), 1, keepdims=True)
    for block in range(COLS // 128):
        value = lax.dot_general(
            pick, s_ref[128 * block : 128 * (block + 1), :], NT, preferred_element_type=F32
        ).reshape(MEMBERS, SLOTS, 128)
        out_ref[:, 6 * block : 6 * block + 6, :] = value[:, :6, :].astype(BF16)
    counts = jnp.broadcast_to(count, (MEMBERS * SLOTS, 128)).reshape(MEMBERS, SLOTS, 128)
    out_ref[:, 54:56, :] = counts[:, :2, :].astype(BF16)


OFFSETS = [[(k, 6 * (e - k)) for k in range(3) if 0 <= e - k <= 2] for e in range(5)]


def spare_lanes(axis):
    entry, spare = iota((WIDE, WIDE), axis), iota((WIDE, WIDE), 1 - axis) - 252
    return ones_where((spare >= 0) & (entry == 108 + 7 * spare))


def product_kernel(
    me_ref, order_l_ref, order_s_ref, a_hbm, s_ref, far_ref, away_ref, near_ref,
    out_ref, far_out, a_ref, sems, group_ref, wide_ref, ap_ref, own_ref, term_ref,
):
    ib = pl.program_id(0)
    me = me_ref[0]

    @pl.when(ib == 0)
    def _():
        start_copies(a_hbm, a_ref, sems, (0, 1, 2))
        r = Order(order_l_ref, order_s_ref)
        before, here, after = local_rows(s_ref[...], r)
        left, right = rim_rows(near_ref[...], away_ref[...], far_ref[...], r, me)
        for k, value in enumerate((before + left, here, after + right)):
            set_wide(wide_ref, k, value)
        term_ref[...] = jnp.zeros_like(term_ref)

    next_groups(a_hbm, a_ref, sems, (0, 1, 2), ib, group_ref)
    lane = iota((8, 128), 1)

    def one_group(step, carry):
        g, half = step // 2, step % 2
        tile = jnp.where(g == 2, 1, 0)
        for e in range(5):
            columns = [3 * half + c for c in range(3)]
            sums = contracted(group_ref, wide_ref, g, tile, OFFSETS[e], columns)
            for c, total in zip(columns, sums):
                ap_ref[g, ib, 6 * e + c] = total.astype(BF16).astype(F32)
        second = (g == 1) | ((g == 2) & (lane >= TILE))
        lower, upper = pl.ds(pl.multiple_of(16 * ib, 8), 8), pl.ds(pl.multiple_of(16 * ib + 8, 8), 8)
        for c in range(9):
            column = 9 * half + c
            own_ref[g, ib, column] = jnp.where(
                second, wide_ref[tile, 1, column, upper, :], wide_ref[tile, 1, column, lower, :]
            )
        return carry

    lax.fori_loop(0, 6, one_group, 0)

    @pl.when(ib == pl.num_programs(0) - 1)
    def _():
        def one_pair(step, carry):
            k, e = step // 5, step % 5
            for c in range(6):
                near, far = [None] * 6, [None] * 6
                for block in range(TILE // 16):
                    for g in range(3):
                        x = own_ref[g, block, 6 * k + c]
                        for d in range(6):
                            term = x * ap_ref[g, block, 6 * e + d]
                            sums = far if g == 2 else near
                            sums[d] = term if sums[d] is None else sums[d] + term
                for d in range(6):
                    row = slice(6 * c + d, 6 * c + d + 1)
                    tail = jnp.sum(far[d], 0, keepdims=True)
                    term_ref[step, row, 0:128] = jnp.sum(near[d], 0, keepdims=True)
                    term_ref[step, row, 128:ROWS] = tail[:, :TILE] + tail[:, TILE:]
            return carry

        lax.fori_loop(0, 15, one_pair, 0)
        r = Order(order_l_ref, order_s_ref)
        owner, rank, after = (x[:, :ROWS] for x in (r.owner_l, r.rank_l, r.after_l))
        member, slot = slot_grid(ROWS)
        mine, row_slot = owner == member, slot < 6.0
        here = ones_where(mine & (rank == slot))
        back_to = member + jnp.where(me == 0, 1.0, 0.0)
        on_to = member - jnp.where(me == MEMBERS - 1, 1.0, 0.0)
        back = (mine & row_slot & (rank == slot + 1.0)) | ((slot == 6.0) & (owner == back_to) & (rank == 0.0))
        on = (mine & row_slot & (rank == slot - 1.0) & (after > 0.0)) | (
            (slot == 7.0) & (owner == on_to) & (after == 0.0)
        )
        picks = [ones_where(back), here, ones_where(on)]
        terms = []
        for k in range(3):
            pieces = [term_ref[5 * k + e][:36, :ROWS] for e in range(5)]
            pieces.append(jnp.zeros((4 + 36 * k, ROWS), F32))
            if k < 2:
                pieces.insert(0, jnp.zeros((72 - 36 * k, ROWS), F32))
            terms.append(jnp.concatenate(pieces, 0))
        total = None
        for k in range(3):
            prod = exact_dot(picks[k], terms[k], NT, True)
            total = prod if total is None else total + prod
        high = total.astype(BF16).astype(F32)
        rest = dot((total - high).astype(BF16), spare_lanes(0))
        out_ref[...] = (high + rest).astype(BF16)
        head, tail = far_pick(r, me, ROWS)
        far_out[...] = exact_dot(head, terms[0], NT, True) + exact_dot(tail, terms[2], NT, True)


def unpack_smooth_kernel(recv_ref, out_ref, pick_out):
    size = MEMBERS * SLOTS
    count = jnp.broadcast_to(recv_ref[:, 54:55, :].astype(F32), (MEMBERS, SLOTS, 128)).reshape(size, 128)
    source, other = iota((size, size), 0) // SLOTS, iota((size, size), 1) // SLOTS
    first_slot = iota((size, size), 1) % SLOTS == 0
    earlier = ones_where((other < source) & first_slot)
    start = dot(earlier, count.astype(BF16))[:, :1]
    count = count[:, :1]
    slot = (iota((size, 1), 0) % SLOTS).astype(F32)
    place = jnp.where(slot < count, start + slot, -1.0)
    column = iota((size, ROWS), 1).astype(F32)
    pick = ones_where(place == column)
    for block in range(COLS // 128):
        rows = recv_ref[:, 6 * block : 6 * block + 6, :].astype(F32)
        rows = jnp.concatenate([rows, jnp.zeros((MEMBERS, 2, 128), F32)], 1).reshape(size, 128)
        value = lax.dot_general(rows.astype(BF16), pick, TN, preferred_element_type=F32)
        out_ref[128 * block : 128 * (block + 1), :] = value.astype(BF16)
    place = jnp.where(slot == 6.0, jnp.where(start == 0.0, ROWS - 1.0, start - 1.0), place)
    stop = start + count
    place = jnp.where(slot == 7.0, jnp.where(stop == float(ROWS), 0.0, stop), place)
    column = iota((size, WIDE), 1).astype(F32)
    pick_out[...] = jnp.where(place == column, 1.0, 0.0).T[:ROWS].astype(BF16)


def unpack_coarse_kernel(me_ref, pick_ref, sums_ref, far_ref, out_ref):
    me = me_ref[0]
    total = dot(pick_ref[...], sums_ref[...])
    total = total + dot(total.astype(BF16), spare_lanes(1))
    row = iota((ROWS, WIDE), 0)
    edge = jnp.where(me == 0, 0, ROWS - 1)
    far = jnp.broadcast_to(far_ref[0:1, :], (ROWS, WIDE))
    total = total + jnp.where(row == edge, far, 0.0)
    out_ref[...] = total[:, :252]


def call(kernel, outs, args, grid=None, in_specs=None, out_specs=None, scratch=(), flops=0, mib=16, name=None):
    whole = lambda shape: pl.BlockSpec(shape, lambda *_: (0,) * len(shape))
    specs = []
    for n, arg in enumerate(args):
        spec = None if in_specs is None else in_specs.get(n)
        if spec is None:
            spec = pl.BlockSpec(memory_space=pltpu.SMEM) if arg.shape == (1,) else whole(arg.shape)
        specs.append(spec)
    moved = sum(a.size * a.dtype.itemsize for a in args) + sum(o.size * o.dtype.itemsize for o in outs)
    return pl.pallas_call(
        kernel,
        grid=(1,) if grid is None else grid,
        in_specs=specs,
        out_specs=[(out_specs or {}).get(n, whole(o.shape)) for n, o in enumerate(outs)],
        out_shape=outs,
        scratch_shapes=list(scratch),
        compiler_params=pltpu.CompilerParams(vmem_limit_bytes=mib * MIB),
        cost_estimate=pl.CostEstimate(flops=flops, bytes_accessed=moved, transcendentals=0),
        name=name,
    )(*args)


def shaped(shape, dtype=BF16):
    return jax.ShapeDtypeStruct(shape, dtype)


def swaps(groups):
    ring, axes = MEMBERS, range(groups)
    both = lambda pairs: [q for a, b in pairs for q in ((a, b), (b, a))]
    across = both([(g * ring - 1, g * ring) for g in range(1, groups)])
    away = both([(g * ring + i, g * ring + (i + 1) % ring) for g in axes for i in range(1, ring, 2)])
    near = both([(g * ring + i, g * ring + i + 1) for g in axes for i in range(0, ring, 2)])
    return across, away, near


def per_device(a_band, p_tent, new_owner):
    axes = ("group", "member")
    across, away_pairs, near_pairs = swaps(lax.axis_size("group"))
    me = lax.axis_index("member").astype(jnp.int32).reshape(1)
    a = a_band.transpose(1, 2, 3, 0)
    p = p_tent.transpose(1, 2, 0).reshape(MODES * TILE, ROWS)
    a_spec = pl.BlockSpec(memory_space=pltpu.HBM)
    grid = (TILE // 16,)

    def a_scratch(planes):
        return [
            pltpu.VMEM((planes, TILE, TILE, ROWS), BF16),
            pltpu.SemaphoreType.DMA((planes, TILE // 16)),
            pltpu.VMEM((3, planes, 8, TILE, 128), F32),
        ]

    def exchanged(far, away, near):
        far = lax.ppermute(far, axes, across)
        away = lax.ppermute(away, axes, away_pairs)
        return far, away, lax.ppermute(near, axes, near_pairs)

    def rims(length):
        return [shaped((8, length)), shaped((length // 2, 128)), shaped((length // 2, 128))]

    order_l, order_s, p, back, *sent = call(
        first_kernel,
        [shaped((8, WIDE), F32), shaped((ROWS, 128), F32), shaped(p.shape), shaped((8, BACK))] + rims(MODES * TILE),
        (me, new_owner.reshape(1, ROWS), p),
        name="rims",
    )
    far, away, near = sent
    on = lax.ppermute(far, axes, across[::2])
    away = lax.ppermute(away, axes, away_pairs)
    near = lax.ppermute(near, axes, near_pairs)
    back = lax.ppermute(back, axes, across[1::2])
    got = on, away, near, back
    local = shaped((2, 2, MODES, TILE, 128), F32)
    parts = call(
        middle_kernel,
        [shaped((MODES, TILE, ROWS)), shaped((TILE // 16, 3, 8, 128), F32), local, shaped((2, TILE, TILE, ROWS))],
        (order_l, order_s, a, p),
        grid=grid,
        in_specs={2: a_spec},
        out_specs={3: pl.BlockSpec(memory_space=pltpu.VMEM)},
        scratch=[
            *a_scratch(1)[:2],
            pltpu.SemaphoreType.DMA((2,)),
            *a_scratch(1)[2:],
            pltpu.VMEM((2, 1, MODES, TILE, 128), F32),
            pltpu.VMEM((3, MODES, 8, 128), F32),
        ],
        flops=10**9,
        mib=46,
        name="middle",
    )
    s, *sent = call(
        smooth_kernel,
        [shaped((18, TILE, ROWS))] + rims(COLS),
        (me, order_l, order_s, *parts, *got),
        grid=grid,
        in_specs={6: pl.BlockSpec(memory_space=pltpu.VMEM)},
        scratch=[a_scratch(2)[2], pltpu.VMEM(local.shape, F32), pltpu.VMEM((3, 12, 8, 128), F32)],
        flops=10**9,
        mib=46,
        name="smooth",
    )
    got = exchanged(*sent)
    s = s.reshape(COLS, ROWS)
    (packed,) = call(pack_kernel, [shaped((MEMBERS, PACKED, 128))], (order_l, s), name="pack")
    packed, *got = lax.optimization_barrier((packed, *got))
    recv = lax.all_to_all(packed, "member", split_axis=0, concat_axis=0, tiled=True)

    sums, far = call(
        product_kernel,
        [shaped((MEMBERS * SLOTS, WIDE)), shaped((8, WIDE), F32)],
        (me, order_l, order_s, a, s, *got),
        grid=grid,
        in_specs={3: a_spec},
        scratch=[
            *a_scratch(3),
            pltpu.VMEM((2, 3, 18, TILE, 128), F32),
            pltpu.VMEM((3, TILE // 16, 30, 8, 128), F32),
            pltpu.VMEM((3, TILE // 16, 18, 8, 128), F32),
            pltpu.VMEM((15, 40, WIDE), F32),
        ],
        flops=10**10,
        mib=50,
        name="product",
    )
    far = lax.ppermute(far, axes, across)
    sums = lax.all_to_all(
        sums.reshape(MEMBERS, SLOTS, WIDE), "member", split_axis=0, concat_axis=0, tiled=True
    ).reshape(MEMBERS * SLOTS, WIDE)
    smooth, pick = call(
        unpack_smooth_kernel,
        [shaped((COLS, ROWS)), shaped((ROWS, MEMBERS * SLOTS))],
        (recv,),
        flops=10**9,
        name="unpack_smooth",
    )
    (coarse,) = call(
        unpack_coarse_kernel, [shaped((ROWS, 252), F32)], (me, pick, sums, far), name="unpack_coarse"
    )
    return smooth.reshape(3, MODES, TILE, ROWS).transpose(3, 0, 1, 2), coarse


def solution(mesh):
    in_specs = (
        P(("group", "member"), None, None, None),
        P(("group", "member"), None, None),
        P(("group", "member")),
    )
    out_specs = (P(("group", "member"), None, None, None), P(("group", "member"), None))
    return jax.shard_map(
        per_device, mesh=mesh, in_specs=in_specs, out_specs=out_specs, check_vma=False
    )
```

```python
import jax
import jax.numpy as jnp
from jax import lax
from jax.experimental import pallas as pl
from jax.experimental.pallas import tpu as pltpu
from jax.sharding import PartitionSpec as P

ROWS = 192
WIDE = 256
TILE = 64
MODES = 6
MEMBERS = 64
SLOTS = 8
COLS = 3 * MODES * TILE
F32 = jnp.float32
BF16 = jnp.bfloat16
NT = (((1,), (1,)), ((), ()))
TN = (((0,), (0,)), ((), ()))
MIB = 1024 * 1024
BACK = 3328
PACKED = 56


def iota(shape, axis):
    return lax.broadcasted_iota(jnp.int32, shape, axis)


def ones_where(mask):
    return jnp.where(mask, 1.0, 0.0).astype(BF16)


def dot(a, b):
    return jnp.dot(a, b, preferred_element_type=F32)


def parts_of(x):
    high = x.astype(BF16)
    rest = x - high.astype(F32)
    mid = rest.astype(BF16)
    low = (rest - mid.astype(F32)).astype(BF16)
    return high, mid, low


def exact_dot(pick, x, dims, pick_first):
    total = None
    for part in parts_of(x):
        ab = (pick, part) if pick_first else (part, pick)
        prod = lax.dot_general(*ab, dims, preferred_element_type=F32)
        total = prod if total is None else total + prod
    return total


def rank_arrays(owner_row):
    owner_row = owner_row.astype(F32)
    owner_row = jnp.concatenate([owner_row, owner_row[:, 128:]], 1)
    wide = jnp.broadcast_to(owner_row, (WIDE, WIDE))
    tall = wide.T[:ROWS]
    wide = wide[:ROWS]
    lane = iota((ROWS, WIDE), 1)
    row_l = jnp.where(lane < ROWS, lane, lane - TILE)
    row_s = iota((ROWS, WIDE), 0)
    one = jnp.where(wide == tall, 1.0, 0.0)
    less, more = row_s < row_l, row_s > row_l
    rank_l = jnp.sum(jnp.where(less, one, 0.0), 0, keepdims=True)
    after_l = jnp.sum(jnp.where(more, one, 0.0), 0, keepdims=True)
    once = jnp.where(lane < ROWS, one, 0.0)
    rank_s = jnp.sum(jnp.where(more, once, 0.0), 1, keepdims=True)
    after_s = jnp.sum(jnp.where(less, once, 0.0), 1, keepdims=True)
    return (wide[:1], rank_l, after_l), (tall[:, :1], rank_s, after_s)


class Order:
    def __init__(self, wide_ref, tall_ref):
        self.owner_l, self.rank_l, self.after_l = (wide_ref[n : n + 1, :] for n in range(3))
        self.owner_s, self.rank_s, self.after_s = (tall_ref[:, n : n + 1] for n in range(3))


def rim_picks(r, me):
    lane = iota((ROWS, 128), 1)
    first, last = r.rank_s == 0.0, r.after_s == 0.0
    even = me % 2 == 0
    picks = []
    for half in (0, 1):
        slot = lane - TILE * half
        inside = (slot >= 0) & (slot < TILE)
        to_left = jnp.where(inside, slot + jnp.where(me == 0, 1, 0), -1).astype(F32)
        to_right = jnp.where(inside, slot - jnp.where(me == MEMBERS - 1, 1, 0), -1).astype(F32)
        left = jnp.where((r.owner_s == to_left) & first, 1.0, 0.0)
        right = jnp.where((r.owner_s == to_right) & last, 1.0, 0.0)
        near = jnp.where(even, right, left).astype(BF16)
        far = jnp.where(even, left, right).astype(BF16)
        picks.append((near, far))
    return picks


def far_pick(r, me, width):
    top = iota((8, width), 0) == 0
    owner, rank, after = r.owner_l[:, :width], r.rank_l[:, :width], r.after_l[:, :width]
    head = top & (me == 0) & (owner == 0.0) & (rank == 0.0)
    tail = top & (me == MEMBERS - 1) & (owner == MEMBERS - 1.0) & (after == 0.0)
    return ones_where(head), ones_where(tail)


def rims_of(rows, r, me):
    half = rows.shape[0] // 2
    top, bottom = rim_picks(r, me)
    rims = [(dot(rows[:half], a) + dot(rows[half:], b)).astype(BF16) for a, b in zip(top, bottom)]
    head, tail = far_pick(r, me, ROWS)
    far = lax.dot_general(head + tail, rows, NT, preferred_element_type=F32).astype(BF16)
    return [far] + rims[::-1]


def local_rows(rows, r):
    lane = iota((ROWS, WIDE), 1)
    row_l = jnp.where(lane < ROWS, lane, lane - TILE)
    same = r.owner_l == r.owner_s
    before = ones_where(same & (r.rank_s + 1.0 == r.rank_l))
    after = ones_where(same & (r.rank_s == r.rank_l + 1.0))
    here = ones_where(iota((ROWS, WIDE), 0) == row_l)
    return [dot(rows, pick) for pick in (before, here, after)]


def rim_rows(near, away, far, r, me):
    bucket = iota((128, WIDE), 0)
    even = me % 2 == 0
    result = []
    for rim, edge, end in zip(
        (jnp.where(even, away, near), jnp.where(even, near, away)), (r.rank_l, r.after_l), far_pick(r, me, WIDE)
    ):
        ends = []
        for side in (0, 1):
            want = bucket - TILE * side
            want = jnp.where((want >= 0) & (want < TILE), want, -1).astype(F32)
            ends.append(dot(rim, ones_where((want == r.owner_l) & (edge == 0.0))))
        result.append(jnp.concatenate(ends, 0) + lax.dot_general(far, end, TN, preferred_element_type=F32))
    return result


def set_wide(ref, k, value):
    for tile in (0, 1):
        part = value[:, 128 * tile : 128 * (tile + 1)]
        ref[tile, k] = part.reshape(-1, TILE, 128)


def chunk_copies(a_hbm, a_ref, sems, planes, n):
    rows = pl.ds(16 * n, 16)
    return [
        pltpu.make_async_copy(a_hbm.at[k, rows], a_ref.at[at, rows], sems.at[at, n])
        for at, k in enumerate(planes)
    ]


def start_copies(a_hbm, a_ref, sems, planes):
    for n in range(TILE // 16):
        for copy in chunk_copies(a_hbm, a_ref, sems, planes, n):
            copy.start()


def next_groups(a_hbm, a_ref, sems, planes, ib, group_ref):
    for copy in chunk_copies(a_hbm, a_ref, sems, planes, ib):
        copy.wait()
    set_groups(a_ref, ib, group_ref)


def set_groups(a_ref, ib, group_ref):
    for k in range(a_ref.shape[0]):
        for i in range(8):
            low, high = (a_ref[k, 16 * ib + i + n].astype(F32) for n in (0, 8))
            group_ref[0, k, i] = low[:, :128]
            group_ref[1, k, i] = high[:, :128]
            group_ref[2, k, i] = jnp.concatenate([low[:, 128:], high[:, 128:]], 1)


def folded(terms):
    sub = iota((8, 128), 0)
    for shift in (1, 2, 4):
        keep = (sub & shift) == 0
        terms = [
            jnp.where(keep, x, y) + pltpu.roll(jnp.where(keep, y, x), shift, 0)
            for x, y in zip(terms[::2], terms[1::2])
        ]
    return terms[0]


def contracted(group_ref, wide_ref, g, tile, pairs, columns):
    totals = [[None] * 8 for _ in columns]
    for jb in range(TILE // 8):
        j = pl.ds(8 * jb, 8)
        for k, base in pairs:
            a = [group_ref[g, k, i, j, :] for i in range(8)]
            for n, column in enumerate(columns):
                x = wide_ref[tile, k, base + column, j, :]
                for i in range(8):
                    term = a[i] * x
                    totals[n][i] = term if totals[n][i] is None else totals[n][i] + term
    return [folded(t) for t in totals]


def contracted_rows(a_ref, wide_ref, k, ib, g, columns):
    totals = [[None] * 8 for _ in columns]
    for pair in range(TILE // 16):
        j = slice(16 * pair, 16 * (pair + 1))
        a = []
        for i in range(8):
            low, high = 16 * ib + i, 16 * ib + 8 + i
            if g < 2:
                part = a_ref[k, high if g else low, j, 0:128].astype(F32)
            else:
                part = jnp.concatenate(
                    [a_ref[k, row, j, 128:ROWS].astype(F32) for row in (low, high)], 1
                )
            a.append(part)
        for half in (0, 1):
            rows = slice(16 * pair + 8 * half, 16 * pair + 8 * half + 8)
            for n, column in enumerate(columns):
                x = wide_ref[g // 2, k, column, rows, :]
                for i in range(8):
                    term = a[i][8 * half : 8 * half + 8] * x
                    totals[n][i] = term if totals[n][i] is None else totals[n][i] + term
    return [folded(t) for t in totals]


def ungrouped(out_ref, index):
    low, high, both = out_ref[0, index], out_ref[1, index], out_ref[2, index]
    top = jnp.concatenate([low, both[:, :TILE]], 1)
    bottom = jnp.concatenate([high, both[:, TILE:]], 1)
    return jnp.concatenate([top, bottom], 0)


def first_kernel(me_ref, owner_ref, p_ref, wide_ref, tall_ref, p_out, back_out, far_out, away_out, near_out):
    rows, columns = rank_arrays(owner_ref[...])
    p_out[...] = p_ref[...]
    wide_ref[...] = jnp.zeros_like(wide_ref)
    for n in range(3):
        wide_ref[n : n + 1, :] = rows[n]
    lane = iota((ROWS, 128), 1)
    tall_ref[...] = jnp.where(lane == 0, columns[0], jnp.where(lane == 1, columns[1], columns[2]))
    r = Order(wide_ref, tall_ref)
    for ref, rim in zip((far_out, away_out, near_out), rims_of(p_ref[...], r, me_ref[0])):
        ref[...] = rim
    back_out[...] = jnp.zeros_like(back_out)
    back_out[:, : MODES * TILE] = far_out[...]


def halves(ib):
    return pl.ds(pl.multiple_of(16 * ib, 8), 8), pl.ds(pl.multiple_of(16 * ib + 8, 8), 8)


def middle_kernel(
    order_l_ref, order_s_ref, a_hbm, p_ref, mid_ref, scale_ref, local_ref, outer_ref,
    a_ref, sems, outer_sem, group_ref, wide_ref, out_ref,
):
    ib = pl.program_id(0)

    @pl.when(ib == 0)
    def _():
        start_copies(a_hbm, a_ref, sems, (1,))
        for at in range(2):
            pltpu.make_async_copy(a_hbm.at[2 * at], outer_ref.at[at], outer_sem.at[at]).start()
        before, here, after = local_rows(p_ref[...], Order(order_l_ref, order_s_ref))
        set_wide(wide_ref, 0, here)
        set_wide(local_ref, 0, before)
        set_wide(local_ref, 1, after)

    next_groups(a_hbm, a_ref, sems, (1,), ib, group_ref)
    sub, lane = iota((8, 128), 0), iota((8, 128), 1)
    lower, upper = halves(ib)

    def one_group(g, carry):
        tile = jnp.where(g == 2, 1, 0)
        second = (g == 1) | ((g == 2) & (lane >= TILE))
        diag = jnp.zeros((8, 128), F32)
        for i in range(8):
            entry = jnp.where(second, group_ref[g, 0, i, upper, :], group_ref[g, 0, i, lower, :])
            diag = jnp.where(sub == i, entry, diag)
        scale = 0.6 * (1.0 / diag)
        scale_ref[ib, g] = scale
        for half in (0, 1):
            columns = [3 * half + c for c in range(3)]
            sums = contracted(group_ref, wide_ref, g, tile, [(0, 0)], columns)
            for c, total in zip(columns, sums):
                own = jnp.where(second, wide_ref[tile, 0, c, upper, :], wide_ref[tile, 0, c, lower, :])
                out_ref[g, c] = own - scale * total
        return carry

    lax.fori_loop(0, 3, one_group, 0, unroll=True)
    rows = pl.ds(pl.multiple_of(16 * ib, 16), 16)
    for index in range(6):
        mid_ref[index, rows, :] = ungrouped(out_ref, index).astype(BF16)

    @pl.when(ib == pl.num_programs(0) - 1)
    def _():
        for at in range(2):
            pltpu.make_async_copy(a_hbm.at[2 * at], outer_ref.at[at], outer_sem.at[at]).wait()


def smooth_kernel(
    me_ref, order_l_ref, order_s_ref, mid_ref, scale_ref, local_ref, outer_ref, on_ref, away_ref, near_ref, back_ref,
    s_ref, far_out, away_out, near_out, wide_ref, out_ref,
):
    ib = pl.program_id(0)
    me = me_ref[0]

    @pl.when(ib == 0)
    def _():
        r = Order(order_l_ref, order_s_ref)
        for k, value in enumerate(rim_rows(near_ref[...], away_ref[...], on_ref[...] + back_ref[:, : MODES * TILE], r, me)):
            set_wide(wide_ref, k, value)
        wide_ref[...] += local_ref[...]
        s_ref[6:12] = mid_ref[...]

    for g in range(3):
        scale = 0.0 - scale_ref[ib, g]
        for k in range(2):
            columns = list(range(6))
            sums = contracted_rows(outer_ref, wide_ref, k, ib, g, columns)
            for c, total in zip(columns, sums):
                out_ref[g, 6 * k + c] = scale * total

    rows = pl.ds(pl.multiple_of(16 * ib, 16), 16)
    for index in range(12):
        s_ref[index if index < 6 else index + 6, rows, :] = ungrouped(out_ref, index).astype(BF16)

    @pl.when(ib == pl.num_programs(0) - 1)
    def _():
        r = Order(order_l_ref, order_s_ref)
        flat = s_ref[...].reshape(COLS, ROWS)
        for ref, rim in zip((far_out, away_out, near_out), rims_of(flat, r, me)):
            ref[...] = rim


def slot_grid(width):
    spot = iota((MEMBERS * SLOTS, width), 0)
    return (spot // SLOTS).astype(F32), (spot % SLOTS).astype(F32)


def pack_kernel(order_l_ref, s_ref, out_ref):
    member, slot = slot_grid(ROWS)
    owner, rank = order_l_ref[0:1, :ROWS], order_l_ref[1:2, :ROWS]
    mine = owner == member
    pick = ones_where(mine & (rank == slot))
    count = jnp.sum(jnp.where(mine, 1.0, 0.0), 1, keepdims=True)
    for block in range(COLS // 128):
        value = lax.dot_general(
            pick, s_ref[128 * block : 128 * (block + 1), :], NT, preferred_element_type=F32
        ).reshape(MEMBERS, SLOTS, 128)
        out_ref[:, 6 * block : 6 * block + 6, :] = value[:, :6, :].astype(BF16)
    counts = jnp.broadcast_to(count, (MEMBERS * SLOTS, 128)).reshape(MEMBERS, SLOTS, 128)
    out_ref[:, 54:56, :] = counts[:, :2, :].astype(BF16)


OFFSETS = [[(k, 6 * (e - k)) for k in range(3) if 0 <= e - k <= 2] for e in range(5)]


def spare_lanes(axis):
    entry, spare = iota((WIDE, WIDE), axis), iota((WIDE, WIDE), 1 - axis) - 252
    return ones_where((spare >= 0) & (entry == 108 + 7 * spare))


def product_kernel(
    me_ref, order_l_ref, order_s_ref, a_hbm, s_ref, far_ref, away_ref, near_ref,
    out_ref, far_out, a_ref, sems, group_ref, wide_ref, ap_ref, own_ref, term_ref,
):
    ib = pl.program_id(0)
    me = me_ref[0]

    @pl.when(ib == 0)
    def _():
        start_copies(a_hbm, a_ref, sems, (0, 1, 2))
        r = Order(order_l_ref, order_s_ref)
        before, here, after = local_rows(s_ref[...], r)
        left, right = rim_rows(near_ref[...], away_ref[...], far_ref[...], r, me)
        for k, value in enumerate((before + left, here, after + right)):
            set_wide(wide_ref, k, value)
        term_ref[...] = jnp.zeros_like(term_ref)

    next_groups(a_hbm, a_ref, sems, (0, 1, 2), ib, group_ref)
    lane = iota((8, 128), 1)

    def one_group(step, carry):
        g, half = step // 2, step % 2
        tile = jnp.where(g == 2, 1, 0)
        for e in range(5):
            columns = [3 * half + c for c in range(3)]
            sums = contracted(group_ref, wide_ref, g, tile, OFFSETS[e], columns)
            for c, total in zip(columns, sums):
                ap_ref[g, ib, 6 * e + c] = total.astype(BF16).astype(F32)
        second = (g == 1) | ((g == 2) & (lane >= TILE))
        lower, upper = pl.ds(pl.multiple_of(16 * ib, 8), 8), pl.ds(pl.multiple_of(16 * ib + 8, 8), 8)
        for c in range(9):
            column = 9 * half + c
            own_ref[g, ib, column] = jnp.where(
                second, wide_ref[tile, 1, column, upper, :], wide_ref[tile, 1, column, lower, :]
            )
        return carry

    lax.fori_loop(0, 6, one_group, 0)

    @pl.when(ib == pl.num_programs(0) - 1)
    def _():
        def one_pair(step, carry):
            k, e = step // 5, step % 5
            for c in range(6):
                near, far = [None] * 6, [None] * 6
                for block in range(TILE // 16):
                    for g in range(3):
                        x = own_ref[g, block, 6 * k + c]
                        for d in range(6):
                            term = x * ap_ref[g, block, 6 * e + d]
                            sums = far if g == 2 else near
                            sums[d] = term if sums[d] is None else sums[d] + term
                for d in range(6):
                    row = slice(6 * c + d, 6 * c + d + 1)
                    tail = jnp.sum(far[d], 0, keepdims=True)
                    term_ref[step, row, 0:128] = jnp.sum(near[d], 0, keepdims=True)
                    term_ref[step, row, 128:ROWS] = tail[:, :TILE] + tail[:, TILE:]
            return carry

        lax.fori_loop(0, 15, one_pair, 0)
        r = Order(order_l_ref, order_s_ref)
        owner, rank, after = (x[:, :ROWS] for x in (r.owner_l, r.rank_l, r.after_l))
        member, slot = slot_grid(ROWS)
        mine, row_slot = owner == member, slot < 6.0
        here = ones_where(mine & (rank == slot))
        back_to = member + jnp.where(me == 0, 1.0, 0.0)
        on_to = member - jnp.where(me == MEMBERS - 1, 1.0, 0.0)
        back = (mine & row_slot & (rank == slot + 1.0)) | ((slot == 6.0) & (owner == back_to) & (rank == 0.0))
        on = (mine & row_slot & (rank == slot - 1.0) & (after > 0.0)) | (
            (slot == 7.0) & (owner == on_to) & (after == 0.0)
        )
        picks = [ones_where(back), here, ones_where(on)]
        terms = []
        for k in range(3):
            pieces = [term_ref[5 * k + e][:36, :ROWS] for e in range(5)]
            pieces.append(jnp.zeros((4 + 36 * k, ROWS), F32))
            if k < 2:
                pieces.insert(0, jnp.zeros((72 - 36 * k, ROWS), F32))
            terms.append(jnp.concatenate(pieces, 0))
        total = None
        for k in range(3):
            prod = exact_dot(picks[k], terms[k], NT, True)
            total = prod if total is None else total + prod
        high = total.astype(BF16).astype(F32)
        rest = dot((total - high).astype(BF16), spare_lanes(0))
        out_ref[...] = (high + rest).astype(BF16)
        head, tail = far_pick(r, me, ROWS)
        far_out[...] = exact_dot(head, terms[0], NT, True) + exact_dot(tail, terms[2], NT, True)


def unpack_smooth_kernel(recv_ref, out_ref, pick_out):
    size = MEMBERS * SLOTS
    count = jnp.broadcast_to(recv_ref[:, 54:55, :].astype(F32), (MEMBERS, SLOTS, 128)).reshape(size, 128)
    source, other = iota((size, size), 0) // SLOTS, iota((size, size), 1) // SLOTS
    first_slot = iota((size, size), 1) % SLOTS == 0
    earlier = ones_where((other < source) & first_slot)
    start = dot(earlier, count.astype(BF16))[:, :1]
    count = count[:, :1]
    slot = (iota((size, 1), 0) % SLOTS).astype(F32)
    place = jnp.where(slot < count, start + slot, -1.0)
    column = iota((size, ROWS), 1).astype(F32)
    pick = ones_where(place == column)
    for block in range(COLS // 128):
        rows = recv_ref[:, 6 * block : 6 * block + 6, :].astype(F32)
        rows = jnp.concatenate([rows, jnp.zeros((MEMBERS, 2, 128), F32)], 1).reshape(size, 128)
        value = lax.dot_general(rows.astype(BF16), pick, TN, preferred_element_type=F32)
        out_ref[128 * block : 128 * (block + 1), :] = value.astype(BF16)
    place = jnp.where(slot == 6.0, jnp.where(start == 0.0, ROWS - 1.0, start - 1.0), place)
    stop = start + count
    place = jnp.where(slot == 7.0, jnp.where(stop == float(ROWS), 0.0, stop), place)
    column = iota((size, WIDE), 1).astype(F32)
    pick_out[...] = jnp.where(place == column, 1.0, 0.0).T[:ROWS].astype(BF16)


def unpack_coarse_kernel(me_ref, pick_ref, sums_ref, far_ref, out_ref):
    me = me_ref[0]
    total = dot(pick_ref[...], sums_ref[...])
    total = total + dot(total.astype(BF16), spare_lanes(1))
    row = iota((ROWS, WIDE), 0)
    edge = jnp.where(me == 0, 0, ROWS - 1)
    far = jnp.broadcast_to(far_ref[0:1, :], (ROWS, WIDE))
    total = total + jnp.where(row == edge, far, 0.0)
    out_ref[...] = total[:, :252]


def call(kernel, outs, args, grid=None, in_specs=None, out_specs=None, scratch=(), flops=0, mib=16, name=None):
    whole = lambda shape: pl.BlockSpec(shape, lambda *_: (0,) * len(shape))
    specs = []
    for n, arg in enumerate(args):
        spec = None if in_specs is None else in_specs.get(n)
        if spec is None:
            spec = pl.BlockSpec(memory_space=pltpu.SMEM) if arg.shape == (1,) else whole(arg.shape)
        specs.append(spec)
    moved = sum(a.size * a.dtype.itemsize for a in args) + sum(o.size * o.dtype.itemsize for o in outs)
    return pl.pallas_call(
        kernel,
        grid=(1,) if grid is None else grid,
        in_specs=specs,
        out_specs=[(out_specs or {}).get(n, whole(o.shape)) for n, o in enumerate(outs)],
        out_shape=outs,
        scratch_shapes=list(scratch),
        compiler_params=pltpu.CompilerParams(vmem_limit_bytes=mib * MIB),
        cost_estimate=pl.CostEstimate(flops=flops, bytes_accessed=moved, transcendentals=0),
        name=name,
    )(*args)


def shaped(shape, dtype=BF16):
    return jax.ShapeDtypeStruct(shape, dtype)


def swaps(groups):
    ring, axes = MEMBERS, range(groups)
    both = lambda pairs: [q for a, b in pairs for q in ((a, b), (b, a))]
    across = both([(g * ring - 1, g * ring) for g in range(1, groups)])
    away = both([(g * ring + i, g * ring + (i + 1) % ring) for g in axes for i in range(1, ring, 2)])
    near = both([(g * ring + i, g * ring + i + 1) for g in axes for i in range(0, ring, 2)])
    return across, away, near


def per_device(a_band, p_tent, new_owner):
    axes = ("group", "member")
    across, away_pairs, near_pairs = swaps(lax.axis_size("group"))
    me = lax.axis_index("member").astype(jnp.int32).reshape(1)
    a = a_band.transpose(1, 2, 3, 0)
    p = p_tent.transpose(1, 2, 0).reshape(MODES * TILE, ROWS)
    a_spec = pl.BlockSpec(memory_space=pltpu.HBM)
    grid = (TILE // 16,)

    def a_scratch(planes):
        return [
            pltpu.VMEM((planes, TILE, TILE, ROWS), BF16),
            pltpu.SemaphoreType.DMA((planes, TILE // 16)),
            pltpu.VMEM((3, planes, 8, TILE, 128), F32),
        ]

    def exchanged(far, away, near):
        far = lax.ppermute(far, axes, across)
        away = lax.ppermute(away, axes, away_pairs)
        return far, away, lax.ppermute(near, axes, near_pairs)

    def rims(length):
        return [shaped((8, length)), shaped((length // 2, 128)), shaped((length // 2, 128))]

    order_l, order_s, p, back, *sent = call(
        first_kernel,
        [shaped((8, WIDE), F32), shaped((ROWS, 128), F32), shaped(p.shape), shaped((8, BACK))] + rims(MODES * TILE),
        (me, new_owner.reshape(1, ROWS), p),
        name="rims",
    )
    far, away, near = sent
    on = lax.ppermute(far, axes, across[::2])
    away = lax.ppermute(away, axes, away_pairs)
    near = lax.ppermute(near, axes, near_pairs)
    back = lax.ppermute(back, axes, across[1::2])
    got = on, away, near, back
    local = shaped((2, 2, MODES, TILE, 128), F32)
    parts = call(
        middle_kernel,
        [shaped((MODES, TILE, ROWS)), shaped((TILE // 16, 3, 8, 128), F32), local, shaped((2, TILE, TILE, ROWS))],
        (order_l, order_s, a, p),
        grid=grid,
        in_specs={2: a_spec},
        out_specs={3: pl.BlockSpec(memory_space=pltpu.VMEM)},
        scratch=[
            *a_scratch(1)[:2],
            pltpu.SemaphoreType.DMA((2,)),
            *a_scratch(1)[2:],
            pltpu.VMEM((2, 1, MODES, TILE, 128), F32),
            pltpu.VMEM((3, MODES, 8, 128), F32),
        ],
        flops=10**9,
        mib=46,
        name="middle",
    )
    s, *sent = call(
        smooth_kernel,
        [shaped((18, TILE, ROWS))] + rims(COLS),
        (me, order_l, order_s, *parts, *got),
        grid=grid,
        in_specs={6: pl.BlockSpec(memory_space=pltpu.VMEM)},
        scratch=[pltpu.VMEM(local.shape, F32), pltpu.VMEM((3, 12, 8, 128), F32)],
        flops=10**9,
        mib=46,
        name="smooth",
    )
    got = exchanged(*sent)
    s = s.reshape(COLS, ROWS)
    (packed,) = call(pack_kernel, [shaped((MEMBERS, PACKED, 128))], (order_l, s), name="pack")
    packed, *got = lax.optimization_barrier((packed, *got))
    recv = lax.all_to_all(packed, "member", split_axis=0, concat_axis=0, tiled=True)

    sums, far = call(
        product_kernel,
        [shaped((MEMBERS * SLOTS, WIDE)), shaped((8, WIDE), F32)],
        (me, order_l, order_s, a, s, *got),
        grid=grid,
        in_specs={3: a_spec},
        scratch=[
            *a_scratch(3),
            pltpu.VMEM((2, 3, 18, TILE, 128), F32),
            pltpu.VMEM((3, TILE // 16, 30, 8, 128), F32),
            pltpu.VMEM((3, TILE // 16, 18, 8, 128), F32),
            pltpu.VMEM((15, 40, WIDE), F32),
        ],
        flops=10**10,
        mib=50,
        name="product",
    )
    far = lax.ppermute(far, axes, across)
    sums = lax.all_to_all(
        sums.reshape(MEMBERS, SLOTS, WIDE), "member", split_axis=0, concat_axis=0, tiled=True
    ).reshape(MEMBERS * SLOTS, WIDE)
    smooth, pick = call(
        unpack_smooth_kernel,
        [shaped((COLS, ROWS)), shaped((ROWS, MEMBERS * SLOTS))],
        (recv,),
        flops=10**9,
        name="unpack_smooth",
    )
    (coarse,) = call(
        unpack_coarse_kernel, [shaped((ROWS, 252), F32)], (me, pick, sums, far), name="unpack_coarse"
    )
    return smooth.reshape(3, MODES, TILE, ROWS).transpose(3, 0, 1, 2), coarse


def solution(mesh):
    in_specs = (
        P(("group", "member"), None, None, None),
        P(("group", "member"), None, None),
        P(("group", "member")),
    )
    out_specs = (P(("group", "member"), None, None, None), P(("group", "member"), None))
    return jax.shard_map(
        per_device, mesh=mesh, in_specs=in_specs, out_specs=out_specs, check_vma=False
    )
```

```python
import jax
import jax.numpy as jnp
from jax import lax
from jax.experimental import pallas as pl
from jax.experimental.pallas import tpu as pltpu
from jax.sharding import PartitionSpec as P

ROWS = 192
WIDE = 256
TILE = 64
MODES = 6
MEMBERS = 64
SLOTS = 8
COLS = 3 * MODES * TILE
F32 = jnp.float32
BF16 = jnp.bfloat16
NT = (((1,), (1,)), ((), ()))
TN = (((0,), (0,)), ((), ()))
MIB = 1024 * 1024
BACK = 3328
PACKED = 56


def iota(shape, axis):
    return lax.broadcasted_iota(jnp.int32, shape, axis)


def ones_where(mask):
    return jnp.where(mask, 1.0, 0.0).astype(BF16)


def dot(a, b):
    return jnp.dot(a, b, preferred_element_type=F32)


def parts_of(x):
    high = x.astype(BF16)
    rest = x - high.astype(F32)
    mid = rest.astype(BF16)
    low = (rest - mid.astype(F32)).astype(BF16)
    return high, mid, low


def exact_dot(pick, x, dims, pick_first):
    total = None
    for part in parts_of(x):
        ab = (pick, part) if pick_first else (part, pick)
        prod = lax.dot_general(*ab, dims, preferred_element_type=F32)
        total = prod if total is None else total + prod
    return total


def rank_arrays(owner_row):
    owner_row = owner_row.astype(F32)
    owner_row = jnp.concatenate([owner_row, owner_row[:, 128:]], 1)
    wide = jnp.broadcast_to(owner_row, (WIDE, WIDE))
    tall = wide.T[:ROWS]
    wide = wide[:ROWS]
    lane = iota((ROWS, WIDE), 1)
    row_l = jnp.where(lane < ROWS, lane, lane - TILE)
    row_s = iota((ROWS, WIDE), 0)
    one = jnp.where(wide == tall, 1.0, 0.0)
    less, more = row_s < row_l, row_s > row_l
    rank_l = jnp.sum(jnp.where(less, one, 0.0), 0, keepdims=True)
    after_l = jnp.sum(jnp.where(more, one, 0.0), 0, keepdims=True)
    once = jnp.where(lane < ROWS, one, 0.0)
    rank_s = jnp.sum(jnp.where(more, once, 0.0), 1, keepdims=True)
    after_s = jnp.sum(jnp.where(less, once, 0.0), 1, keepdims=True)
    return (wide[:1], rank_l, after_l), (tall[:, :1], rank_s, after_s)


class Order:
    def __init__(self, wide_ref, tall_ref):
        self.owner_l, self.rank_l, self.after_l = (wide_ref[n : n + 1, :] for n in range(3))
        self.owner_s, self.rank_s, self.after_s = (tall_ref[:, n : n + 1] for n in range(3))


def rim_picks(r, me):
    lane = iota((ROWS, 128), 1)
    first, last = r.rank_s == 0.0, r.after_s == 0.0
    even = me % 2 == 0
    picks = []
    for half in (0, 1):
        slot = lane - TILE * half
        inside = (slot >= 0) & (slot < TILE)
        to_left = jnp.where(inside, slot + jnp.where(me == 0, 1, 0), -1).astype(F32)
        to_right = jnp.where(inside, slot - jnp.where(me == MEMBERS - 1, 1, 0), -1).astype(F32)
        left = jnp.where((r.owner_s == to_left) & first, 1.0, 0.0)
        right = jnp.where((r.owner_s == to_right) & last, 1.0, 0.0)
        near = jnp.where(even, right, left).astype(BF16)
        far = jnp.where(even, left, right).astype(BF16)
        picks.append((near, far))
    return picks


def far_pick(r, me, width):
    top = iota((8, width), 0) == 0
    owner, rank, after = r.owner_l[:, :width], r.rank_l[:, :width], r.after_l[:, :width]
    head = top & (me == 0) & (owner == 0.0) & (rank == 0.0)
    tail = top & (me == MEMBERS - 1) & (owner == MEMBERS - 1.0) & (after == 0.0)
    return ones_where(head), ones_where(tail)


def rims_of(rows, r, me, picks):
    half = rows.shape[0] // 2
    top, bottom = picks
    rims = [(dot(rows[:half], a) + dot(rows[half:], b)).astype(BF16) for a, b in zip(top, bottom)]
    head, tail = far_pick(r, me, ROWS)
    far = lax.dot_general(head + tail, rows, NT, preferred_element_type=F32).astype(BF16)
    return [far] + rims[::-1]


def local_rows(rows, r):
    lane = iota((ROWS, WIDE), 1)
    row_l = jnp.where(lane < ROWS, lane, lane - TILE)
    same = r.owner_l == r.owner_s
    before = ones_where(same & (r.rank_s + 1.0 == r.rank_l))
    after = ones_where(same & (r.rank_s == r.rank_l + 1.0))
    here = ones_where(iota((ROWS, WIDE), 0) == row_l)
    return [dot(rows, pick) for pick in (before, here, after)]


def rim_rows(near, away, far, r, me):
    bucket = iota((128, WIDE), 0)
    even = me % 2 == 0
    result = []
    for rim, edge, end in zip(
        (jnp.where(even, away, near), jnp.where(even, near, away)), (r.rank_l, r.after_l), far_pick(r, me, WIDE)
    ):
        ends = []
        for side in (0, 1):
            want = bucket - TILE * side
            want = jnp.where((want >= 0) & (want < TILE), want, -1).astype(F32)
            ends.append(dot(rim, ones_where((want == r.owner_l) & (edge == 0.0))))
        result.append(jnp.concatenate(ends, 0) + lax.dot_general(far, end, TN, preferred_element_type=F32))
    return result


def set_wide(ref, k, value):
    for tile in (0, 1):
        part = value[:, 128 * tile : 128 * (tile + 1)]
        ref[tile, k] = part.reshape(-1, TILE, 128)


def chunk_copies(a_hbm, a_ref, sems, planes, n):
    rows = pl.ds(16 * n, 16)
    return [
        pltpu.make_async_copy(a_hbm.at[k, rows], a_ref.at[at, rows], sems.at[at, n])
        for at, k in enumerate(planes)
    ]


def start_copies(a_hbm, a_ref, sems, planes):
    for n in range(TILE // 16):
        for copy in chunk_copies(a_hbm, a_ref, sems, planes, n):
            copy.start()


def next_groups(a_hbm, a_ref, sems, planes, ib, group_ref):
    for copy in chunk_copies(a_hbm, a_ref, sems, planes, ib):
        copy.wait()
    set_groups(a_ref, ib, group_ref)


def set_groups(a_ref, ib, group_ref):
    for k in range(a_ref.shape[0]):
        for i in range(8):
            low, high = (a_ref[k, 16 * ib + i + n].astype(F32) for n in (0, 8))
            group_ref[0, k, i] = low[:, :128]
            group_ref[1, k, i] = high[:, :128]
            group_ref[2, k, i] = jnp.concatenate([low[:, 128:], high[:, 128:]], 1)


def folded(terms):
    sub = iota((8, 128), 0)
    for shift in (1, 2, 4):
        keep = (sub & shift) == 0
        terms = [
            jnp.where(keep, x, y) + pltpu.roll(jnp.where(keep, y, x), shift, 0)
            for x, y in zip(terms[::2], terms[1::2])
        ]
    return terms[0]


def contracted(group_ref, wide_ref, g, tile, pairs, columns):
    totals = [[None] * 8 for _ in columns]
    for jb in range(TILE // 8):
        j = pl.ds(8 * jb, 8)
        for k, base in pairs:
            a = [group_ref[g, k, i, j, :] for i in range(8)]
            for n, column in enumerate(columns):
                x = wide_ref[tile, k, base + column, j, :]
                for i in range(8):
                    term = a[i] * x
                    totals[n][i] = term if totals[n][i] is None else totals[n][i] + term
    return [folded(t) for t in totals]


def contracted_rows(a_ref, wide_ref, k, ib, g, columns):
    totals = [[None] * 8 for _ in columns]
    for pair in range(TILE // 16):
        j = slice(16 * pair, 16 * (pair + 1))
        a = []
        for i in range(8):
            low, high = 16 * ib + i, 16 * ib + 8 + i
            if g < 2:
                part = a_ref[k, high if g else low, j, 0:128].astype(F32)
            else:
                part = jnp.concatenate(
                    [a_ref[k, row, j, 128:ROWS].astype(F32) for row in (low, high)], 1
                )
            a.append(part)
        for half in (0, 1):
            rows = slice(16 * pair + 8 * half, 16 * pair + 8 * half + 8)
            for n, column in enumerate(columns):
                x = wide_ref[g // 2, k, column, rows, :]
                for i in range(8):
                    term = a[i][8 * half : 8 * half + 8] * x
                    totals[n][i] = term if totals[n][i] is None else totals[n][i] + term
    return [folded(t) for t in totals]


def ungrouped(out_ref, index):
    low, high, both = out_ref[0, index], out_ref[1, index], out_ref[2, index]
    top = jnp.concatenate([low, both[:, :TILE]], 1)
    bottom = jnp.concatenate([high, both[:, TILE:]], 1)
    return jnp.concatenate([top, bottom], 0)


def first_kernel(me_ref, owner_ref, p_ref, wide_ref, tall_ref, p_out, picks_out, back_out, far_out, away_out, near_out):
    rows, columns = rank_arrays(owner_ref[...])
    p_out[...] = p_ref[...]
    wide_ref[...] = jnp.zeros_like(wide_ref)
    for n in range(3):
        wide_ref[n : n + 1, :] = rows[n]
    lane = iota((ROWS, 128), 1)
    tall_ref[...] = jnp.where(lane == 0, columns[0], jnp.where(lane == 1, columns[1], columns[2]))
    r = Order(wide_ref, tall_ref)
    picks = rim_picks(r, me_ref[0])
    for n in range(4):
        picks_out[n] = picks[n // 2][n % 2]
    for ref, rim in zip((far_out, away_out, near_out), rims_of(p_ref[...], r, me_ref[0], picks)):
        ref[...] = rim
    back_out[...] = jnp.zeros_like(back_out)
    back_out[:, : MODES * TILE] = far_out[...]


def halves(ib):
    return pl.ds(pl.multiple_of(16 * ib, 8), 8), pl.ds(pl.multiple_of(16 * ib + 8, 8), 8)


def middle_kernel(
    order_l_ref, order_s_ref, a_hbm, p_ref, mid_ref, scale_ref, local_ref, outer_ref,
    a_ref, sems, outer_sem, group_ref, wide_ref, out_ref,
):
    ib = pl.program_id(0)

    @pl.when(ib == 0)
    def _():
        start_copies(a_hbm, a_ref, sems, (1,))
        for at in range(2):
            pltpu.make_async_copy(a_hbm.at[2 * at], outer_ref.at[at], outer_sem.at[at]).start()
        before, here, after = local_rows(p_ref[...], Order(order_l_ref, order_s_ref))
        set_wide(wide_ref, 0, here)
        set_wide(local_ref, 0, before)
        set_wide(local_ref, 1, after)

    next_groups(a_hbm, a_ref, sems, (1,), ib, group_ref)
    sub, lane = iota((8, 128), 0), iota((8, 128), 1)
    lower, upper = halves(ib)

    def one_group(g, carry):
        tile = jnp.where(g == 2, 1, 0)
        second = (g == 1) | ((g == 2) & (lane >= TILE))
        diag = jnp.zeros((8, 128), F32)
        for i in range(8):
            entry = jnp.where(second, group_ref[g, 0, i, upper, :], group_ref[g, 0, i, lower, :])
            diag = jnp.where(sub == i, entry, diag)
        scale = 0.6 * (1.0 / diag)
        scale_ref[ib, g] = scale
        for half in (0, 1):
            columns = [3 * half + c for c in range(3)]
            sums = contracted(group_ref, wide_ref, g, tile, [(0, 0)], columns)
            for c, total in zip(columns, sums):
                own = jnp.where(second, wide_ref[tile, 0, c, upper, :], wide_ref[tile, 0, c, lower, :])
                out_ref[g, c] = own - scale * total
        return carry

    lax.fori_loop(0, 3, one_group, 0, unroll=True)
    rows = pl.ds(pl.multiple_of(16 * ib, 16), 16)
    for index in range(6):
        mid_ref[index, rows, :] = ungrouped(out_ref, index).astype(BF16)

    @pl.when(ib == pl.num_programs(0) - 1)
    def _():
        for at in range(2):
            pltpu.make_async_copy(a_hbm.at[2 * at], outer_ref.at[at], outer_sem.at[at]).wait()


def smooth_kernel(
    me_ref, order_l_ref, order_s_ref, picks_ref, mid_ref, scale_ref, local_ref, outer_ref, on_ref, away_ref, near_ref, back_ref,
    s_ref, far_out, away_out, near_out, wide_ref, out_ref,
):
    ib = pl.program_id(0)
    me = me_ref[0]

    @pl.when(ib == 0)
    def _():
        r = Order(order_l_ref, order_s_ref)
        for k, value in enumerate(rim_rows(near_ref[...], away_ref[...], on_ref[...] + back_ref[:, : MODES * TILE], r, me)):
            set_wide(wide_ref, k, value)
        wide_ref[...] += local_ref[...]
        s_ref[6:12] = mid_ref[...]

    for g in range(3):
        scale = 0.0 - scale_ref[ib, g]
        for k in range(2):
            columns = list(range(6))
            sums = contracted_rows(outer_ref, wide_ref, k, ib, g, columns)
            for c, total in zip(columns, sums):
                out_ref[g, 6 * k + c] = scale * total

    rows = pl.ds(pl.multiple_of(16 * ib, 16), 16)
    for index in range(12):
        s_ref[index if index < 6 else index + 6, rows, :] = ungrouped(out_ref, index).astype(BF16)

    @pl.when(ib == pl.num_programs(0) - 1)
    def _():
        r = Order(order_l_ref, order_s_ref)
        picks = (picks_ref[0], picks_ref[1]), (picks_ref[2], picks_ref[3])
        flat = s_ref[...].reshape(COLS, ROWS)
        for ref, rim in zip((far_out, away_out, near_out), rims_of(flat, r, me, picks)):
            ref[...] = rim


def slot_grid(width):
    spot = iota((MEMBERS * SLOTS, width), 0)
    return (spot // SLOTS).astype(F32), (spot % SLOTS).astype(F32)


def pack_kernel(order_l_ref, s_ref, out_ref):
    member, slot = slot_grid(ROWS)
    owner, rank = order_l_ref[0:1, :ROWS], order_l_ref[1:2, :ROWS]
    mine = owner == member
    pick = ones_where(mine & (rank == slot))
    count = jnp.sum(jnp.where(mine, 1.0, 0.0), 1, keepdims=True)
    for block in range(COLS // 128):
        value = lax.dot_general(
            pick, s_ref[128 * block : 128 * (block + 1), :], NT, preferred_element_type=F32
        ).reshape(MEMBERS, SLOTS, 128)
        out_ref[:, 6 * block : 6 * block + 6, :] = value[:, :6, :].astype(BF16)
    counts = jnp.broadcast_to(count, (MEMBERS * SLOTS, 128)).reshape(MEMBERS, SLOTS, 128)
    out_ref[:, 54:56, :] = counts[:, :2, :].astype(BF16)


OFFSETS = [[(k, 6 * (e - k)) for k in range(3) if 0 <= e - k <= 2] for e in range(5)]


def spare_lanes(axis):
    entry, spare = iota((WIDE, WIDE), axis), iota((WIDE, WIDE), 1 - axis) - 252
    return ones_where((spare >= 0) & (entry == 108 + 7 * spare))


def product_kernel(
    me_ref, order_l_ref, order_s_ref, a_hbm, s_ref, far_ref, away_ref, near_ref,
    out_ref, far_out, a_ref, sems, group_ref, wide_ref, ap_ref, own_ref, term_ref,
):
    ib = pl.program_id(0)
    me = me_ref[0]

    @pl.when(ib == 0)
    def _():
        start_copies(a_hbm, a_ref, sems, (0, 1, 2))
        r = Order(order_l_ref, order_s_ref)
        before, here, after = local_rows(s_ref[...], r)
        left, right = rim_rows(near_ref[...], away_ref[...], far_ref[...], r, me)
        for k, value in enumerate((before + left, here, after + right)):
            set_wide(wide_ref, k, value)
        term_ref[...] = jnp.zeros_like(term_ref)

    next_groups(a_hbm, a_ref, sems, (0, 1, 2), ib, group_ref)
    lane = iota((8, 128), 1)

    def one_group(step, carry):
        g, half = step // 2, step % 2
        tile = jnp.where(g == 2, 1, 0)
        for e in range(5):
            columns = [3 * half + c for c in range(3)]
            sums = contracted(group_ref, wide_ref, g, tile, OFFSETS[e], columns)
            for c, total in zip(columns, sums):
                ap_ref[g, ib, 6 * e + c] = total.astype(BF16).astype(F32)
        second = (g == 1) | ((g == 2) & (lane >= TILE))
        lower, upper = pl.ds(pl.multiple_of(16 * ib, 8), 8), pl.ds(pl.multiple_of(16 * ib + 8, 8), 8)
        for c in range(9):
            column = 9 * half + c
            own_ref[g, ib, column] = jnp.where(
                second, wide_ref[tile, 1, column, upper, :], wide_ref[tile, 1, column, lower, :]
            )
        return carry

    lax.fori_loop(0, 6, one_group, 0)

    @pl.when(ib == pl.num_programs(0) - 1)
    def _():
        def one_pair(step, carry):
            k, e = step // 5, step % 5
            for c in range(6):
                near, far = [None] * 6, [None] * 6
                for block in range(TILE // 16):
                    for g in range(3):
                        x = own_ref[g, block, 6 * k + c]
                        for d in range(6):
                            term = x * ap_ref[g, block, 6 * e + d]
                            sums = far if g == 2 else near
                            sums[d] = term if sums[d] is None else sums[d] + term
                for d in range(6):
                    row = slice(6 * c + d, 6 * c + d + 1)
                    tail = jnp.sum(far[d], 0, keepdims=True)
                    term_ref[step, row, 0:128] = jnp.sum(near[d], 0, keepdims=True)
                    term_ref[step, row, 128:ROWS] = tail[:, :TILE] + tail[:, TILE:]
            return carry

        lax.fori_loop(0, 15, one_pair, 0)
        r = Order(order_l_ref, order_s_ref)
        owner, rank, after = (x[:, :ROWS] for x in (r.owner_l, r.rank_l, r.after_l))
        member, slot = slot_grid(ROWS)
        mine, row_slot = owner == member, slot < 6.0
        here = ones_where(mine & (rank == slot))
        back_to = member + jnp.where(me == 0, 1.0, 0.0)
        on_to = member - jnp.where(me == MEMBERS - 1, 1.0, 0.0)
        back = (mine & row_slot & (rank == slot + 1.0)) | ((slot == 6.0) & (owner == back_to) & (rank == 0.0))
        on = (mine & row_slot & (rank == slot - 1.0) & (after > 0.0)) | (
            (slot == 7.0) & (owner == on_to) & (after == 0.0)
        )
        picks = [ones_where(back), here, ones_where(on)]
        terms = []
        for k in range(3):
            pieces = [term_ref[5 * k + e][:36, :ROWS] for e in range(5)]
            pieces.append(jnp.zeros((4 + 36 * k, ROWS), F32))
            if k < 2:
                pieces.insert(0, jnp.zeros((72 - 36 * k, ROWS), F32))
            terms.append(jnp.concatenate(pieces, 0))
        total = None
        for k in range(3):
            prod = exact_dot(picks[k], terms[k], NT, True)
            total = prod if total is None else total + prod
        high = total.astype(BF16).astype(F32)
        rest = dot((total - high).astype(BF16), spare_lanes(0))
        out_ref[...] = (high + rest).astype(BF16)
        head, tail = far_pick(r, me, ROWS)
        far_out[...] = exact_dot(head, terms[0], NT, True) + exact_dot(tail, terms[2], NT, True)


def unpack_smooth_kernel(recv_ref, out_ref, pick_out):
    size = MEMBERS * SLOTS
    count = jnp.broadcast_to(recv_ref[:, 54:55, :].astype(F32), (MEMBERS, SLOTS, 128)).reshape(size, 128)
    source, other = iota((size, size), 0) // SLOTS, iota((size, size), 1) // SLOTS
    first_slot = iota((size, size), 1) % SLOTS == 0
    earlier = ones_where((other < source) & first_slot)
    start = dot(earlier, count.astype(BF16))[:, :1]
    count = count[:, :1]
    slot = (iota((size, 1), 0) % SLOTS).astype(F32)
    place = jnp.where(slot < count, start + slot, -1.0)
    column = iota((size, ROWS), 1).astype(F32)
    pick = ones_where(place == column)
    for block in range(COLS // 128):
        rows = recv_ref[:, 6 * block : 6 * block + 6, :].astype(F32)
        rows = jnp.concatenate([rows, jnp.zeros((MEMBERS, 2, 128), F32)], 1).reshape(size, 128)
        value = lax.dot_general(rows.astype(BF16), pick, TN, preferred_element_type=F32)
        out_ref[128 * block : 128 * (block + 1), :] = value.astype(BF16)
    place = jnp.where(slot == 6.0, jnp.where(start == 0.0, ROWS - 1.0, start - 1.0), place)
    stop = start + count
    place = jnp.where(slot == 7.0, jnp.where(stop == float(ROWS), 0.0, stop), place)
    column = iota((size, WIDE), 1).astype(F32)
    pick_out[...] = jnp.where(place == column, 1.0, 0.0).T[:ROWS].astype(BF16)


def unpack_coarse_kernel(me_ref, pick_ref, sums_ref, far_ref, out_ref):
    me = me_ref[0]
    total = dot(pick_ref[...], sums_ref[...])
    total = total + dot(total.astype(BF16), spare_lanes(1))
    row = iota((ROWS, WIDE), 0)
    edge = jnp.where(me == 0, 0, ROWS - 1)
    far = jnp.broadcast_to(far_ref[0:1, :], (ROWS, WIDE))
    total = total + jnp.where(row == edge, far, 0.0)
    out_ref[...] = total[:, :252]


def call(kernel, outs, args, grid=None, in_specs=None, out_specs=None, scratch=(), flops=0, mib=16, name=None):
    whole = lambda shape: pl.BlockSpec(shape, lambda *_: (0,) * len(shape))
    specs = []
    for n, arg in enumerate(args):
        spec = None if in_specs is None else in_specs.get(n)
        if spec is None:
            spec = pl.BlockSpec(memory_space=pltpu.SMEM) if arg.shape == (1,) else whole(arg.shape)
        specs.append(spec)
    moved = sum(a.size * a.dtype.itemsize for a in args) + sum(o.size * o.dtype.itemsize for o in outs)
    return pl.pallas_call(
        kernel,
        grid=(1,) if grid is None else grid,
        in_specs=specs,
        out_specs=[(out_specs or {}).get(n, whole(o.shape)) for n, o in enumerate(outs)],
        out_shape=outs,
        scratch_shapes=list(scratch),
        compiler_params=pltpu.CompilerParams(vmem_limit_bytes=mib * MIB),
        cost_estimate=pl.CostEstimate(flops=flops, bytes_accessed=moved, transcendentals=0),
        name=name,
    )(*args)


def shaped(shape, dtype=BF16):
    return jax.ShapeDtypeStruct(shape, dtype)


def swaps(groups):
    ring, axes = MEMBERS, range(groups)
    both = lambda pairs: [q for a, b in pairs for q in ((a, b), (b, a))]
    across = both([(g * ring - 1, g * ring) for g in range(1, groups)])
    away = both([(g * ring + i, g * ring + (i + 1) % ring) for g in axes for i in range(1, ring, 2)])
    near = both([(g * ring + i, g * ring + i + 1) for g in axes for i in range(0, ring, 2)])
    return across, away, near


def per_device(a_band, p_tent, new_owner):
    axes = ("group", "member")
    across, away_pairs, near_pairs = swaps(lax.axis_size("group"))
    me = lax.axis_index("member").astype(jnp.int32).reshape(1)
    a = a_band.transpose(1, 2, 3, 0)
    p = p_tent.transpose(1, 2, 0).reshape(MODES * TILE, ROWS)
    a_spec = pl.BlockSpec(memory_space=pltpu.HBM)
    grid = (TILE // 16,)

    def a_scratch(planes):
        return [
            pltpu.VMEM((planes, TILE, TILE, ROWS), BF16),
            pltpu.SemaphoreType.DMA((planes, TILE // 16)),
            pltpu.VMEM((3, planes, 8, TILE, 128), F32),
        ]

    def exchanged(far, away, near):
        far = lax.ppermute(far, axes, across)
        away = lax.ppermute(away, axes, away_pairs)
        return far, away, lax.ppermute(near, axes, near_pairs)

    def rims(length):
        return [shaped((8, length)), shaped((length // 2, 128)), shaped((length // 2, 128))]

    order_l, order_s, p, picks, back, *sent = call(
        first_kernel,
        [shaped((8, WIDE), F32), shaped((ROWS, 128), F32), shaped(p.shape), shaped((4, ROWS, 128)), shaped((8, BACK))] + rims(MODES * TILE),
        (me, new_owner.reshape(1, ROWS), p),
        name="rims",
    )
    far, away, near = sent
    on = lax.ppermute(far, axes, across[::2])
    away = lax.ppermute(away, axes, away_pairs)
    near = lax.ppermute(near, axes, near_pairs)
    back = lax.ppermute(back, axes, across[1::2])
    got = on, away, near, back
    local = shaped((2, 2, MODES, TILE, 128), F32)
    parts = call(
        middle_kernel,
        [shaped((MODES, TILE, ROWS)), shaped((TILE // 16, 3, 8, 128), F32), local, shaped((2, TILE, TILE, ROWS))],
        (order_l, order_s, a, p),
        grid=grid,
        in_specs={2: a_spec},
        out_specs={3: pl.BlockSpec(memory_space=pltpu.VMEM)},
        scratch=[
            *a_scratch(1)[:2],
            pltpu.SemaphoreType.DMA((2,)),
            *a_scratch(1)[2:],
            pltpu.VMEM((2, 1, MODES, TILE, 128), F32),
            pltpu.VMEM((3, MODES, 8, 128), F32),
        ],
        flops=10**9,
        mib=46,
        name="middle",
    )
    s, *sent = call(
        smooth_kernel,
        [shaped((18, TILE, ROWS))] + rims(COLS),
        (me, order_l, order_s, picks, *parts, *got),
        grid=grid,
        in_specs={7: pl.BlockSpec(memory_space=pltpu.VMEM)},
        scratch=[pltpu.VMEM(local.shape, F32), pltpu.VMEM((3, 12, 8, 128), F32)],
        flops=10**9,
        mib=46,
        name="smooth",
    )
    got = exchanged(*sent)
    s = s.reshape(COLS, ROWS)
    (packed,) = call(pack_kernel, [shaped((MEMBERS, PACKED, 128))], (order_l, s), name="pack")
    packed, *got = lax.optimization_barrier((packed, *got))
    recv = lax.all_to_all(packed, "member", split_axis=0, concat_axis=0, tiled=True)

    sums, far = call(
        product_kernel,
        [shaped((MEMBERS * SLOTS, WIDE)), shaped((8, WIDE), F32)],
        (me, order_l, order_s, a, s, *got),
        grid=grid,
        in_specs={3: a_spec},
        scratch=[
            *a_scratch(3),
            pltpu.VMEM((2, 3, 18, TILE, 128), F32),
            pltpu.VMEM((3, TILE // 16, 30, 8, 128), F32),
            pltpu.VMEM((3, TILE // 16, 18, 8, 128), F32),
            pltpu.VMEM((15, 40, WIDE), F32),
        ],
        flops=10**10,
        mib=50,
        name="product",
    )
    far = lax.ppermute(far, axes, across)
    sums = lax.all_to_all(
        sums.reshape(MEMBERS, SLOTS, WIDE), "member", split_axis=0, concat_axis=0, tiled=True
    ).reshape(MEMBERS * SLOTS, WIDE)
    smooth, pick = call(
        unpack_smooth_kernel,
        [shaped((COLS, ROWS)), shaped((ROWS, MEMBERS * SLOTS))],
        (recv,),
        flops=10**9,
        name="unpack_smooth",
    )
    (coarse,) = call(
        unpack_coarse_kernel, [shaped((ROWS, 252), F32)], (me, pick, sums, far), name="unpack_coarse"
    )
    return smooth.reshape(3, MODES, TILE, ROWS).transpose(3, 0, 1, 2), coarse


def solution(mesh):
    in_specs = (
        P(("group", "member"), None, None, None),
        P(("group", "member"), None, None),
        P(("group", "member")),
    )
    out_specs = (P(("group", "member"), None, None, None), P(("group", "member"), None))
    return jax.shard_map(
        per_device, mesh=mesh, in_specs=in_specs, out_specs=out_specs, check_vma=False
    )
```
